256 devices in a mesh: patch: 64 (over z, y, core), mp: 4 (over x).
Axes of the slice: x: 4, y: 4, z: 8, core: 2. Of those that a mesh axis runs over, the one named last changes fastest.
Arguments:
- grid_latent: bfloat16 [65536, 512], P('patch'), may hold values from -6 to 6
- mesh_latent: bfloat16 [8192, 512], P('patch', 'mp'), may hold values from -6 to 6
- edge_weight: bfloat16 [768, 128, 128], P('patch'), may hold values from -0.15625 to 0.15625
- block_source: int32 [768], P('patch'), may hold values from 0 to 511, as said below
- block_live: int32 [768], P('patch'), may hold values from 0 to 1
- mlp_first: bfloat16 [512, 512], replicated, may hold values from -0.25 to 0.25
- mlp_second: bfloat16 [512, 512], P(None, 'mp'), may hold values from -0.25 to 0.25
- mesh_cotangent: bfloat16 [8192, 512], P('patch', 'mp'), may hold values from -6 to 6
Outputs:
- mesh_out: bfloat16 [8192, 512], P('patch', 'mp')
- grad_first: float32 [512, 512], P(None, 'mp')
- grad_second: float32 [512, 512], P(None, 'mp')
The draws below stay inside these ranges and needn't reach their ends.
Inputs may be any that keep to these rules, and one draw needn't show every extreme that they name: `block_source`: grid patch g lies on the device of index g // 8 along patch, and slot b on the device of index b // 12. On every device at most 1 slots take their source from one device, and some device supplies exactly 1 slots to some device.
All inputs are finite; a program needn't handle non-finite values.
Results may differ from the reference program's by a relative error of at most 0.0058.
Values may be sent and summed in bfloat16 or wider, within the bound.
A program may use at most 64 MiB of HBM per device.

```python
import math
import jax
import jax.numpy as jnp

D = 512
HID = 512
PATCH = 128
GPD = 8
BPM = 12
EBD = 12
NB = 768
NGP = 512
NG = 65536
NMP = 64
NM = 8192
N_PATCH = 64


def linked_blocks(key):
    slot_order = jnp.arange(EBD, dtype=jnp.int32)
    far_offset = N_PATCH // 2

    def receiver_lists(receiver, one_key):
        first_key, second_key, third_key = jax.random.split(one_key, 3)
        offsets = jax.random.permutation(first_key, N_PATCH).astype(jnp.int32)
        far_place = jnp.argmax((offsets == far_offset).astype(jnp.int32)).astype(jnp.int32)
        rolled = jnp.roll(offsets, -far_place)
        offsets = jnp.where(receiver == 0, rolled, offsets)
        chosen = offsets[jnp.mod(slot_order, N_PATCH)]
        source_device = jnp.mod(receiver + chosen, N_PATCH).astype(jnp.int32)
        patch_pick = jax.random.randint(second_key, (EBD,), 0, GPD).astype(jnp.int32)
        live = (jax.random.randint(third_key, (EBD,), 0, 3) > 0).astype(jnp.int32)
        live = jnp.where((receiver == 0) & (slot_order == 0), 1, live).astype(jnp.int32)
        return ((source_device * GPD + patch_pick).astype(jnp.int32), live)
    receivers = jnp.arange(N_PATCH, dtype=jnp.int32)
    keys = jax.random.split(jax.random.fold_in(key, 11), N_PATCH)
    global_id, flags = jax.vmap(receiver_lists)(receivers, keys)
    return (global_id.reshape(-1).astype(jnp.int32), flags.reshape(-1).astype(jnp.int32))


def draw_block_source(key, part):
    return linked_blocks(key)[0]


def draw_block_live(key, part):
    return linked_blocks(key)[1]


def levels(key, dims, cuts, low, top_value):
    loudness, own = 1.0, jax.random.fold_in(key, 6)
    for position, shards_of in cuts:
        draws = jnp.exp(jax.random.uniform(jax.random.fold_in(own, position), (shards_of,), jnp.float32, low / len(cuts), top_value / len(cuts)))
        loudness = loudness * jnp.repeat(draws, dims[position] // shards_of).reshape([-1 if axis == position else 1 for axis in range(len(dims))])
    return loudness


def bell_draw(own_key, extent, spread, bound, shards=(), kind=jnp.bfloat16):
    values = spread * jax.random.normal(own_key, extent, jnp.float32)
    if shards:
        values = values * levels(own_key, extent, shards, -0.22, 0.18)
    return jnp.clip(values, -bound, bound).astype(kind)


def setup_inputs(seed: int = 0) -> dict:
    key_of = jax.random.split(jax.random.key(seed), 9)
    return {
        "grid_latent": bell_draw(key_of[0], (NG, D), 1.0, 6.0, ((0, 64),)),
        "mesh_latent": bell_draw(key_of[1], (NM, D), 1.0, 6.0, ((0, 64), (1, 4))),
        "edge_weight": bell_draw(key_of[2], (NB, PATCH, PATCH), (PATCH * BPM) ** -0.5, 0.15625, ((0, 64),)),
        "block_source": draw_block_source(jax.random.fold_in(key_of[8], 71), 0),
        "block_live": draw_block_live(jax.random.fold_in(key_of[8], 71), 0),
        "mlp_first": bell_draw(key_of[5], (D, HID), D ** -0.5, 0.25),
        "mlp_second": bell_draw(key_of[6], (HID, D), HID ** -0.5, 0.25, ((1, 4),)),
        "mesh_cotangent": bell_draw(key_of[7], (NM, D), 1.0, 6.0, ((0, 64), (1, 4))),
    }


def silu_slope(values):
    sigmoid = jax.nn.sigmoid(values)
    return sigmoid * (1.0 + values * (1.0 - sigmoid))

def reference(grid_latent, mesh_latent, edge_weight, block_source, block_live, mlp_first, mlp_second, mesh_cotangent):
    pre_act = jnp.dot(grid_latent, mlp_first, preferred_element_type=jnp.float32)
    hidden = jax.nn.silu(pre_act).astype(jnp.bfloat16)
    message = jnp.dot(hidden, mlp_second, preferred_element_type=jnp.float32).astype(jnp.bfloat16)
    patches = message.reshape(NGP, PATCH, D)
    live_flag = block_live.astype(jnp.float32)[:, None, None]
    weights = edge_weight.astype(jnp.float32)
    sources = jnp.take(patches, block_source.astype(jnp.int32), axis=0).astype(jnp.float32)
    products = jnp.einsum('bpq,bqc->bpc', weights, sources) * live_flag
    summed = products.reshape(NMP, BPM, PATCH, D).sum(axis=1).reshape(NM, D)
    mesh_out = (mesh_latent.astype(jnp.float32) + summed).astype(jnp.bfloat16)
    cotangent = jnp.repeat(mesh_cotangent.reshape(NMP, PATCH, D), BPM, axis=0).astype(jnp.float32)
    adjoint = (jnp.einsum('bqp,bqc->bpc', weights, cotangent) * live_flag).astype(jnp.bfloat16)
    grad_message = jnp.zeros((NGP, PATCH, D), jnp.float32).at[block_source.astype(jnp.int32)].add(adjoint.astype(jnp.float32))
    grad_message = grad_message.reshape(NG, D).astype(jnp.bfloat16)
    scaling = 1.0 / math.sqrt(NG)
    grad_second = jnp.dot(hidden.T, grad_message, preferred_element_type=jnp.float32) * scaling
    grad_hidden = jnp.dot(grad_message, mlp_second.T, preferred_element_type=jnp.float32)
    grad_pre = (grad_hidden * silu_slope(pre_act)).astype(jnp.bfloat16)
    grad_first = jnp.dot(grid_latent.T, grad_pre, preferred_element_type=jnp.float32) * scaling
    return (mesh_out, grad_first, grad_second)
```

```python
import functools
import math

import jax
import jax.numpy as jnp
from jax import lax
from jax.experimental import pallas as pl
from jax.experimental.pallas import tpu as pltpu
from jax.sharding import Mesh
from jax.sharding import PartitionSpec as P

PATCH = 128
PATCH_AXES = ("patch_0", "patch_1", "patch_2")
AXES = PATCH_AXES + ("mp",)
F32 = jnp.float32
BF16 = jnp.bfloat16


def dot(a, b, dims=((1,), (0,))):
    return lax.dot_general(a, b, (dims, ((), ())), preferred_element_type=F32)


def kernel(
    sizes,
    scaling,
    tab_ref,
    meta_ref,
    grid_ref,
    latent_ref,
    w_ref,
    first_ref,
    second_ref,
    cot_ref,
    mesh_out,
    first_out,
    second_out,
    slots,
    V,
    cotb,
    metab,
    second,
    slope,
    hidden,
    msg,
    vbig,
    vbig_t,
    c_send,
    c_recv,
    y_send,
    y_recv,
    y_own,
    z_send,
    z_recv,
    x_send,
    x_recv,
    gm,
    gpre,
    gc_send,
    gc_recv,
    g_own,
    gx_send,
    gx_recv,
    gz_send,
    gz_recv,
    gy_send,
    gy_recv,
    fin,
    w_s,
    w_r,
    sec_s,
    sec_r,
    cx_s,
    cx_r,
    cz_s,
    cz_r,
    cy_s,
    cy_r,
    cc_s,
    cc_r,
    fc_s,
    fc_r,
    fy_s,
    fy_r,
    fz_s,
    fz_r,
    fx_s,
    fx_r,
    gc_s,
    gc_r,
    gx_s,
    gx_r,
    gz_s,
    gz_r,
    gy_s,
    gy_r,
    ay_s,
    ay_r,
    az_s,
    az_r,
    ac_s,
    ac_r,
    loc,
):
    Z, Y, C, X = sizes
    NP = Z * Y * C
    R, D = grid_ref.shape
    H = first_ref.shape[1]
    F = second_ref.shape[1]
    PX = PATCH // X
    GPD = R // PATCH
    HC = D // 2
    z, y, c, x = (lax.axis_index(a) for a in AXES)
    oc = 1 - c
    sent = []

    def send(src, dst, ss, rs, **where):
        place = {"patch_0": z, "patch_1": y, "patch_2": c, "mp": x}
        place.update(where)
        copy = pltpu.make_async_remote_copy(
            src_ref=src,
            dst_ref=dst,
            send_sem=ss,
            recv_sem=rs,
            device_id=place,
            device_id_type=pl.DeviceIdType.MESH,
        )
        copy.start()
        sent.append((src, dst, ss, rs))

    def arrive(dst, rs):
        pltpu.make_async_copy(dst, dst, rs).wait()

    def step(i, k, n):
        return lax.rem(i + k, n)

    xf = pl.ds(pl.multiple_of(x * F, F), F)
    xp = pl.ds(pl.multiple_of(x * PX, PX), PX)

    own_cot = pltpu.make_async_copy(cot_ref.at[xp, :], cotb.at[c, y, z, :, xf], loc.at[0])
    own_cot.start()
    own_second = pltpu.make_async_copy(second_ref, second.at[:, xf], loc.at[1])
    own_second.start()
    own_meta = pltpu.make_async_copy(meta_ref, metab.at[c, y, z], loc.at[2])
    own_meta.start()
    for k in range(1, X):
        to = step(x, k, X)
        rows = pl.ds(pl.multiple_of(to * PX, PX), PX)
        send(cot_ref.at[rows, :], cotb.at[c, y, z, :, xf], cx_s.at[k - 1], cx_r.at[k - 1], mp=to)
    for k in range(1, X):
        to = step(x, k, X)
        send(second_ref, second.at[:, xf], sec_s.at[k - 1], sec_r.at[k - 1], mp=to)

    def pack(i, carry):
        c1, y1, z1 = i // (Y * Z), (i // Z) % Y, i % Z
        natural = (z1 * Y + y1) * 2 + c1
        block = w_ref[tab_ref[0, natural], xp, :]
        live = tab_ref[1, natural]
        slots[i] = (block.astype(F32) * live.astype(F32)).astype(BF16)
        return carry

    lax.fori_loop(0, NP, pack, 0)
    here = (c * Y + y) * Z + z
    own_slot = pltpu.make_async_copy(slots.at[here], V.at[here], loc.at[3])
    own_slot.start()

    def send_slot(j, carry):
        dz, dy, dc = j // (Y * 2), (j // 2) % Y, j % 2
        z1, y1, c1 = lax.rem(z + dz, Z), lax.rem(y + dy, Y), lax.rem(c + dc, 2)
        pltpu.make_async_remote_copy(
            src_ref=slots.at[(c1 * Y + y1) * Z + z1],
            dst_ref=V.at[here],
            send_sem=w_s,
            recv_sem=w_r,
            device_id={"patch_0": z1, "patch_1": y1, "patch_2": c1, "mp": x},
            device_id_type=pl.DeviceIdType.MESH,
        ).start()
        return carry

    lax.fori_loop(1, NP, send_slot, 0)

    own_cot.wait()
    own_meta.wait()
    for k in range(1, X):
        arrive(cotb.at[c, y, z, :, xf], cx_r.at[k - 1])
    for k in range(1, Z):
        to = step(z, k, Z)
        send(cotb.at[c, y, z], cotb.at[c, y, z], cz_s.at[0, k - 1], cz_r.at[0, k - 1], patch_0=to)
        send(metab.at[c, y, z], metab.at[c, y, z], cz_s.at[1, k - 1], cz_r.at[1, k - 1], patch_0=to)

    TR = PATCH

    def first_layer(i, carry):
        rows = pl.ds(pl.multiple_of(i * TR, TR), TR)
        pre = dot(grid_ref[rows, :], first_ref[...])
        s = jax.nn.sigmoid(pre)
        hidden[rows, :] = (pre * s).astype(BF16)
        slope[rows, :] = s * (1.0 + pre * (1.0 - s))
        return carry

    lax.fori_loop(0, R // TR, first_layer, 0)

    for k in range(1, Z):
        frm = step(z, Z - k, Z)
        arrive(cotb.at[c, y, frm], cz_r.at[0, k - 1])
        arrive(metab.at[c, y, frm], cz_r.at[1, k - 1])
    for k in range(1, Y):
        to = step(y, k, Y)
        send(cotb.at[c, y], cotb.at[c, y], cy_s.at[0, k - 1], cy_r.at[0, k - 1], patch_1=to)
        send(metab.at[c, y], metab.at[c, y], cy_s.at[1, k - 1], cy_r.at[1, k - 1], patch_1=to)

    own_second.wait()
    for k in range(1, X):
        frm = step(x, X - k, X)
        arrive(second.at[:, pl.ds(pl.multiple_of(frm * F, F), F)], sec_r.at[k - 1])

    def second_layer(i, carry):
        rows = pl.ds(pl.multiple_of(i * TR, TR), TR)
        msg[rows, :] = dot(hidden[rows, :], second[...]).astype(BF16)
        return carry

    lax.fori_loop(0, R // TR, second_layer, 0)

    for k in range(1, Y):
        frm = step(y, Y - k, Y)
        arrive(cotb.at[c, frm], cy_r.at[0, k - 1])
        arrive(metab.at[c, frm], cy_r.at[1, k - 1])
    send(cotb.at[c], cotb.at[c], cc_s.at[0], cc_r.at[0], patch_2=oc)
    send(metab.at[c], metab.at[c], cc_s.at[1], cc_r.at[1], patch_2=oc)
    arrive(metab.at[oc], cc_r.at[1])

    own_slot.wait()
    pltpu.make_async_remote_copy(
        src_ref=all_but_one(slots, NP),
        dst_ref=all_but_one(V, NP),
        send_sem=w_s,
        recv_sem=w_r,
        device_id={"patch_0": z, "patch_1": y, "patch_2": oc, "mp": x},
        device_id_type=pl.DeviceIdType.MESH,
    ).wait_recv()
    own_natural = (z * Y + y) * 2 + c
    lanes = lax.broadcasted_iota(jnp.int32, (Z, PATCH), 1)
    TC = Z * PX

    def spread(i, carry):
        meta = metab[i // Y, lax.rem(i, Y)].reshape(Z, PATCH)
        patch_of = jnp.sum(jnp.where(lanes == own_natural, meta, 0.0), axis=1, keepdims=True)
        patch_rows = jnp.broadcast_to(
            jnp.broadcast_to(patch_of, (Z, PATCH))[:, None, :], (Z, PX, PATCH)
        ).reshape(TC, PATCH)
        blocks = V[pl.ds(pl.multiple_of(i * Z, Z), Z)].reshape(TC, PATCH).astype(F32)
        rows = pl.ds(pl.multiple_of(i * TC, TC), TC)
        blocks_t = blocks.T
        patch_cols = patch_rows.T
        for g in range(GPD):
            vbig[rows, g * PATCH : (g + 1) * PATCH] = jnp.where(
                patch_rows == float(g), blocks, 0.0
            ).astype(BF16)
            vbig_t[g * PATCH : (g + 1) * PATCH, rows] = jnp.where(
                patch_cols == float(g), blocks_t, 0.0
            ).astype(BF16)
        return carry

    lax.fori_loop(0, C * Y, spread, 0)


    def contribution(core, yy):
        at = pl.multiple_of((core * Y + yy) * TC, TC)
        return dot(vbig[pl.ds(at, TC), :], msg[...])

    for k in range(1, Y + 1):
        yy = step(y, k % Y, Y)
        c_send[yy] = contribution(oc, yy).astype(BF16).reshape(Z, PX, D)
        send(c_send.at[yy], c_recv.at[yy], fc_s.at[k - 1], fc_r.at[k - 1], patch_2=oc)
    for k in range(1, Y + 1):
        yy = step(y, k % Y, Y)
        part = contribution(c, yy)
        arrive(c_recv.at[yy], fc_r.at[k - 1])
        part = part + c_recv[yy].astype(F32).reshape(TC, D)
        if k < Y:
            y_send[k - 1] = part.astype(BF16).reshape(Z, PX, D)
            send(y_send.at[k - 1], y_recv.at[k - 1], fy_s.at[k - 1], fy_r.at[k - 1], patch_1=yy)
        else:
            y_own[...] = part.reshape(Z, PX, D)

    arrive(cotb.at[oc], cc_r.at[0])

    def message_gradient(i, carry):
        rows = pl.ds(pl.multiple_of(i * TR, TR), TR)
        gm[rows, :] = dot(vbig_t[rows, :], cotb[...].reshape(NP * PX, D)).astype(BF16)
        return carry

    lax.fori_loop(0, GPD, message_gradient, 0)

    for k in range(1, Y):
        arrive(y_recv.at[k - 1], fy_r.at[k - 1])
    total = y_own[...]
    for k in range(1, Y):
        total = total + y_recv[k - 1].astype(F32)
    y_own[...] = total
    z_send[...] = total.astype(BF16)
    for k in range(1, Z):
        to = step(z, k, Z)
        send(z_send.at[to], z_recv.at[k - 1], fz_s.at[k - 1], fz_r.at[k - 1], patch_0=to)

    def halves(which, left_ref, right_ref):
        for core in (oc, c):
            cols = pl.ds(pl.multiple_of(core * HC, HC), HC)
            part = dot(left_ref[:, cols], right_ref[...], ((0,), (0,))) * scaling
            for q in range(X):
                piece = part[:, q * F : (q + 1) * F]
                if core is oc:
                    gc_send[which, q] = piece.astype(BF16)
                else:
                    g_own[which, q] = piece
            if core is oc:
                send(
                    gc_send.at[which],
                    gc_recv.at[which],
                    gc_s.at[which],
                    gc_r.at[which],
                    patch_2=oc,
                )

    def over_mp(which):
        arrive(gc_recv.at[which], gc_r.at[which])
        for k in range(1, X):
            to = step(x, k, X)
            gx_send[which, k - 1] = (g_own[which, to] + gc_recv[which, to].astype(F32)).astype(BF16)
            send(
                gx_send.at[which, k - 1],
                gx_recv.at[which, k - 1],
                gx_s.at[which, k - 1],
                gx_r.at[which, k - 1],
                mp=to,
            )
        g_own[which, x] = g_own[which, x] + gc_recv[which, x].astype(F32)

    halves(0, hidden, gm)

    def pre_gradient(i, carry):
        rows = pl.ds(pl.multiple_of(i * TR, TR), TR)
        back = dot(gm[rows, :], second[...], ((1,), (1,)))
        gpre[rows, :] = (back * slope[rows, :]).astype(BF16)
        return carry

    lax.fori_loop(0, R // TR, pre_gradient, 0)
    over_mp(0)

    total = y_own[z]
    for k in range(1, Z):
        arrive(z_recv.at[k - 1], fz_r.at[k - 1])
        total = total + z_recv[k - 1].astype(F32)
    for q in range(X):
        x_send[q] = total[:, q * F : (q + 1) * F]
    own_sum = pltpu.make_async_copy(x_send.at[x], x_recv.at[x], loc.at[0])
    own_sum.start()
    for k in range(1, X):
        to = step(x, k, X)
        send(x_send.at[to], x_recv.at[x], fx_s.at[k - 1], fx_r.at[k - 1], mp=to)

    halves(1, grid_ref, gpre)
    over_mp(1)

    own_sum.wait()
    for k in range(1, X):
        arrive(x_recv.at[step(x, X - k, X)], fx_r.at[k - 1])
    mesh_out[...] = (latent_ref[...].astype(F32) + x_recv[...].reshape(PATCH, F)).astype(BF16)

    NR = HC // (Z * Y)
    for which in range(2):
        total = g_own[which, x]
        for k in range(1, X):
            arrive(gx_recv.at[which, k - 1], gx_r.at[which, k - 1])
            total = total + gx_recv[which, k - 1].astype(F32)
        gz_send[:, :, which] = total.reshape(Z, Y, NR, F)
    for k in range(1, Z):
        to = step(z, k, Z)
        send(gz_send.at[to], gz_recv.at[k - 1], gz_s.at[k - 1], gz_r.at[k - 1], patch_0=to)
    total = gz_send[z]
    for k in range(1, Z):
        arrive(gz_recv.at[k - 1], gz_r.at[k - 1])
        total = total + gz_recv[k - 1]
    gy_send[...] = total
    for k in range(1, Y):
        to = step(y, k, Y)
        send(gy_send.at[to], gy_recv.at[k - 1], gy_s.at[k - 1], gy_r.at[k - 1], patch_1=to)
    total = gy_send[y]
    for k in range(1, Y):
        arrive(gy_recv.at[k - 1], gy_r.at[k - 1])
        total = total + gy_recv[k - 1]
    fin[c, z, y] = total
    for k in range(1, Y):
        to = step(y, k, Y)
        send(fin.at[c, z, y], fin.at[c, z, y], ay_s.at[k - 1], ay_r.at[k - 1], patch_1=to)
    for k in range(1, Y):
        arrive(fin.at[c, z, step(y, Y - k, Y)], ay_r.at[k - 1])
    for k in range(1, Z):
        to = step(z, k, Z)
        send(fin.at[c, z], fin.at[c, z], az_s.at[k - 1], az_r.at[k - 1], patch_0=to)
    for k in range(1, Z):
        arrive(fin.at[c, step(z, Z - k, Z)], az_r.at[k - 1])
    send(fin.at[c], fin.at[c], ac_s.at[0], ac_r.at[0], patch_2=oc)
    arrive(fin.at[oc], ac_r.at[0])
    for core in range(2):
        rows = slice(core * HC, (core + 1) * HC)
        second_out[rows, :] = fin[core, :, :, 0].reshape(HC, F)
        first_out[rows, :] = fin[core, :, :, 1].reshape(HC, F)

    pltpu.make_async_remote_copy(
        src_ref=all_but_one(slots, NP),
        dst_ref=all_but_one(V, NP),
        send_sem=w_s,
        recv_sem=w_r,
        device_id={"patch_0": z, "patch_1": y, "patch_2": oc, "mp": x},
        device_id_type=pl.DeviceIdType.MESH,
    ).wait_send()
    for src, dst, ss, rs in sent:
        pltpu.make_async_copy(src, src, ss).wait()


def all_but_one(ref, n):
    return ref.at[pl.ds(0, n - 1)]


def per_device(
    grid_latent,
    mesh_latent,
    edge_weight,
    block_source,
    block_live,
    mlp_first,
    mlp_second,
    mesh_cotangent,
):
    Z, Y, C = (lax.axis_size(a) for a in PATCH_AXES)
    X = lax.axis_size("mp")
    NP = Z * Y * C
    R, D = grid_latent.shape
    H = mlp_first.shape[1]
    F = mlp_second.shape[1]
    PX = PATCH // X
    GPD = R // PATCH
    HC = D // 2
    NR = HC // (Z * Y)
    slots_of = edge_weight.shape[0]
    hit = (block_source // GPD)[:, None] == jnp.arange(PATCH)[None, :]
    values = jnp.stack([jnp.arange(slots_of, dtype=jnp.int32), block_live, block_source % GPD])
    tab = jnp.sum(jnp.where(hit[None], values[:, :, None], 0), axis=1)
    meta = tab[2:3].astype(F32)
    scaling = 1.0 / math.sqrt(R * NP)

    vm = pltpu.VMEM
    dma = pltpu.SemaphoreType.DMA
    scratch = [
        vm((NP, PX, PATCH), BF16),
        vm((NP, PX, PATCH), BF16),
        vm((C, Y, Z, PX, D), BF16),
        vm((C, Y, Z, 1, PATCH), F32),
        vm((H, D), BF16),
        vm((R, H), F32),
        vm((R, H), BF16),
        vm((R, D), BF16),
        vm((NP * PX, R), BF16),
        vm((R, NP * PX), BF16),
        vm((Y, Z, PX, D), BF16),
        vm((Y, Z, PX, D), BF16),
        vm((Y - 1, Z, PX, D), BF16),
        vm((Y - 1, Z, PX, D), BF16),
        vm((Z, PX, D), F32),
        vm((Z, PX, D), BF16),
        vm((Z - 1, PX, D), BF16),
        vm((X, PX, F), F32),
        vm((X, PX, F), F32),
        vm((R, D), BF16),
        vm((R, H), BF16),
        vm((2, X, HC, F), BF16),
        vm((2, X, HC, F), BF16),
        vm((2, X, HC, F), F32),
        vm((2, X - 1, HC, F), BF16),
        vm((2, X - 1, HC, F), BF16),
        vm((Z, Y, 2, NR, F), F32),
        vm((Z - 1, Y, 2, NR, F), F32),
        vm((Y, 2, NR, F), F32),
        vm((Y - 1, 2, NR, F), F32),
        vm((C, Z, Y, 2, NR, F), F32),
        dma,
        dma,
        dma((X - 1,)),
        dma((X - 1,)),
        dma((X - 1,)),
        dma((X - 1,)),
        dma((2, Z - 1)),
        dma((2, Z - 1)),
        dma((2, Y - 1)),
        dma((2, Y - 1)),
        dma((2,)),
        dma((2,)),
        dma((Y,)),
        dma((Y,)),
        dma((Y - 1,)),
        dma((Y - 1,)),
        dma((Z - 1,)),
        dma((Z - 1,)),
        dma((X - 1,)),
        dma((X - 1,)),
        dma((2,)),
        dma((2,)),
        dma((2, X - 1)),
        dma((2, X - 1)),
        dma((Z - 1,)),
        dma((Z - 1,)),
        dma((Y - 1,)),
        dma((Y - 1,)),
        dma((Y - 1,)),
        dma((Y - 1,)),
        dma((Z - 1,)),
        dma((Z - 1,)),
        dma((1,)),
        dma((1,)),
        dma((4,)),
    ]
    in_vmem = pl.BlockSpec(memory_space=pltpu.VMEM)
    mesh_out, grad_first, grad_second = pl.pallas_call(
        functools.partial(kernel, (Z, Y, C, X), scaling),
        out_shape=(
            jax.ShapeDtypeStruct((PATCH, F), BF16),
            jax.ShapeDtypeStruct((D, F), F32),
            jax.ShapeDtypeStruct((H, F), F32),
        ),
        in_specs=[pl.BlockSpec(memory_space=pltpu.SMEM)] + [in_vmem] * 7,
        out_specs=(in_vmem, in_vmem, in_vmem),
        scratch_shapes=scratch,
        compiler_params=pltpu.CompilerParams(
            has_side_effects=True, vmem_limit_bytes=62 * 1024 * 1024
        ),
    )(
        tab,
        meta,
        grid_latent,
        mesh_latent,
        edge_weight,
        mlp_first,
        mlp_second,
        mesh_cotangent,
    )
    return mesh_out, grad_first, grad_second


def solution(mesh):
    mp = mesh.shape["mp"]
    cores = 2
    rows = mesh.shape["patch"] // cores
    depth = 8 if rows % 8 == 0 else 2
    torus = Mesh(mesh.devices.reshape(depth, rows // depth, cores, mp), AXES)
    in_specs = (
        P(PATCH_AXES, None),
        P(PATCH_AXES, "mp"),
        P(PATCH_AXES, None, None),
        P(PATCH_AXES),
        P(PATCH_AXES),
        P(),
        P(None, "mp"),
        P(PATCH_AXES, "mp"),
    )
    out_specs = (P(PATCH_AXES, "mp"), P(None, "mp"), P(None, "mp"))
    return jax.shard_map(
        per_device, mesh=torus, in_specs=in_specs, out_specs=out_specs, check_vma=False
    )
```

```python
import functools
import math

import jax
import jax.numpy as jnp
from jax import lax
from jax.experimental import pallas as pl
from jax.experimental.pallas import tpu as pltpu
from jax.sharding import Mesh
from jax.sharding import PartitionSpec as P

PATCH = 128
PATCH_AXES = ("patch_0", "patch_1", "patch_2")
AXES = PATCH_AXES + ("mp",)
F32 = jnp.float32
BF16 = jnp.bfloat16


def dot(a, b, dims=((1,), (0,))):
    return lax.dot_general(a, b, (dims, ((), ())), preferred_element_type=F32)


def kernel(
    sizes,
    scaling,
    tab_ref,
    meta_ref,
    grid_in,
    latent_in,
    w_in,
    first_in,
    second_in,
    cot_in,
    mesh_out,
    first_out,
    second_out,
    grid_ref,
    latent_ref,
    w_ref,
    first_ref,
    second_ref,
    cot_ref,
    slots,
    V,
    cotb,
    metab,
    second,
    slope,
    hidden,
    msg,
    vbig,
    vbig_t,
    c_send,
    c_recv,
    y_send,
    y_recv,
    y_own,
    z_send,
    z_recv,
    x_send,
    x_recv,
    gm,
    gpre,
    gc_send,
    gc_recv,
    g_own,
    gx_send,
    gx_recv,
    gz_send,
    gz_recv,
    gy,
    own,
    fin,
    w_s,
    w_r,
    sec_s,
    sec_r,
    cx_s,
    cx_r,
    cz_s,
    cz_r,
    cy_s,
    cy_r,
    cc_s,
    cc_r,
    fc_s,
    fc_r,
    fy_s,
    fy_r,
    fz_s,
    fz_r,
    fx_s,
    fx_r,
    gc_s,
    gc_r,
    gx_s,
    gx_r,
    gz_s,
    gz_r,
    gy_s,
    gy_r,
    az_s,
    az_r,
    ac_s,
    ac_r,
    loc,
    load_s,
):
    Z, Y, C, X = sizes
    NP = Z * Y * C
    R, D = grid_in.shape
    H = first_in.shape[1]
    F = second_in.shape[1]
    PX = PATCH // X
    GPD = R // PATCH
    HC = D // 2
    z, y, c, x = (lax.axis_index(a) for a in AXES)
    oc = 1 - c
    sent = []

    def send(src, dst, ss, rs, **where):
        place = {"patch_0": z, "patch_1": y, "patch_2": c, "mp": x}
        place.update(where)
        copy = pltpu.make_async_remote_copy(
            src_ref=src,
            dst_ref=dst,
            send_sem=ss,
            recv_sem=rs,
            device_id=place,
            device_id_type=pl.DeviceIdType.MESH,
        )
        copy.start()
        sent.append((src, dst, ss, rs))

    def arrive(dst, rs):
        pltpu.make_async_copy(dst, dst, rs).wait()

    def step(i, k, n):
        return lax.rem(i + k, n)

    xf = pl.ds(pl.multiple_of(x * F, F), F)
    xp = pl.ds(pl.multiple_of(x * PX, PX), PX)

    loads = {}
    for i, (name, src, dst) in enumerate(
        (
            ("cot", cot_in, cot_ref),
            ("w", w_in, w_ref),
            ("second", second_in, second_ref),
            ("grid", grid_in, grid_ref),
            ("first", first_in, first_ref),
            ("latent", latent_in, latent_ref),
        )
    ):
        loads[name] = pltpu.make_async_copy(src, dst, load_s.at[i])
        loads[name].start()

    barrier = pltpu.get_barrier_semaphore()

    def greet(j, carry):
        dz, dy, dc = j // (Y * 2), (j // 2) % Y, j % 2
        pl.semaphore_signal(
            barrier,
            inc=1,
            device_id={
                "patch_0": lax.rem(z + dz, Z),
                "patch_1": lax.rem(y + dy, Y),
                "patch_2": lax.rem(c + dc, 2),
                "mp": x,
            },
            device_id_type=pl.DeviceIdType.MESH,
        )
        return carry

    for k in range(1, X):
        pl.semaphore_signal(
            barrier,
            inc=1,
            device_id={"patch_0": z, "patch_1": y, "patch_2": c, "mp": step(x, k, X)},
            device_id_type=pl.DeviceIdType.MESH,
        )
    lax.fori_loop(1, NP, greet, 0)
    loads["cot"].wait()
    pl.semaphore_wait(barrier, NP - 1 + X - 1)

    own_cot = pltpu.make_async_copy(cot_ref.at[xp, :], cotb.at[c, y, z, :, xf], loc.at[0])
    own_cot.start()
    own_meta = pltpu.make_async_copy(meta_ref, metab.at[c, y, z], loc.at[2])
    own_meta.start()
    for k in range(1, X):
        to = step(x, k, X)
        rows = pl.ds(pl.multiple_of(to * PX, PX), PX)
        send(cot_ref.at[rows, :], cotb.at[c, y, z, :, xf], cx_s.at[k - 1], cx_r.at[k - 1], mp=to)
    loads["second"].wait()
    own_second = pltpu.make_async_copy(second_ref, second.at[:, xf], loc.at[1])
    own_second.start()
    for k in range(1, X):
        to = step(x, k, X)
        send(second_ref, second.at[:, xf], sec_s.at[k - 1], sec_r.at[k - 1], mp=to)

    def pack(i, carry):
        c1, y1, z1 = i // (Y * Z), (i // Z) % Y, i % Z
        natural = (z1 * Y + y1) * 2 + c1
        block = w_ref[tab_ref[0, natural], xp, :]
        live = tab_ref[1, natural]
        slots[i] = (block.astype(F32) * live.astype(F32)).astype(BF16)
        return carry

    loads["w"].wait()
    lax.fori_loop(0, NP, pack, 0)

    own_cot.wait()
    own_meta.wait()
    for k in range(1, X):
        arrive(cotb.at[c, y, z, :, xf], cx_r.at[k - 1])
    for k in range(1, Z):
        to = step(z, k, Z)
        send(cotb.at[c, y, z], cotb.at[c, y, z], cz_s.at[0, k - 1], cz_r.at[0, k - 1], patch_0=to)
        send(metab.at[c, y, z], metab.at[c, y, z], cz_s.at[1, k - 1], cz_r.at[1, k - 1], patch_0=to)

    here = (c * Y + y) * Z + z
    own_slot = pltpu.make_async_copy(slots.at[here], V.at[here], loc.at[3])
    own_slot.start()

    def send_slot(j, carry):
        dz, dy, dc = j // (Y * 2), (j // 2) % Y, j % 2
        z1, y1, c1 = lax.rem(z + dz, Z), lax.rem(y + dy, Y), lax.rem(c + dc, 2)
        pltpu.make_async_remote_copy(
            src_ref=slots.at[(c1 * Y + y1) * Z + z1],
            dst_ref=V.at[here],
            send_sem=w_s,
            recv_sem=w_r,
            device_id={"patch_0": z1, "patch_1": y1, "patch_2": c1, "mp": x},
            device_id_type=pl.DeviceIdType.MESH,
        ).start()
        return carry

    lax.fori_loop(1, NP, send_slot, 0)

    TR = PATCH
    loads["grid"].wait()
    loads["first"].wait()

    def first_layer(i, carry):
        rows = pl.ds(pl.multiple_of(i * TR, TR), TR)
        pre = dot(grid_ref[rows, :], first_ref[...])
        s = jax.nn.sigmoid(pre)
        hidden[rows, :] = (pre * s).astype(BF16)
        slope[rows, :] = s * (1.0 + pre * (1.0 - s))
        return carry

    lax.fori_loop(0, R // TR, first_layer, 0)

    for k in range(1, Z):
        frm = step(z, Z - k, Z)
        arrive(cotb.at[c, y, frm], cz_r.at[0, k - 1])
        arrive(metab.at[c, y, frm], cz_r.at[1, k - 1])
    ring = Y == 4
    up, down, across = step(y, 1, Y), step(y, Y - 1, Y), step(y, 2, Y)
    for k in range(1, Y):
        to = step(y, k, Y)
        send(metab.at[c, y], metab.at[c, y], cy_s.at[1, k - 1], cy_r.at[1, k - 1], patch_1=to)
        if not ring or k != 2:
            send(cotb.at[c, y], cotb.at[c, y], cy_s.at[0, k - 1], cy_r.at[0, k - 1], patch_1=to)

    own_second.wait()
    for k in range(1, X):
        frm = step(x, X - k, X)
        arrive(second.at[:, pl.ds(pl.multiple_of(frm * F, F), F)], sec_r.at[k - 1])

    def second_layer(i, carry):
        rows = pl.ds(pl.multiple_of(i * TR, TR), TR)
        msg[rows, :] = dot(hidden[rows, :], second[...]).astype(BF16)
        return carry

    lax.fori_loop(0, R // TR, second_layer, 0)

    for k in range(1, Y):
        frm = step(y, Y - k, Y)
        arrive(metab.at[c, frm], cy_r.at[1, k - 1])
        if not ring or k != 2:
            arrive(cotb.at[c, frm], cy_r.at[0, k - 1])
    if ring:
        for i, (frm, to) in enumerate(((down, up), (up, down))):
            half = pl.ds(i * (Z // 2), Z // 2)
            send(
                cotb.at[c, frm, half],
                cotb.at[c, frm, half],
                cy_s.at[i, Y - 1],
                cy_r.at[i, Y - 1],
                patch_1=to,
            )
    send(metab.at[c], metab.at[c], cc_s.at[1], cc_r.at[1], patch_2=oc)
    arrive(metab.at[oc], cc_r.at[1])

    own_slot.wait()
    pltpu.make_async_remote_copy(
        src_ref=all_but_one(slots, NP),
        dst_ref=all_but_one(V, NP),
        send_sem=w_s,
        recv_sem=w_r,
        device_id={"patch_0": z, "patch_1": y, "patch_2": oc, "mp": x},
        device_id_type=pl.DeviceIdType.MESH,
    ).wait_recv()
    own_natural = (z * Y + y) * 2 + c
    lanes = lax.broadcasted_iota(jnp.int32, (Z, PATCH), 1)
    TC = Z * PX

    def spread(i, carry):
        meta = metab[i // Y, lax.rem(i, Y)].reshape(Z, PATCH)
        patch_of = jnp.sum(jnp.where(lanes == own_natural, meta, 0.0), axis=1, keepdims=True)
        patch_rows = jnp.broadcast_to(
            jnp.broadcast_to(patch_of, (Z, PATCH))[:, None, :], (Z, PX, PATCH)
        ).reshape(TC, PATCH)
        blocks = V[pl.ds(pl.multiple_of(i * Z, Z), Z)].reshape(TC, PATCH).astype(F32)
        rows = pl.ds(pl.multiple_of(i * TC, TC), TC)
        blocks_t = blocks.T
        patch_cols = patch_rows.T
        for g in range(GPD):
            vbig[rows, g * PATCH : (g + 1) * PATCH] = jnp.where(
                patch_rows == float(g), blocks, 0.0
            ).astype(BF16)
            vbig_t[g * PATCH : (g + 1) * PATCH, rows] = jnp.where(
                patch_cols == float(g), blocks_t, 0.0
            ).astype(BF16)
        return carry

    lax.fori_loop(0, C * Y, spread, 0)


    def contribution(core, yy):
        at = pl.multiple_of((core * Y + yy) * TC, TC)
        return dot(vbig[pl.ds(at, TC), :], msg[...])

    for k in range(1, Y + 1):
        yy = step(y, k % Y, Y)
        c_send[yy] = contribution(oc, yy).astype(BF16).reshape(Z, PX, D)
        send(c_send.at[yy], c_recv.at[yy], fc_s.at[k - 1], fc_r.at[k - 1], patch_2=oc)
    if ring:
        for i in range(2):
            arrive(cotb.at[c, across, pl.ds(i * (Z // 2), Z // 2)], cy_r.at[i, Y - 1])
    send(cotb.at[c], cotb.at[c], cc_s.at[0], cc_r.at[0], patch_2=oc)
    for k in range(1, Y + 1):
        yy = step(y, k % Y, Y)
        part = contribution(c, yy)
        arrive(c_recv.at[yy], fc_r.at[k - 1])
        part = part + c_recv[yy].astype(F32).reshape(TC, D)
        if k < Y:
            y_send[k - 1] = part.astype(BF16).reshape(Z, PX, D)
            send(y_send.at[k - 1], y_recv.at[k - 1], fy_s.at[k - 1], fy_r.at[k - 1], patch_1=yy)
        else:
            y_own[...] = part.reshape(Z, PX, D)

    arrive(cotb.at[oc], cc_r.at[0])

    def message_gradient(i, carry):
        rows = pl.ds(pl.multiple_of(i * TR, TR), TR)
        gm[rows, :] = dot(vbig_t[rows, :], cotb[...].reshape(NP * PX, D)).astype(BF16)
        return carry

    lax.fori_loop(0, GPD, message_gradient, 0)

    def halves(which, left_ref, right_ref):
        for core in (oc, c):
            cols = pl.ds(pl.multiple_of(core * HC, HC), HC)
            part = dot(left_ref[:, cols], right_ref[...], ((0,), (0,))) * scaling
            for q in range(X):
                piece = part[:, q * F : (q + 1) * F]
                if core is oc:
                    gc_send[which, q] = piece
                else:
                    g_own[which, q] = piece
            if core is oc:
                send(
                    gc_send.at[which],
                    gc_recv.at[which],
                    gc_s.at[which],
                    gc_r.at[which],
                    patch_2=oc,
                )

    def over_mp(which):
        arrive(gc_recv.at[which], gc_r.at[which])
        for k in range(1, X):
            to = step(x, k, X)
            gx_send[which, k - 1] = (g_own[which, to] + gc_recv[which, to]).astype(BF16)
            send(
                gx_send.at[which, k - 1],
                gx_recv.at[which, k - 1],
                gx_s.at[which, k - 1],
                gx_r.at[which, k - 1],
                mp=to,
            )
        g_own[which, x] = g_own[which, x] + gc_recv[which, x]

    halves(0, hidden, gm)

    def pre_gradient(i, carry):
        rows = pl.ds(pl.multiple_of(i * TR, TR), TR)
        back = dot(gm[rows, :], second[...], ((1,), (1,)))
        gpre[rows, :] = (back * slope[rows, :]).astype(BF16)
        return carry

    lax.fori_loop(0, R // TR, pre_gradient, 0)
    over_mp(0)

    halves(1, grid_ref, gpre)

    for k in range(1, Y):
        arrive(y_recv.at[k - 1], fy_r.at[k - 1])
    total = y_own[...]
    for k in range(1, Y):
        total = total + y_recv[k - 1].astype(F32)
    y_own[...] = total
    z_send[...] = total.astype(BF16)
    for k in range(1, Z):
        to = step(z, k, Z)
        send(z_send.at[to], z_recv.at[k - 1], fz_s.at[k - 1], fz_r.at[k - 1], patch_0=to)

    over_mp(1)

    ZR = HC // Z
    for which in range(2):
        total = g_own[which, x]
        for k in range(1, X):
            arrive(gx_recv.at[which, k - 1], gx_r.at[which, k - 1])
            total = total + gx_recv[which, k - 1].astype(F32)
        g_own[which, x] = total
        gz_send[:, which] = total.reshape(Z, ZR, F).astype(BF16)
    for k in range(1, Z):
        to = step(z, k, Z)
        send(gz_send.at[to], gz_recv.at[k - 1], gz_s.at[k - 1], gz_r.at[k - 1], patch_0=to)

    total = y_own[z]
    for k in range(1, Z):
        arrive(z_recv.at[k - 1], fz_r.at[k - 1])
        total = total + z_recv[k - 1].astype(F32)
    for q in range(X):
        x_send[q] = total[:, q * F : (q + 1) * F]
    own_sum = pltpu.make_async_copy(x_send.at[x], x_recv.at[x], loc.at[0])
    own_sum.start()
    for k in range(1, X):
        to = step(x, k, X)
        send(x_send.at[to], x_recv.at[x], fx_s.at[k - 1], fx_r.at[k - 1], mp=to)

    total = g_own[:, x, pl.ds(pl.multiple_of(z * ZR, ZR), ZR)]
    for k in range(1, Z):
        arrive(gz_recv.at[k - 1], gz_r.at[k - 1])
        total = total + gz_recv[k - 1].astype(F32)
    gy[y] = total
    for k in range(1, Y):
        to = step(y, k, Y)
        send(gy.at[y], gy.at[y], gy_s.at[k - 1], gy_r.at[k - 1], patch_1=to)

    own_sum.wait()
    for k in range(1, X):
        arrive(x_recv.at[step(x, X - k, X)], fx_r.at[k - 1])
    loads["latent"].wait()
    mesh_out[...] = (latent_ref[...].astype(F32) + x_recv[...].reshape(PATCH, F)).astype(BF16)

    for k in range(1, Y):
        arrive(gy.at[step(y, Y - k, Y)], gy_r.at[k - 1])
    total = gy[0]
    for yy in range(1, Y):
        total = total + gy[yy]
    own[...] = total.astype(BF16)
    for k in range(1, Z):
        to = step(z, k, Z)
        send(own, fin.at[c, z], az_s.at[k - 1], az_r.at[k - 1], patch_0=to)
    fin[c, z] = own[...]
    for k in range(1, Z):
        arrive(fin.at[c, step(z, Z - k, Z)], az_r.at[k - 1])
    send(fin.at[c], fin.at[c], ac_s.at[0], ac_r.at[0], patch_2=oc)
    arrive(fin.at[oc], ac_r.at[0])
    for core in range(2):
        rows = slice(core * HC, (core + 1) * HC)
        second_out[rows, :] = fin[core, :, 0].reshape(HC, F).astype(F32)
        first_out[rows, :] = fin[core, :, 1].reshape(HC, F).astype(F32)

    pltpu.make_async_remote_copy(
        src_ref=all_but_one(slots, NP),
        dst_ref=all_but_one(V, NP),
        send_sem=w_s,
        recv_sem=w_r,
        device_id={"patch_0": z, "patch_1": y, "patch_2": oc, "mp": x},
        device_id_type=pl.DeviceIdType.MESH,
    ).wait_send()
    for src, dst, ss, rs in sent:
        pltpu.make_async_copy(src, src, ss).wait()


def all_but_one(ref, n):
    return ref.at[pl.ds(0, n - 1)]


def per_device(
    grid_latent,
    mesh_latent,
    edge_weight,
    block_source,
    block_live,
    mlp_first,
    mlp_second,
    mesh_cotangent,
):
    Z, Y, C = (lax.axis_size(a) for a in PATCH_AXES)
    X = lax.axis_size("mp")
    NP = Z * Y * C
    R, D = grid_latent.shape
    H = mlp_first.shape[1]
    F = mlp_second.shape[1]
    PX = PATCH // X
    GPD = R // PATCH
    HC = D // 2
    ZR = HC // Z
    slots_of = edge_weight.shape[0]
    hit = (block_source // GPD)[:, None] == jnp.arange(PATCH)[None, :]
    values = jnp.stack([jnp.arange(slots_of, dtype=jnp.int32), block_live, block_source % GPD])
    tab = jnp.sum(jnp.where(hit[None], values[:, :, None], 0), axis=1)
    meta = tab[2:3].astype(F32)
    scaling = 1.0 / math.sqrt(R * NP)

    vm = pltpu.VMEM
    dma = pltpu.SemaphoreType.DMA
    scratch = [
        vm(grid_latent.shape, BF16),
        vm(mesh_latent.shape, BF16),
        vm(edge_weight.shape, BF16),
        vm(mlp_first.shape, BF16),
        vm(mlp_second.shape, BF16),
        vm(mesh_cotangent.shape, BF16),
        vm((NP, PX, PATCH), BF16),
        vm((NP, PX, PATCH), BF16),
        vm((C, Y, Z, PX, D), BF16),
        vm((C, Y, Z, 1, PATCH), F32),
        vm((H, D), BF16),
        vm((R, H), F32),
        vm((R, H), BF16),
        vm((R, D), BF16),
        vm((NP * PX, R), BF16),
        vm((R, NP * PX), BF16),
        vm((Y, Z, PX, D), BF16),
        vm((Y, Z, PX, D), BF16),
        vm((Y - 1, Z, PX, D), BF16),
        vm((Y - 1, Z, PX, D), BF16),
        vm((Z, PX, D), F32),
        vm((Z, PX, D), BF16),
        vm((Z - 1, PX, D), BF16),
        vm((X, PX, F), F32),
        vm((X, PX, F), F32),
        vm((R, D), BF16),
        vm((R, H), BF16),
        vm((2, X, HC, F), F32),
        vm((2, X, HC, F), F32),
        vm((2, X, HC, F), F32),
        vm((2, X - 1, HC, F), BF16),
        vm((2, X - 1, HC, F), BF16),
        vm((Z, 2, ZR, F), BF16),
        vm((Z - 1, 2, ZR, F), BF16),
        vm((Y, 2, ZR, F), F32),
        vm((2, ZR, F), BF16),
        vm((C, Z, 2, ZR, F), BF16),
        dma,
        dma,
        dma((X - 1,)),
        dma((X - 1,)),
        dma((X - 1,)),
        dma((X - 1,)),
        dma((2, Z - 1)),
        dma((2, Z - 1)),
        dma((2, Y)),
        dma((2, Y)),
        dma((2,)),
        dma((2,)),
        dma((Y,)),
        dma((Y,)),
        dma((Y - 1,)),
        dma((Y - 1,)),
        dma((Z - 1,)),
        dma((Z - 1,)),
        dma((X - 1,)),
        dma((X - 1,)),
        dma((2,)),
        dma((2,)),
        dma((2, X - 1)),
        dma((2, X - 1)),
        dma((Z - 1,)),
        dma((Z - 1,)),
        dma((Y - 1,)),
        dma((Y - 1,)),
        dma((Z - 1,)),
        dma((Z - 1,)),
        dma((1,)),
        dma((1,)),
        dma((4,)),
        dma((6,)),
    ]
    in_vmem = pl.BlockSpec(memory_space=pltpu.VMEM)
    mesh_out, grad_first, grad_second = pl.pallas_call(
        functools.partial(kernel, (Z, Y, C, X), scaling),
        out_shape=(
            jax.ShapeDtypeStruct((PATCH, F), BF16),
            jax.ShapeDtypeStruct((D, F), F32),
            jax.ShapeDtypeStruct((H, F), F32),
        ),
        in_specs=[pl.BlockSpec(memory_space=pltpu.SMEM), in_vmem]
        + [pl.BlockSpec(memory_space=pl.ANY)] * 6,
        out_specs=(in_vmem, in_vmem, in_vmem),
        scratch_shapes=scratch,
        compiler_params=pltpu.CompilerParams(
            collective_id=0, has_side_effects=True, vmem_limit_bytes=62 * 1024 * 1024
        ),
    )(
        tab,
        meta,
        grid_latent,
        mesh_latent,
        edge_weight,
        mlp_first,
        mlp_second,
        mesh_cotangent,
    )
    return mesh_out, grad_first, grad_second


def solution(mesh):
    mp = mesh.shape["mp"]
    cores = 2
    rows = mesh.shape["patch"] // cores
    depth = 8 if rows % 8 == 0 else 2
    torus = Mesh(mesh.devices.reshape(depth, rows // depth, cores, mp), AXES)
    in_specs = (
        P(PATCH_AXES, None),
        P(PATCH_AXES, "mp"),
        P(PATCH_AXES, None, None),
        P(PATCH_AXES),
        P(PATCH_AXES),
        P(),
        P(None, "mp"),
        P(PATCH_AXES, "mp"),
    )
    out_specs = (P(PATCH_AXES, "mp"), P(None, "mp"), P(None, "mp"))
    return jax.shard_map(
        per_device, mesh=torus, in_specs=in_specs, out_specs=out_specs, check_vma=False
    )
```

```python
import functools
import math

import jax
import jax.numpy as jnp
from jax import lax
from jax.experimental import pallas as pl
from jax.experimental.pallas import tpu as pltpu
from jax.sharding import Mesh
from jax.sharding import PartitionSpec as P

PATCH = 128
PATCH_AXES = ("patch_0", "patch_1", "patch_2")
AXES = PATCH_AXES + ("mp",)
F32 = jnp.float32
BF16 = jnp.bfloat16


def dot(a, b, dims=((1,), (0,))):
    return lax.dot_general(a, b, (dims, ((), ())), preferred_element_type=F32)


def kernel(
    sizes,
    scaling,
    source_ref,
    live_ref,
    grid_in,
    latent_in,
    w_in,
    first_in,
    second_in,
    cot_in,
    mesh_out,
    first_out,
    second_out,
    meta_ref,
    grid_ref,
    latent_ref,
    w_ref,
    first_ref,
    second_ref,
    cot_ref,
    slots,
    V,
    cotb,
    metab,
    second,
    slope,
    hidden,
    msg,
    vbig,
    vbig_t,
    c_send,
    c_recv,
    y_send,
    y_recv,
    y_own,
    z_send,
    z_recv,
    x_send,
    x_recv,
    gm,
    gpre,
    gc_send,
    gc_recv,
    g_own,
    gx_send,
    gx_recv,
    gz_send,
    gz_recv,
    gy,
    own,
    fin,
    w_s,
    w_r,
    sec_s,
    sec_r,
    cx_s,
    cx_r,
    cz_s,
    cz_r,
    cy_s,
    cy_r,
    ch_s,
    ch_r,
    cc_s,
    cc_r,
    mz_s,
    mz_r,
    my_s,
    my_r,
    mc_s,
    mc_r,
    fc_s,
    fc_r,
    fy_s,
    fy_r,
    fz_s,
    fz_r,
    fx_s,
    fx_r,
    gc_s,
    gc_r,
    gx_s,
    gx_r,
    gz_s,
    gz_r,
    gy_s,
    gy_r,
    az_s,
    az_r,
    ac_s,
    ac_r,
    loc,
    load_s,
):
    Z, Y, C, X = sizes
    NP = Z * Y * C
    R, D = grid_in.shape
    H = first_in.shape[1]
    F = second_in.shape[1]
    PX = PATCH // X
    GPD = R // PATCH
    HC = D // 2
    z, y, c, x = (lax.axis_index(a) for a in AXES)
    oc = 1 - c
    sent = []

    def send(src, dst, ss, rs, **where):
        place = {"patch_0": z, "patch_1": y, "patch_2": c, "mp": x}
        place.update(where)
        copy = pltpu.make_async_remote_copy(
            src_ref=src,
            dst_ref=dst,
            send_sem=ss,
            recv_sem=rs,
            device_id=place,
            device_id_type=pl.DeviceIdType.MESH,
        )
        copy.start()
        sent.append((src, dst, ss, rs))

    def arrive(dst, rs):
        pltpu.make_async_copy(dst, dst, rs).wait()

    def step(i, k, n):
        return lax.rem(i + k, n)

    xf = pl.ds(pl.multiple_of(x * F, F), F)
    xp = pl.ds(pl.multiple_of(x * PX, PX), PX)

    loads = {}
    for i, (name, src, dst) in enumerate(
        (
            ("cot", cot_in, cot_ref),
            ("w", w_in, w_ref),
            ("second", second_in, second_ref),
            ("grid", grid_in, grid_ref),
            ("first", first_in, first_ref),
            ("latent", latent_in, latent_ref),
        )
    ):
        loads[name] = pltpu.make_async_copy(src, dst, load_s.at[i])
        loads[name].start()

    barrier = pltpu.get_barrier_semaphore()

    def greet(j, carry):
        dz, dy, dc = j // (Y * 2), (j // 2) % Y, j % 2
        pl.semaphore_signal(
            barrier,
            inc=1,
            device_id={
                "patch_0": lax.rem(z + dz, Z),
                "patch_1": lax.rem(y + dy, Y),
                "patch_2": lax.rem(c + dc, 2),
                "mp": x,
            },
            device_id_type=pl.DeviceIdType.MESH,
        )
        return carry

    for k in range(1, X):
        pl.semaphore_signal(
            barrier,
            inc=1,
            device_id={"patch_0": z, "patch_1": y, "patch_2": c, "mp": step(x, k, X)},
            device_id_type=pl.DeviceIdType.MESH,
        )
    lax.fori_loop(1, NP, greet, 0)

    n_slots = w_in.shape[0]

    def feeder(j):
        return jnp.where(live_ref[j] == 1, lax.div(source_ref[j], GPD), -1)

    lane = lax.broadcasted_iota(jnp.int32, (1, PATCH), 1)
    meta = jnp.zeros((1, PATCH), F32)
    for j in range(n_slots):
        inside = lax.rem(source_ref[j], GPD).astype(F32)
        meta = jnp.where(lane == feeder(j), inside, meta)
    meta_ref[...] = meta
    loads["w"].wait()

    def pack(i, carry):
        c1, y1, z1 = i // (Y * Z), (i // Z) % Y, i % Z
        natural = (z1 * Y + y1) * 2 + c1
        slot, live = jnp.int32(0), jnp.int32(0)
        for j in range(n_slots):
            hit = feeder(j) == natural
            slot = jnp.where(hit, j, slot)
            live = jnp.where(hit, 1, live)
        block = w_ref[slot, xp, :]
        slots[i] = (block.astype(F32) * live.astype(F32)).astype(BF16)
        return carry

    lax.fori_loop(0, NP, pack, 0)
    loads["cot"].wait()
    loads["second"].wait()
    own_cot = pltpu.make_async_copy(cot_ref.at[xp, :], cotb.at[c, y, z, :, xf], loc.at[0])
    own_cot.start()
    own_second = pltpu.make_async_copy(second_ref, second.at[:, xf], loc.at[1])
    own_second.start()
    own_meta = pltpu.make_async_copy(meta_ref, metab.at[c, y, z], loc.at[2])
    own_meta.start()
    here = (c * Y + y) * Z + z
    own_slot = pltpu.make_async_copy(slots.at[here], V.at[here], loc.at[3])
    own_slot.start()
    pl.semaphore_wait(barrier, NP - 1 + X - 1)

    for k in range(1, X):
        to = step(x, k, X)
        rows = pl.ds(pl.multiple_of(to * PX, PX), PX)
        send(cot_ref.at[rows, :], cotb.at[c, y, z, :, xf], cx_s.at[k - 1], cx_r.at[k - 1], mp=to)
    for k in range(1, X):
        to = step(x, k, X)
        send(second_ref, second.at[:, xf], sec_s.at[k - 1], sec_r.at[k - 1], mp=to)

    def send_slot(j, carry):
        dz, dy, dc = j // (Y * 2), (j // 2) % Y, j % 2
        z1, y1, c1 = lax.rem(z + dz, Z), lax.rem(y + dy, Y), lax.rem(c + dc, 2)
        pltpu.make_async_remote_copy(
            src_ref=slots.at[(c1 * Y + y1) * Z + z1],
            dst_ref=V.at[here],
            send_sem=w_s,
            recv_sem=w_r.at[c * Y + y],
            device_id={"patch_0": z1, "patch_1": y1, "patch_2": c1, "mp": x},
            device_id_type=pl.DeviceIdType.MESH,
        ).start()
        return carry

    def send_slots(dz):
        lax.fori_loop(max(1, dz * Y * 2), (dz + 1) * Y * 2, send_slot, 0)

    TR = 2 * PATCH
    T = R // TR

    def first_layer(i):
        rows = pl.ds(i * TR, TR)
        pre = dot(grid_ref[rows, :], first_ref[...])
        s = jax.nn.sigmoid(pre)
        hidden[rows, :] = (pre * s).astype(BF16)
        slope[rows, :] = s * (1.0 + pre * (1.0 - s))

    def second_layer(i):
        rows = pl.ds(i * TR, TR)
        msg[rows, :] = dot(hidden[rows, :], second[...]).astype(BF16)

    up, down, across = step(y, 1, Y), step(y, Y - 1, Y), step(y, 2, Y)
    above, below = step(z, 1, Z), step(z, Z - 1, Z)
    HALVES = (pl.ds(0, PX // 2), pl.ds(PX // 2, PX // 2))
    y_ways = ((0, up), (1, down)) if Y > 2 else ((0, up),)

    def over_y(k):
        at = step(z, k % Z, Z)
        for way, to in y_ways:
            send(
                cotb.at[c, y, at],
                cotb.at[c, y, at],
                cy_s.at[way, k % Z],
                cy_r.at[way, k % Z],
                patch_1=to,
            )

    def across_y(k):
        at = step(z, k % Z, Z)
        for way, frm in ((0, down), (1, up))[: len(y_ways)]:
            arrive(cotb.at[c, frm, at], cy_r.at[way, k % Z])
        if Y > 2:
            for way, frm, to in ((0, down, up), (1, up, down)):
                send(
                    cotb.at[c, frm, at, HALVES[way]],
                    cotb.at[c, frm, at, HALVES[way]],
                    ch_s.at[way, k % Z],
                    ch_r.at[way, k % Z],
                    patch_1=to,
                )

    def round_z(t):
        last = 2 * t == Z
        for way, k, to in ((0, 1 - t, above), (1, t - 1, below)):
            at = step(z, k % Z, Z)
            part = cotb.at[c, y, at, HALVES[way]] if last else cotb.at[c, y, at]
            send(part, part, cz_s.at[way, t - 1], cz_r.at[way, t - 1], patch_0=to)

    def from_z(t):
        last = 2 * t == Z
        for way in (0, 1):
            at = step(z, Z - t, Z) if way == 0 else step(z, t % Z, Z)
            part = cotb.at[c, y, at, HALVES[way]] if last else cotb.at[c, y, at]
            arrive(part, cz_r.at[way, t - 1])
        over_y(Z - t)
        if not last:
            over_y(t)

    send_slots(0)
    own_cot.wait()
    own_meta.wait()
    for k in range(1, X):
        frm = step(x, X - k, X)
        arrive(cotb.at[c, y, z, :, pl.ds(pl.multiple_of(frm * F, F), F)], cx_r.at[k - 1])
    round_z(1)
    over_y(0)
    for k in range(1, Z):
        to = step(z, k, Z)
        send(metab.at[c, y, z], metab.at[c, y, z], mz_s.at[k - 1], mz_r.at[k - 1], patch_0=to)
    steps = Z // 2
    for t in range(1, steps + 1):
        for dz in (t, Z - t) if 2 * t < Z else (t,):
            send_slots(dz)
        if t == 1:
            loads["grid"].wait()
            loads["first"].wait()
        if t <= T:
            first_layer(t - 1)
        from_z(t)
        if t < steps:
            round_z(t + 1)
    for i in range(steps, T):
        first_layer(i)
    for k in range(1, Z):
        arrive(metab.at[c, y, step(z, Z - k, Z)], mz_r.at[k - 1])
    for k in range(1, Y):
        to = step(y, k, Y)
        send(metab.at[c, y], metab.at[c, y], my_s.at[k - 1], my_r.at[k - 1], patch_1=to)
    send(cotb.at[c, y], cotb.at[c, y], cc_s.at[0], cc_r.at[0], patch_2=oc)
    own_second.wait()
    for k in range(1, X):
        frm = step(x, X - k, X)
        arrive(second.at[:, pl.ds(pl.multiple_of(frm * F, F), F)], sec_r.at[k - 1])
    order = [0]
    for t in range(1, steps + 1):
        order += [Z - t, t] if 2 * t < Z else [t]
    per = -(-Z // T)
    for i in range(T):
        second_layer(i)
        for k in order[i * per : (i + 1) * per]:
            across_y(k)
    for way, frm in ((0, down), (1, up))[: len(y_ways)]:
        send(cotb.at[c, frm], cotb.at[c, frm], cc_s.at[1 + way], cc_r.at[1 + way], patch_2=oc)
    for k in range(1, Y):
        arrive(metab.at[c, step(y, Y - k, Y)], my_r.at[k - 1])
    send(metab.at[c], metab.at[c], mc_s.at[0], mc_r.at[0], patch_2=oc)
    arrive(metab.at[oc], mc_r.at[0])

    own_slot.wait()
    own_natural = (z * Y + y) * 2 + c
    lanes = lax.broadcasted_iota(jnp.int32, (Z, PATCH), 1)
    TC = Z * PX

    def spread(i, carry):
        meta = metab[i // Y, lax.rem(i, Y)].reshape(Z, PATCH)
        patch_of = jnp.sum(jnp.where(lanes == own_natural, meta, 0.0), axis=1, keepdims=True)
        patch_rows = jnp.broadcast_to(
            jnp.broadcast_to(patch_of, (Z, PATCH))[:, None, :], (Z, PX, PATCH)
        ).reshape(TC, PATCH)
        blocks = V[pl.ds(pl.multiple_of(i * Z, Z), Z)].reshape(TC, PATCH).astype(F32)
        rows = pl.ds(pl.multiple_of(i * TC, TC), TC)
        blocks_t = blocks.T
        patch_cols = patch_rows.T
        for g in range(GPD):
            vbig[rows, g * PATCH : (g + 1) * PATCH] = jnp.where(
                patch_rows == float(g), blocks, 0.0
            ).astype(BF16)
            vbig_t[g * PATCH : (g + 1) * PATCH, rows] = jnp.where(
                patch_cols == float(g), blocks_t, 0.0
            ).astype(BF16)
        return carry

    own_g = c * Y + y
    arrive(V.at[pl.ds(0, Z - 1)], w_r.at[own_g])
    for k in range(1, C * Y):
        arrive(V.at[pl.ds(0, Z)], w_r.at[lax.rem(own_g + k, C * Y)])
    lax.fori_loop(0, C * Y, spread, 0)


    def contribution(core, yy):
        at = pl.multiple_of((core * Y + yy) * TC, TC)
        return dot(vbig[pl.ds(at, TC), :], msg[...])

    for k in range(1, Y + 1):
        yy = step(y, k % Y, Y)
        c_send[yy] = contribution(oc, yy).astype(BF16).reshape(Z, PX, D)
        send(c_send.at[yy], c_recv.at[yy], fc_s.at[k - 1], fc_r.at[k - 1], patch_2=oc)
    if Y > 2:
        for k in order:
            for way in (0, 1):
                arrive(cotb.at[c, across, step(z, k % Z, Z), HALVES[way]], ch_r.at[way, k % Z])
        send(cotb.at[c, across], cotb.at[c, across], cc_s.at[3], cc_r.at[3], patch_2=oc)
    for k in range(1, Y + 1):
        yy = step(y, k % Y, Y)
        part = contribution(c, yy)
        arrive(c_recv.at[yy], fc_r.at[k - 1])
        part = part + c_recv[yy].astype(F32).reshape(TC, D)
        if k < Y:
            y_send[k - 1] = part.astype(BF16).reshape(Z, PX, D)
            send(y_send.at[k - 1], y_recv.at[k - 1], fy_s.at[k - 1], fy_r.at[k - 1], patch_1=yy)
        else:
            y_own[...] = part.reshape(Z, PX, D)

    columns = (y, down, up, across) if Y > 2 else (y, up)
    for i, yy in enumerate(columns):
        arrive(cotb.at[oc, yy], cc_r.at[i])

    def message_gradient(i, carry):
        rows = pl.ds(pl.multiple_of(i * TR, TR), TR)
        gm[rows, :] = dot(vbig_t[rows, :], cotb[...].reshape(NP * PX, D)).astype(BF16)
        return carry

    lax.fori_loop(0, R // TR, message_gradient, 0)

    def halves(which, left_ref, right_ref):
        for core in (oc, c):
            cols = pl.ds(pl.multiple_of(core * HC, HC), HC)
            part = dot(left_ref[:, cols], right_ref[...], ((0,), (0,))) * scaling
            for q in range(X):
                piece = part[:, q * F : (q + 1) * F]
                if core is oc:
                    gc_send[which, q] = piece
                else:
                    g_own[which, q] = piece
            if core is oc:
                send(
                    gc_send.at[which],
                    gc_recv.at[which],
                    gc_s.at[which],
                    gc_r.at[which],
                    patch_2=oc,
                )

    def over_mp(which):
        arrive(gc_recv.at[which], gc_r.at[which])
        for k in range(1, X):
            to = step(x, k, X)
            gx_send[which, k - 1] = (g_own[which, to] + gc_recv[which, to]).astype(BF16)
            send(
                gx_send.at[which, k - 1],
                gx_recv.at[which, k - 1],
                gx_s.at[which, k - 1],
                gx_r.at[which, k - 1],
                mp=to,
            )
        g_own[which, x] = g_own[which, x] + gc_recv[which, x]

    halves(0, hidden, gm)

    def pre_gradient(i, carry):
        rows = pl.ds(pl.multiple_of(i * TR, TR), TR)
        back = dot(gm[rows, :], second[...], ((1,), (1,)))
        gpre[rows, :] = (back * slope[rows, :]).astype(BF16)
        return carry

    lax.fori_loop(0, R // TR, pre_gradient, 0)
    over_mp(0)

    halves(1, grid_ref, gpre)

    for k in range(1, Y):
        arrive(y_recv.at[k - 1], fy_r.at[k - 1])
    total = y_own[...]
    for k in range(1, Y):
        total = total + y_recv[k - 1].astype(F32)
    y_own[...] = total
    z_send[...] = total.astype(BF16)
    for k in range(1, Z):
        to = step(z, k, Z)
        send(z_send.at[to], z_recv.at[k - 1], fz_s.at[k - 1], fz_r.at[k - 1], patch_0=to)

    over_mp(1)

    ZR = HC // Z
    for which in range(2):
        total = g_own[which, x]
        for k in range(1, X):
            arrive(gx_recv.at[which, k - 1], gx_r.at[which, k - 1])
            total = total + gx_recv[which, k - 1].astype(F32)
        g_own[which, x] = total
        gz_send[:, which] = total.reshape(Z, ZR, F).astype(BF16)
    for k in range(1, Z):
        to = step(z, k, Z)
        send(gz_send.at[to], gz_recv.at[k - 1], gz_s.at[k - 1], gz_r.at[k - 1], patch_0=to)

    total = y_own[z]
    for k in range(1, Z):
        arrive(z_recv.at[k - 1], fz_r.at[k - 1])
        total = total + z_recv[k - 1].astype(F32)
    for q in range(X):
        x_send[q] = total[:, q * F : (q + 1) * F]
    own_sum = pltpu.make_async_copy(x_send.at[x], x_recv.at[x], loc.at[0])
    own_sum.start()
    for k in range(1, X):
        to = step(x, k, X)
        send(x_send.at[to], x_recv.at[x], fx_s.at[k - 1], fx_r.at[k - 1], mp=to)

    total = g_own[:, x, pl.ds(pl.multiple_of(z * ZR, ZR), ZR)]
    for k in range(1, Z):
        arrive(gz_recv.at[k - 1], gz_r.at[k - 1])
        total = total + gz_recv[k - 1].astype(F32)
    gy[y] = total
    for k in range(1, Y):
        to = step(y, k, Y)
        send(gy.at[y], gy.at[y], gy_s.at[k - 1], gy_r.at[k - 1], patch_1=to)

    own_sum.wait()
    for k in range(1, X):
        arrive(x_recv.at[step(x, X - k, X)], fx_r.at[k - 1])
    loads["latent"].wait()
    mesh_out[...] = (latent_ref[...].astype(F32) + x_recv[...].reshape(PATCH, F)).astype(BF16)

    for k in range(1, Y):
        arrive(gy.at[step(y, Y - k, Y)], gy_r.at[k - 1])
    total = gy[0]
    for yy in range(1, Y):
        total = total + gy[yy]
    own[...] = total.astype(BF16)
    for k in range(1, Z):
        to = step(z, k, Z)
        send(own, fin.at[c, z], az_s.at[k - 1], az_r.at[k - 1], patch_0=to)
    fin[c, z] = own[...]
    for k in range(1, Z):
        arrive(fin.at[c, step(z, Z - k, Z)], az_r.at[k - 1])
    send(fin.at[c], fin.at[c], ac_s.at[0], ac_r.at[0], patch_2=oc)
    arrive(fin.at[oc], ac_r.at[0])
    for core in range(2):
        rows = slice(core * HC, (core + 1) * HC)
        second_out[rows, :] = fin[core, :, 0].reshape(HC, F).astype(F32)
        first_out[rows, :] = fin[core, :, 1].reshape(HC, F).astype(F32)

    pltpu.make_async_remote_copy(
        src_ref=all_but_one(slots, NP),
        dst_ref=all_but_one(V, NP),
        send_sem=w_s,
        recv_sem=w_r.at[0],
        device_id={"patch_0": z, "patch_1": y, "patch_2": oc, "mp": x},
        device_id_type=pl.DeviceIdType.MESH,
    ).wait_send()
    for src, dst, ss, rs in sent:
        pltpu.make_async_copy(src, src, ss).wait()


def all_but_one(ref, n):
    return ref.at[pl.ds(0, n - 1)]


def per_device(
    grid_latent,
    mesh_latent,
    edge_weight,
    block_source,
    block_live,
    mlp_first,
    mlp_second,
    mesh_cotangent,
):
    Z, Y, C = (lax.axis_size(a) for a in PATCH_AXES)
    X = lax.axis_size("mp")
    NP = Z * Y * C
    R, D = grid_latent.shape
    H = mlp_first.shape[1]
    F = mlp_second.shape[1]
    PX = PATCH // X
    GPD = R // PATCH
    HC = D // 2
    ZR = HC // Z
    scaling = 1.0 / math.sqrt(R * NP)

    vm = pltpu.VMEM
    dma = pltpu.SemaphoreType.DMA
    scratch = [
        vm((1, PATCH), F32),
        vm(grid_latent.shape, BF16),
        vm(mesh_latent.shape, BF16),
        vm(edge_weight.shape, BF16),
        vm(mlp_first.shape, BF16),
        vm(mlp_second.shape, BF16),
        vm(mesh_cotangent.shape, BF16),
        vm((NP, PX, PATCH), BF16),
        vm((NP, PX, PATCH), BF16),
        vm((C, Y, Z, PX, D), BF16),
        vm((C, Y, Z, 1, PATCH), F32),
        vm((H, D), BF16),
        vm((R, H), F32),
        vm((R, H), BF16),
        vm((R, D), BF16),
        vm((NP * PX, R), BF16),
        vm((R, NP * PX), BF16),
        vm((Y, Z, PX, D), BF16),
        vm((Y, Z, PX, D), BF16),
        vm((Y - 1, Z, PX, D), BF16),
        vm((Y - 1, Z, PX, D), BF16),
        vm((Z, PX, D), F32),
        vm((Z, PX, D), BF16),
        vm((Z - 1, PX, D), BF16),
        vm((X, PX, F), F32),
        vm((X, PX, F), F32),
        vm((R, D), BF16),
        vm((R, H), BF16),
        vm((2, X, HC, F), F32),
        vm((2, X, HC, F), F32),
        vm((2, X, HC, F), F32),
        vm((2, X - 1, HC, F), BF16),
        vm((2, X - 1, HC, F), BF16),
        vm((Z, 2, ZR, F), BF16),
        vm((Z - 1, 2, ZR, F), BF16),
        vm((Y, 2, ZR, F), F32),
        vm((2, ZR, F), BF16),
        vm((C, Z, 2, ZR, F), BF16),
        dma,
        dma((C * Y,)),
        dma((X - 1,)),
        dma((X - 1,)),
        dma((X - 1,)),
        dma((X - 1,)),
        dma((2, Z // 2)),
        dma((2, Z // 2)),
        dma((2, Z)),
        dma((2, Z)),
        dma((2, Z)),
        dma((2, Z)),
        dma((4,)),
        dma((4,)),
        dma((Z - 1,)),
        dma((Z - 1,)),
        dma((Y - 1,)),
        dma((Y - 1,)),
        dma((1,)),
        dma((1,)),
        dma((Y,)),
        dma((Y,)),
        dma((Y - 1,)),
        dma((Y - 1,)),
        dma((Z - 1,)),
        dma((Z - 1,)),
        dma((X - 1,)),
        dma((X - 1,)),
        dma((2,)),
        dma((2,)),
        dma((2, X - 1)),
        dma((2, X - 1)),
        dma((Z - 1,)),
        dma((Z - 1,)),
        dma((Y - 1,)),
        dma((Y - 1,)),
        dma((Z - 1,)),
        dma((Z - 1,)),
        dma((1,)),
        dma((1,)),
        dma((4,)),
        dma((6,)),
    ]
    in_vmem = pl.BlockSpec(memory_space=pltpu.VMEM)
    mesh_out, grad_first, grad_second = pl.pallas_call(
        functools.partial(kernel, (Z, Y, C, X), scaling),
        out_shape=(
            jax.ShapeDtypeStruct((PATCH, F), BF16),
            jax.ShapeDtypeStruct((D, F), F32),
            jax.ShapeDtypeStruct((H, F), F32),
        ),
        in_specs=[pl.BlockSpec(memory_space=pltpu.SMEM)] * 2
        + [pl.BlockSpec(memory_space=pl.ANY)] * 6,
        out_specs=(in_vmem, in_vmem, in_vmem),
        scratch_shapes=scratch,
        compiler_params=pltpu.CompilerParams(
            collective_id=0, has_side_effects=True, vmem_limit_bytes=62 * 1024 * 1024
        ),
    )(
        block_source,
        block_live,
        grid_latent,
        mesh_latent,
        edge_weight,
        mlp_first,
        mlp_second,
        mesh_cotangent,
    )
    return mesh_out, grad_first, grad_second


def torus_of(mesh):
    return Mesh(mesh.devices.reshape(8, 4, 2, mesh.shape["mp"]), AXES)


def solution(mesh):
    torus = torus_of(mesh)
    in_specs = (
        P(PATCH_AXES, None),
        P(PATCH_AXES, "mp"),
        P(PATCH_AXES, None, None),
        P(PATCH_AXES),
        P(PATCH_AXES),
        P(),
        P(None, "mp"),
        P(PATCH_AXES, "mp"),
    )
    out_specs = (P(PATCH_AXES, "mp"), P(None, "mp"), P(None, "mp"))
    return jax.shard_map(
        per_device, mesh=torus, in_specs=in_specs, out_specs=out_specs, check_vma=False
    )
```

```python
import functools
import math

import jax
import jax.numpy as jnp
from jax import lax
from jax.experimental import pallas as pl
from jax.experimental.pallas import tpu as pltpu
from jax.sharding import Mesh
from jax.sharding import PartitionSpec as P

PATCH = 128
PATCH_AXES = ("patch_0", "patch_1", "patch_2")
AXES = PATCH_AXES + ("mp",)
F32 = jnp.float32
BF16 = jnp.bfloat16


def dot(a, b, dims=((1,), (0,))):
    return lax.dot_general(a, b, (dims, ((), ())), preferred_element_type=F32)


def kernel(
    sizes,
    scaling,
    source_ref,
    live_ref,
    grid_in,
    latent_in,
    w_in,
    first_in,
    second_in,
    cot_in,
    mesh_out,
    first_out,
    second_out,
    meta_ref,
    grid_ref,
    latent_ref,
    w_ref,
    first_ref,
    second_ref,
    cot_ref,
    slots,
    V,
    cotb,
    metab,
    second,
    slope,
    hidden,
    msg,
    vbig,
    vbig_t,
    c_send,
    c_recv,
    y_send,
    y_recv,
    y_own,
    z_send,
    z_recv,
    x_send,
    x_recv,
    gm,
    gpre,
    gc_send,
    gc_recv,
    g_own,
    gx_send,
    gx_recv,
    gz_send,
    gz_recv,
    gy,
    own,
    fin,
    w_s,
    w_r,
    sec_s,
    sec_r,
    cx_s,
    cx_r,
    cz_s,
    cz_r,
    cy_s,
    cy_r,
    cc_s,
    cc_r,
    mz_s,
    mz_r,
    my_s,
    my_r,
    mc_s,
    mc_r,
    fc_s,
    fc_r,
    fy_s,
    fy_r,
    fz_s,
    fz_r,
    fx_s,
    fx_r,
    gc_s,
    gc_r,
    gx_s,
    gx_r,
    gz_s,
    gz_r,
    gy_s,
    gy_r,
    az_s,
    az_r,
    ac_s,
    ac_r,
    loc,
    load_s,
):
    Z, Y, C, X = sizes
    NP = Z * Y * C
    R, D = grid_in.shape
    H = first_in.shape[1]
    F = second_in.shape[1]
    PX = PATCH // X
    GPD = R // PATCH
    HC = D // 2
    z, y, c, x = (lax.axis_index(a) for a in AXES)
    oc = 1 - c
    sent = []

    def send(src, dst, ss, rs, **where):
        place = {"patch_0": z, "patch_1": y, "patch_2": c, "mp": x}
        place.update(where)
        copy = pltpu.make_async_remote_copy(
            src_ref=src,
            dst_ref=dst,
            send_sem=ss,
            recv_sem=rs,
            device_id=place,
            device_id_type=pl.DeviceIdType.MESH,
        )
        copy.start()
        sent.append((src, dst, ss, rs))

    def arrive(dst, rs):
        pltpu.make_async_copy(dst, dst, rs).wait()

    def step(i, k, n):
        return lax.rem(i + k, n)

    xf = pl.ds(pl.multiple_of(x * F, F), F)
    xp = pl.ds(pl.multiple_of(x * PX, PX), PX)

    loads = {}
    for i, (name, src, dst) in enumerate(
        (
            ("cot", cot_in, cot_ref),
            ("w", w_in, w_ref),
            ("second", second_in, second_ref),
            ("grid", grid_in, grid_ref),
            ("first", first_in, first_ref),
            ("latent", latent_in, latent_ref),
        )
    ):
        loads[name] = pltpu.make_async_copy(src, dst, load_s.at[i])
        loads[name].start()

    barrier = pltpu.get_barrier_semaphore()

    def greet(j, carry):
        dz, dy, dc = j // (Y * 2), (j // 2) % Y, j % 2
        pl.semaphore_signal(
            barrier,
            inc=1,
            device_id={
                "patch_0": lax.rem(z + dz, Z),
                "patch_1": lax.rem(y + dy, Y),
                "patch_2": lax.rem(c + dc, 2),
                "mp": x,
            },
            device_id_type=pl.DeviceIdType.MESH,
        )
        return carry

    def greet_mp(j, carry):
        pl.semaphore_signal(
            barrier,
            inc=1,
            device_id={
                "patch_0": lax.rem(z + j % Z, Z),
                "patch_1": y,
                "patch_2": c,
                "mp": lax.rem(x + j // Z, X),
            },
            device_id_type=pl.DeviceIdType.MESH,
        )
        return carry

    lax.fori_loop(1, NP, greet, 0)
    lax.fori_loop(Z, X * Z, greet_mp, 0)

    n_slots = w_in.shape[0]

    def feeder(j):
        return jnp.where(live_ref[j] == 1, lax.div(source_ref[j], GPD), -1)

    lane = lax.broadcasted_iota(jnp.int32, (1, PATCH), 1)
    meta = jnp.zeros((1, PATCH), F32)
    for j in range(n_slots):
        inside = lax.rem(source_ref[j], GPD).astype(F32)
        meta = jnp.where(lane == feeder(j), inside, meta)
    meta_ref[...] = meta
    loads["w"].wait()

    def pack(i, carry):
        c1, y1, z1 = i // (Y * Z), (i // Z) % Y, i % Z
        natural = (z1 * Y + y1) * 2 + c1
        slot, live = jnp.int32(0), jnp.int32(0)
        for j in range(n_slots):
            hit = feeder(j) == natural
            slot = jnp.where(hit, j, slot)
            live = jnp.where(hit, 1, live)
        block = w_ref[slot, xp, :]
        slots[i] = (block.astype(F32) * live.astype(F32)).astype(BF16)
        return carry

    lax.fori_loop(0, NP, pack, 0)
    loads["cot"].wait()
    loads["second"].wait()
    own_cot = pltpu.make_async_copy(cot_ref.at[xp, :], cotb.at[c, y, z, :, xf], loc.at[0])
    own_cot.start()
    own_second = pltpu.make_async_copy(second_ref, second.at[:, xf], loc.at[1])
    own_second.start()
    own_meta = pltpu.make_async_copy(meta_ref, metab.at[c, y, z], loc.at[2])
    own_meta.start()
    here = (c * Y + y) * Z + z
    own_slot = pltpu.make_async_copy(slots.at[here], V.at[here], loc.at[3])
    own_slot.start()
    pl.semaphore_wait(barrier, NP - 1 + (X - 1) * Z)

    own_meta.wait()
    near = [0]
    for t in range(1, Z // 2 + 1):
        near += [t, Z - t] if 2 * t < Z else [t]
    for k in near:
        for m in range(X):
            if k or m:
                to = step(x, m, X)
                rows = pl.ds(pl.multiple_of(to * PX, PX), PX)
                send(
                    cot_ref.at[rows, :],
                    cotb.at[c, y, z, :, xf],
                    cz_s.at[k, m],
                    cz_r.at[k],
                    patch_0=step(z, k, Z),
                    mp=to,
                )
        if k:
            send(
                metab.at[c, y, z],
                metab.at[c, y, z],
                mz_s.at[k - 1],
                mz_r.at[k - 1],
                patch_0=step(z, k, Z),
            )
    for k in range(1, X):
        to = step(x, k, X)
        send(second_ref, second.at[:, xf], sec_s.at[k - 1], sec_r.at[k - 1], mp=to)

    def send_slot(j, carry):
        dz, dy, dc = j // (Y * 2), (j // 2) % Y, j % 2
        z1, y1, c1 = lax.rem(z + dz, Z), lax.rem(y + dy, Y), lax.rem(c + dc, 2)
        pltpu.make_async_remote_copy(
            src_ref=slots.at[(c1 * Y + y1) * Z + z1],
            dst_ref=V.at[here],
            send_sem=w_s,
            recv_sem=w_r.at[c * Y + y],
            device_id={"patch_0": z1, "patch_1": y1, "patch_2": c1, "mp": x},
            device_id_type=pl.DeviceIdType.MESH,
        ).start()
        return carry

    lax.fori_loop(1, NP, send_slot, 0)

    TR = 2 * PATCH
    T = R // TR

    def first_layer(i):
        rows = pl.ds(i * TR, TR)
        pre = dot(grid_ref[rows, :], first_ref[...])
        s = jax.nn.sigmoid(pre)
        hidden[rows, :] = (pre * s).astype(BF16)
        slope[rows, :] = s * (1.0 + pre * (1.0 - s))

    def second_layer(i):
        rows = pl.ds(i * TR, TR)
        msg[rows, :] = dot(hidden[rows, :], second[...]).astype(BF16)

    def over_y(k):
        at = step(z, (Z - k) % Z, Z)
        if k:
            arrive(cotb.at[c, y, at], cz_r.at[k])
        else:
            own_cot.wait()
            arrive(cotb.at[c, y, at, :, pl.ds(0, (X - 1) * F)], cz_r.at[k])
        for m in range(1, Y):
            block = cotb.at[c, y, at]
            send(block, block, cy_s.at[m - 1, k], cy_r.at[m - 1], patch_1=step(y, m, Y))

    loads["grid"].wait()
    loads["first"].wait()
    per = -(-Z // T)
    for i in range(T):
        first_layer(i)
        for k in near[i * per : (i + 1) * per]:
            over_y(k)
    for k in range(1, Z):
        arrive(metab.at[c, y, step(z, Z - k, Z)], mz_r.at[k - 1])
    for m in range(1, Y):
        to = step(y, m, Y)
        send(metab.at[c, y], metab.at[c, y], my_s.at[m - 1], my_r.at[m - 1], patch_1=to)
    send(cotb.at[c, y], cotb.at[c, y], cc_s.at[0], cc_r.at[0], patch_2=oc)
    own_second.wait()
    for k in range(1, X):
        frm = step(x, X - k, X)
        arrive(second.at[:, pl.ds(pl.multiple_of(frm * F, F), F)], sec_r.at[k - 1])
    for i in range(T):
        second_layer(i)
    for m in range(1, Y):
        arrive(metab.at[c, step(y, Y - m, Y)], my_r.at[m - 1])
    send(metab.at[c], metab.at[c], mc_s.at[0], mc_r.at[0], patch_2=oc)
    for m in range(1, Y):
        frm = step(y, Y - m, Y)
        arrive(cotb.at[c, frm], cy_r.at[m - 1])
        send(cotb.at[c, frm], cotb.at[c, frm], cc_s.at[m], cc_r.at[m], patch_2=oc)
    arrive(metab.at[oc], mc_r.at[0])

    own_slot.wait()
    own_natural = (z * Y + y) * 2 + c
    lanes = lax.broadcasted_iota(jnp.int32, (Z, PATCH), 1)
    TC = Z * PX

    def spread(i, carry):
        meta = metab[i // Y, lax.rem(i, Y)].reshape(Z, PATCH)
        patch_of = jnp.sum(jnp.where(lanes == own_natural, meta, 0.0), axis=1, keepdims=True)
        patch_rows = jnp.broadcast_to(
            jnp.broadcast_to(patch_of, (Z, PATCH))[:, None, :], (Z, PX, PATCH)
        ).reshape(TC, PATCH)
        blocks = V[pl.ds(pl.multiple_of(i * Z, Z), Z)].reshape(TC, PATCH).astype(F32)
        rows = pl.ds(pl.multiple_of(i * TC, TC), TC)
        blocks_t = blocks.T
        patch_cols = patch_rows.T
        for g in range(GPD):
            vbig[rows, g * PATCH : (g + 1) * PATCH] = jnp.where(
                patch_rows == float(g), blocks, 0.0
            ).astype(BF16)
            vbig_t[g * PATCH : (g + 1) * PATCH, rows] = jnp.where(
                patch_cols == float(g), blocks_t, 0.0
            ).astype(BF16)
        return carry

    own_g = c * Y + y
    arrive(V.at[pl.ds(0, Z - 1)], w_r.at[own_g])
    for k in range(1, C * Y):
        arrive(V.at[pl.ds(0, Z)], w_r.at[lax.rem(own_g + k, C * Y)])
    lax.fori_loop(0, C * Y, spread, 0)


    def contribution(core, yy):
        at = pl.multiple_of((core * Y + yy) * TC, TC)
        return dot(vbig[pl.ds(at, TC), :], msg[...])

    for k in range(1, Y + 1):
        yy = step(y, k % Y, Y)
        c_send[yy] = contribution(oc, yy).astype(BF16).reshape(Z, PX, D)
        send(c_send.at[yy], c_recv.at[yy], fc_s.at[k - 1], fc_r.at[k - 1], patch_2=oc)
    for k in range(1, Y + 1):
        yy = step(y, k % Y, Y)
        part = contribution(c, yy)
        arrive(c_recv.at[yy], fc_r.at[k - 1])
        part = part + c_recv[yy].astype(F32).reshape(TC, D)
        if k < Y:
            y_send[k - 1] = part.astype(BF16).reshape(Z, PX, D)
            send(y_send.at[k - 1], y_recv.at[k - 1], fy_s.at[k - 1], fy_r.at[k - 1], patch_1=yy)
        else:
            y_own[...] = part.reshape(Z, PX, D)

    for m in range(Y):
        arrive(cotb.at[oc, step(y, Y - m, Y)], cc_r.at[m])

    def message_gradient(i, carry):
        rows = pl.ds(pl.multiple_of(i * TR, TR), TR)
        gm[rows, :] = dot(vbig_t[rows, :], cotb[...].reshape(NP * PX, D)).astype(BF16)
        return carry

    lax.fori_loop(0, R // TR, message_gradient, 0)

    def halves(which, left_ref, right_ref):
        for core in (oc, c):
            cols = pl.ds(pl.multiple_of(core * HC, HC), HC)
            part = dot(left_ref[:, cols], right_ref[...], ((0,), (0,))) * scaling
            for q in range(X):
                piece = part[:, q * F : (q + 1) * F]
                if core is oc:
                    gc_send[which, q] = piece
                else:
                    g_own[which, q] = piece
            if core is oc:
                send(
                    gc_send.at[which],
                    gc_recv.at[which],
                    gc_s.at[which],
                    gc_r.at[which],
                    patch_2=oc,
                )

    def over_mp(which):
        arrive(gc_recv.at[which], gc_r.at[which])
        for k in range(1, X):
            to = step(x, k, X)
            gx_send[which, k - 1] = (g_own[which, to] + gc_recv[which, to]).astype(BF16)
            send(
                gx_send.at[which, k - 1],
                gx_recv.at[which, k - 1],
                gx_s.at[which, k - 1],
                gx_r.at[which, k - 1],
                mp=to,
            )
        g_own[which, x] = g_own[which, x] + gc_recv[which, x]

    halves(0, hidden, gm)

    def pre_gradient(i, carry):
        rows = pl.ds(pl.multiple_of(i * TR, TR), TR)
        back = dot(gm[rows, :], second[...], ((1,), (1,)))
        gpre[rows, :] = (back * slope[rows, :]).astype(BF16)
        return carry

    lax.fori_loop(0, R // TR, pre_gradient, 0)
    over_mp(0)

    halves(1, grid_ref, gpre)

    for k in range(1, Y):
        arrive(y_recv.at[k - 1], fy_r.at[k - 1])
    total = y_own[...]
    for k in range(1, Y):
        total = total + y_recv[k - 1].astype(F32)
    y_own[...] = total
    z_send[...] = total.astype(BF16)
    for k in range(1, Z):
        to = step(z, k, Z)
        send(z_send.at[to], z_recv.at[k - 1], fz_s.at[k - 1], fz_r.at[k - 1], patch_0=to)

    over_mp(1)

    ZR = HC // Z
    for which in range(2):
        total = g_own[which, x]
        for k in range(1, X):
            arrive(gx_recv.at[which, k - 1], gx_r.at[which, k - 1])
            total = total + gx_recv[which, k - 1].astype(F32)
        g_own[which, x] = total
        gz_send[:, which] = total.reshape(Z, ZR, F).astype(BF16)
    for k in range(1, Z):
        to = step(z, k, Z)
        send(gz_send.at[to], gz_recv.at[k - 1], gz_s.at[k - 1], gz_r.at[k - 1], patch_0=to)

    total = y_own[z]
    for k in range(1, Z):
        arrive(z_recv.at[k - 1], fz_r.at[k - 1])
        total = total + z_recv[k - 1].astype(F32)
    for q in range(X):
        x_send[q] = total[:, q * F : (q + 1) * F]
    own_sum = pltpu.make_async_copy(x_send.at[x], x_recv.at[x], loc.at[0])
    own_sum.start()
    for k in range(1, X):
        to = step(x, k, X)
        send(x_send.at[to], x_recv.at[x], fx_s.at[k - 1], fx_r.at[k - 1], mp=to)

    total = g_own[:, x, pl.ds(pl.multiple_of(z * ZR, ZR), ZR)]
    for k in range(1, Z):
        arrive(gz_recv.at[k - 1], gz_r.at[k - 1])
        total = total + gz_recv[k - 1].astype(F32)
    gy[y] = total
    for k in range(1, Y):
        to = step(y, k, Y)
        send(gy.at[y], gy.at[y], gy_s.at[k - 1], gy_r.at[k - 1], patch_1=to)

    own_sum.wait()
    for k in range(1, X):
        arrive(x_recv.at[step(x, X - k, X)], fx_r.at[k - 1])
    loads["latent"].wait()
    mesh_out[...] = (latent_ref[...].astype(F32) + x_recv[...].reshape(PATCH, F)).astype(BF16)

    for k in range(1, Y):
        arrive(gy.at[step(y, Y - k, Y)], gy_r.at[k - 1])
    total = gy[0]
    for yy in range(1, Y):
        total = total + gy[yy]
    own[...] = total.astype(BF16)
    for k in range(1, Z):
        to = step(z, k, Z)
        send(own, fin.at[c, z], az_s.at[k - 1], az_r.at[k - 1], patch_0=to)
    fin[c, z] = own[...]
    for k in range(1, Z):
        arrive(fin.at[c, step(z, Z - k, Z)], az_r.at[k - 1])
    send(fin.at[c], fin.at[c], ac_s.at[0], ac_r.at[0], patch_2=oc)
    arrive(fin.at[oc], ac_r.at[0])
    for core in range(2):
        rows = slice(core * HC, (core + 1) * HC)
        second_out[rows, :] = fin[core, :, 0].reshape(HC, F).astype(F32)
        first_out[rows, :] = fin[core, :, 1].reshape(HC, F).astype(F32)

    pltpu.make_async_remote_copy(
        src_ref=all_but_one(slots, NP),
        dst_ref=all_but_one(V, NP),
        send_sem=w_s,
        recv_sem=w_r.at[0],
        device_id={"patch_0": z, "patch_1": y, "patch_2": oc, "mp": x},
        device_id_type=pl.DeviceIdType.MESH,
    ).wait_send()
    for src, dst, ss, rs in sent:
        pltpu.make_async_copy(src, src, ss).wait()


def all_but_one(ref, n):
    return ref.at[pl.ds(0, n - 1)]


def per_device(
    grid_latent,
    mesh_latent,
    edge_weight,
    block_source,
    block_live,
    mlp_first,
    mlp_second,
    mesh_cotangent,
):
    Z, Y, C = (lax.axis_size(a) for a in PATCH_AXES)
    X = lax.axis_size("mp")
    NP = Z * Y * C
    R, D = grid_latent.shape
    H = mlp_first.shape[1]
    F = mlp_second.shape[1]
    PX = PATCH // X
    GPD = R // PATCH
    HC = D // 2
    ZR = HC // Z
    scaling = 1.0 / math.sqrt(R * NP)

    vm = pltpu.VMEM
    dma = pltpu.SemaphoreType.DMA
    scratch = [
        vm((1, PATCH), F32),
        vm(grid_latent.shape, BF16),
        vm(mesh_latent.shape, BF16),
        vm(edge_weight.shape, BF16),
        vm(mlp_first.shape, BF16),
        vm(mlp_second.shape, BF16),
        vm(mesh_cotangent.shape, BF16),
        vm((NP, PX, PATCH), BF16),
        vm((NP, PX, PATCH), BF16),
        vm((C, Y, Z, PX, D), BF16),
        vm((C, Y, Z, 1, PATCH), F32),
        vm((H, D), BF16),
        vm((R, H), F32),
        vm((R, H), BF16),
        vm((R, D), BF16),
        vm((NP * PX, R), BF16),
        vm((R, NP * PX), BF16),
        vm((Y, Z, PX, D), BF16),
        vm((Y, Z, PX, D), BF16),
        vm((Y - 1, Z, PX, D), BF16),
        vm((Y - 1, Z, PX, D), BF16),
        vm((Z, PX, D), F32),
        vm((Z, PX, D), BF16),
        vm((Z - 1, PX, D), BF16),
        vm((X, PX, F), F32),
        vm((X, PX, F), F32),
        vm((R, D), BF16),
        vm((R, H), BF16),
        vm((2, X, HC, F), F32),
        vm((2, X, HC, F), F32),
        vm((2, X, HC, F), F32),
        vm((2, X - 1, HC, F), BF16),
        vm((2, X - 1, HC, F), BF16),
        vm((Z, 2, ZR, F), BF16),
        vm((Z - 1, 2, ZR, F), BF16),
        vm((Y, 2, ZR, F), F32),
        vm((2, ZR, F), BF16),
        vm((C, Z, 2, ZR, F), BF16),
        dma,
        dma((C * Y,)),
        dma((X - 1,)),
        dma((X - 1,)),
        dma((X - 1,)),
        dma((X - 1,)),
        dma((Z, X)),
        dma((Z,)),
        dma((Y - 1, Z)),
        dma((Y - 1,)),
        dma((4,)),
        dma((4,)),
        dma((Z - 1,)),
        dma((Z - 1,)),
        dma((Y - 1,)),
        dma((Y - 1,)),
        dma((1,)),
        dma((1,)),
        dma((Y,)),
        dma((Y,)),
        dma((Y - 1,)),
        dma((Y - 1,)),
        dma((Z - 1,)),
        dma((Z - 1,)),
        dma((X - 1,)),
        dma((X - 1,)),
        dma((2,)),
        dma((2,)),
        dma((2, X - 1)),
        dma((2, X - 1)),
        dma((Z - 1,)),
        dma((Z - 1,)),
        dma((Y - 1,)),
        dma((Y - 1,)),
        dma((Z - 1,)),
        dma((Z - 1,)),
        dma((1,)),
        dma((1,)),
        dma((4,)),
        dma((6,)),
    ]
    in_vmem = pl.BlockSpec(memory_space=pltpu.VMEM)
    mesh_out, grad_first, grad_second = pl.pallas_call(
        functools.partial(kernel, (Z, Y, C, X), scaling),
        out_shape=(
            jax.ShapeDtypeStruct((PATCH, F), BF16),
            jax.ShapeDtypeStruct((D, F), F32),
            jax.ShapeDtypeStruct((H, F), F32),
        ),
        in_specs=[pl.BlockSpec(memory_space=pltpu.SMEM)] * 2
        + [pl.BlockSpec(memory_space=pl.ANY)] * 6,
        out_specs=(in_vmem, in_vmem, in_vmem),
        scratch_shapes=scratch,
        compiler_params=pltpu.CompilerParams(
            collective_id=0, has_side_effects=True, vmem_limit_bytes=62 * 1024 * 1024
        ),
    )(
        block_source,
        block_live,
        grid_latent,
        mesh_latent,
        edge_weight,
        mlp_first,
        mlp_second,
        mesh_cotangent,
    )
    return mesh_out, grad_first, grad_second


def torus_of(mesh):
    return Mesh(mesh.devices.reshape(8, 4, 2, mesh.shape["mp"]), AXES)


def solution(mesh):
    torus = torus_of(mesh)
    in_specs = (
        P(PATCH_AXES, None),
        P(PATCH_AXES, "mp"),
        P(PATCH_AXES, None, None),
        P(PATCH_AXES),
        P(PATCH_AXES),
        P(),
        P(None, "mp"),
        P(PATCH_AXES, "mp"),
    )
    out_specs = (P(PATCH_AXES, "mp"), P(None, "mp"), P(None, "mp"))
    return jax.shard_map(
        per_device, mesh=torus, in_specs=in_specs, out_specs=out_specs, check_vma=False
    )
```

```python
import functools
import math

import jax
import jax.numpy as jnp
from jax import lax
from jax.experimental import pallas as pl
from jax.experimental.pallas import tpu as pltpu
from jax.sharding import Mesh
from jax.sharding import PartitionSpec as P

PATCH = 128
PATCH_AXES = ("patch_0", "patch_1", "patch_2")
AXES = PATCH_AXES + ("mp",)
F32 = jnp.float32
BF16 = jnp.bfloat16


def dot(a, b, dims=((1,), (0,))):
    return lax.dot_general(a, b, (dims, ((), ())), preferred_element_type=F32)


def kernel(
    sizes,
    scaling,
    source_ref,
    live_ref,
    grid_in,
    latent_in,
    w_in,
    first_in,
    second_in,
    cot_in,
    mesh_out,
    fin,
    meta_ref,
    grid_ref,
    latent_ref,
    w_ref,
    first_ref,
    second_ref,
    cot_ref,
    slots,
    V,
    cotb,
    metab,
    second,
    slope,
    hidden,
    msg,
    vbig,
    vbig_t,
    c_send,
    c_recv,
    y_send,
    y_recv,
    y_own,
    z_send,
    z_recv,
    x_send,
    x_recv,
    gm,
    gpre,
    gc_send,
    gc_recv,
    g_own,
    gx_send,
    gx_recv,
    gz_send,
    gz_recv,
    gy,
    own,
    w_s,
    w_r,
    sec_s,
    sec_r,
    cx_s,
    cx_r,
    cz_s,
    cz_r,
    cy_s,
    cy_r,
    cc_s,
    cc_r,
    mz_s,
    mz_r,
    my_s,
    my_r,
    mc_s,
    mc_r,
    fc_s,
    fc_r,
    fy_s,
    fy_r,
    fz_s,
    fz_r,
    fx_s,
    fx_r,
    gc_s,
    gc_r,
    gx_s,
    gx_r,
    gz_s,
    gz_r,
    gy_s,
    gy_r,
    az_s,
    az_r,
    ac_s,
    ac_r,
    loc,
    load_s,
):
    Z, Y, C, X = sizes
    NP = Z * Y * C
    R, D = grid_in.shape
    H = first_in.shape[1]
    F = second_in.shape[1]
    PX = PATCH // X
    GPD = R // PATCH
    HC = D // 2
    z, y, c, x = (lax.axis_index(a) for a in AXES)
    oc = 1 - c
    sent = []

    def send(src, dst, ss, rs, **where):
        place = {"patch_0": z, "patch_1": y, "patch_2": c, "mp": x}
        place.update(where)
        copy = pltpu.make_async_remote_copy(
            src_ref=src,
            dst_ref=dst,
            send_sem=ss,
            recv_sem=rs,
            device_id=place,
            device_id_type=pl.DeviceIdType.MESH,
        )
        copy.start()
        sent.append((src, dst, ss, rs))

    def arrive(dst, rs):
        pltpu.make_async_copy(dst, dst, rs).wait()

    def step(i, k, n):
        return lax.rem(i + k, n)

    xf = pl.ds(pl.multiple_of(x * F, F), F)
    xp = pl.ds(pl.multiple_of(x * PX, PX), PX)

    loads = {}
    for i, (name, src, dst) in enumerate(
        (
            ("cot", cot_in, cot_ref),
            ("w", w_in, w_ref),
            ("second", second_in, second_ref),
            ("grid", grid_in, grid_ref),
            ("first", first_in, first_ref),
            ("latent", latent_in, latent_ref),
        )
    ):
        loads[name] = pltpu.make_async_copy(src, dst, load_s.at[i])
        loads[name].start()

    barrier = pltpu.get_barrier_semaphore()

    def greet(j, carry):
        dz, dy, dc = j // (Y * 2), (j // 2) % Y, j % 2
        pl.semaphore_signal(
            barrier,
            inc=1,
            device_id={
                "patch_0": lax.rem(z + dz, Z),
                "patch_1": lax.rem(y + dy, Y),
                "patch_2": lax.rem(c + dc, 2),
                "mp": x,
            },
            device_id_type=pl.DeviceIdType.MESH,
        )
        return carry

    def greet_mp(j, carry):
        pl.semaphore_signal(
            barrier,
            inc=1,
            device_id={
                "patch_0": lax.rem(z + j % Z, Z),
                "patch_1": y,
                "patch_2": c,
                "mp": lax.rem(x + j // Z, X),
            },
            device_id_type=pl.DeviceIdType.MESH,
        )
        return carry

    lax.fori_loop(1, NP, greet, 0)
    lax.fori_loop(Z, X * Z, greet_mp, 0)

    n_slots = w_in.shape[0]

    def feeder(j):
        return jnp.where(live_ref[j] == 1, lax.div(source_ref[j], GPD), -1)

    lane = lax.broadcasted_iota(jnp.int32, (1, PATCH), 1)
    meta = jnp.zeros((1, PATCH), F32)
    for j in range(n_slots):
        inside = lax.rem(source_ref[j], GPD).astype(F32)
        meta = jnp.where(lane == feeder(j), inside, meta)
    meta_ref[...] = meta
    loads["w"].wait()

    def pack(i, carry):
        z1, c1, y1 = i // (2 * Y), (i // Y) % 2, i % Y
        natural = (z1 * Y + y1) * 2 + c1
        slot, live = jnp.int32(0), jnp.int32(0)
        for j in range(n_slots):
            hit = feeder(j) == natural
            slot = jnp.where(hit, j, slot)
            live = jnp.where(hit, 1, live)
        block = w_ref[slot, xp, :]
        slots[i] = (block.astype(F32) * live.astype(F32)).astype(BF16)
        return carry

    lax.fori_loop(0, NP, pack, 0)
    loads["cot"].wait()
    loads["second"].wait()
    own_cot = pltpu.make_async_copy(cot_ref.at[xp, :], cotb.at[z, c, y, :, xf], loc.at[0])
    own_cot.start()
    own_second = pltpu.make_async_copy(second_ref, second.at[:, xf], loc.at[1])
    own_second.start()
    own_meta = pltpu.make_async_copy(meta_ref, metab.at[z, c, y], loc.at[2])
    own_meta.start()
    here = (z * 2 + c) * Y + y
    own_slot = pltpu.make_async_copy(slots.at[here], V.at[here], loc.at[3])
    own_slot.start()
    pl.semaphore_wait(barrier, NP - 1 + (X - 1) * Z)

    own_meta.wait()
    near = [0]
    for t in range(1, Z // 2 + 1):
        near += [t, Z - t] if 2 * t < Z else [t]
    for k in near:
        for m in range(X):
            if k or m:
                to = step(x, m, X)
                rows = pl.ds(pl.multiple_of(to * PX, PX), PX)
                send(
                    cot_ref.at[rows, :],
                    cotb.at[z, c, y, :, xf],
                    cz_s.at[k, m],
                    cz_r.at[k],
                    patch_0=step(z, k, Z),
                    mp=to,
                )
        if k:
            send(
                metab.at[z, c, y],
                metab.at[z, c, y],
                mz_s.at[k - 1],
                mz_r.at[k - 1],
                patch_0=step(z, k, Z),
            )
    for k in range(1, X):
        to = step(x, k, X)
        send(second_ref, second.at[:, xf], sec_s.at[k - 1], sec_r.at[k - 1], mp=to)

    def send_slot(j, carry):
        dz, dy, dc = j // (Y * 2), (j // 2) % Y, j % 2
        z1, y1, c1 = lax.rem(z + dz, Z), lax.rem(y + dy, Y), lax.rem(c + dc, 2)
        pltpu.make_async_remote_copy(
            src_ref=slots.at[(z1 * 2 + c1) * Y + y1],
            dst_ref=V.at[here],
            send_sem=w_s,
            recv_sem=w_r.at[z],
            device_id={"patch_0": z1, "patch_1": y1, "patch_2": c1, "mp": x},
            device_id_type=pl.DeviceIdType.MESH,
        ).start()
        return carry

    lax.fori_loop(1, NP, send_slot, 0)

    TR = 2 * PATCH
    T = R // TR

    def first_layer(i):
        rows = pl.ds(i * TR, TR)
        pre = dot(grid_ref[rows, :], first_ref[...])
        s = jax.nn.sigmoid(pre)
        hidden[rows, :] = (pre * s).astype(BF16)
        slope[rows, :] = s * (1.0 + pre * (1.0 - s))

    def second_layer(i):
        rows = pl.ds(i * TR, TR)
        msg[rows, :] = dot(hidden[rows, :], second[...]).astype(BF16)

    def over_y(k):
        at = step(z, (Z - k) % Z, Z)
        if k:
            arrive(cotb.at[at, c, y], cz_r.at[k])
        else:
            own_cot.wait()
            arrive(cotb.at[at, c, y, :, pl.ds(0, (X - 1) * F)], cz_r.at[k])
        for m in range(1, Y):
            block = cotb.at[at, c, y]
            send(block, block, cy_s.at[m - 1, k], cy_r.at[m - 1], patch_1=step(y, m, Y))

    loads["grid"].wait()
    loads["first"].wait()
    per = -(-Z // T)
    for i in range(T):
        first_layer(i)
        for k in near[i * per : (i + 1) * per]:
            over_y(k)
    for k in range(1, Z):
        arrive(metab.at[step(z, Z - k, Z), c, y], mz_r.at[k - 1])
    for m in range(1, Y):
        to = step(y, m, Y)
        send(metab.at[:, c, y], metab.at[:, c, y], my_s.at[m - 1], my_r.at[m - 1], patch_1=to)
    send(cotb.at[:, c, y], cotb.at[:, c, y], cc_s.at[0], cc_r.at[0], patch_2=oc)
    own_second.wait()
    for k in range(1, X):
        frm = step(x, X - k, X)
        arrive(second.at[:, pl.ds(pl.multiple_of(frm * F, F), F)], sec_r.at[k - 1])
    for i in range(T):
        second_layer(i)
    for m in range(1, Y):
        arrive(metab.at[:, c, step(y, Y - m, Y)], my_r.at[m - 1])
    send(metab.at[:, c], metab.at[:, c], mc_s.at[0], mc_r.at[0], patch_2=oc)
    for m in range(1, Y):
        frm = step(y, Y - m, Y)
        arrive(cotb.at[:, c, frm], cy_r.at[m - 1])
        send(cotb.at[:, c, frm], cotb.at[:, c, frm], cc_s.at[m], cc_r.at[m], patch_2=oc)
    arrive(metab.at[:, oc], mc_r.at[0])

    own_natural = (z * Y + y) * 2 + c
    PL = C * Y
    TP = PL * PX
    TC = Z * PX
    lanes = lax.broadcasted_iota(jnp.int32, (PL, PATCH), 1)

    def spread(i, carry):
        at = lax.rem(z + i, Z)
        meta = metab[at].reshape(PL, PATCH)
        patch_of = jnp.sum(jnp.where(lanes == own_natural, meta, 0.0), axis=1, keepdims=True)
        patch_rows = jnp.broadcast_to(
            jnp.broadcast_to(patch_of, (PL, PATCH))[:, None, :], (PL, PX, PATCH)
        ).reshape(TP, PATCH)
        blocks = V[pl.ds(pl.multiple_of(at * PL, PL), PL)].reshape(TP, PATCH).astype(F32)
        cols = pl.ds(pl.multiple_of(at * TP, TP), TP)
        blocks_t = blocks.T
        patch_cols = patch_rows.T
        for g in range(GPD):
            part = jnp.where(patch_rows == float(g), blocks, 0.0).astype(BF16)
            vbig[:, at, :, g * PATCH : (g + 1) * PATCH] = part.reshape(PL, PX, PATCH)
            vbig_t[g * PATCH : (g + 1) * PATCH, cols] = jnp.where(
                patch_cols == float(g), blocks_t, 0.0
            ).astype(BF16)
        return carry

    own_slot.wait()
    for k in near:
        frm = step(z, (Z - k) % Z, Z)
        arrive(V.at[pl.ds(0, PL if k else PL - 1)], w_r.at[frm])
        spread((Z - k) % Z, 0)


    def contribution(core, yy):
        return dot(vbig[core * Y + yy].reshape(TC, R), msg[...])

    for k in range(1, Y + 1):
        yy = step(y, k % Y, Y)
        c_send[yy] = contribution(oc, yy).astype(BF16).reshape(Z, PX, D)
        send(c_send.at[yy], c_recv.at[yy], fc_s.at[k - 1], fc_r.at[k - 1], patch_2=oc)
    for k in range(1, Y + 1):
        yy = step(y, k % Y, Y)
        part = contribution(c, yy)
        arrive(c_recv.at[yy], fc_r.at[k - 1])
        part = part + c_recv[yy].astype(F32).reshape(TC, D)
        if k < Y:
            y_send[k - 1] = part.astype(BF16).reshape(Z, PX, D)
            send(y_send.at[k - 1], y_recv.at[k - 1], fy_s.at[k - 1], fy_r.at[k - 1], patch_1=yy)
        else:
            y_own[...] = part.reshape(Z, PX, D)

    for m in range(Y):
        arrive(cotb.at[:, oc, step(y, Y - m, Y)], cc_r.at[m])

    def message_gradient(i, carry):
        rows = pl.ds(pl.multiple_of(i * TR, TR), TR)
        gm[rows, :] = dot(vbig_t[rows, :], cotb[...].reshape(NP * PX, D)).astype(BF16)
        return carry

    lax.fori_loop(0, R // TR, message_gradient, 0)

    def halves(which, left_ref, right_ref):
        for core in (oc, c):
            cols = pl.ds(pl.multiple_of(core * HC, HC), HC)
            part = dot(left_ref[:, cols], right_ref[...], ((0,), (0,))) * scaling
            for q in range(X):
                piece = part[:, q * F : (q + 1) * F]
                if core is oc:
                    gc_send[which, q] = piece
                else:
                    g_own[which, q] = piece
            if core is oc:
                send(
                    gc_send.at[which],
                    gc_recv.at[which],
                    gc_s.at[which],
                    gc_r.at[which],
                    patch_2=oc,
                )

    def over_mp(which):
        arrive(gc_recv.at[which], gc_r.at[which])
        for k in range(1, X):
            to = step(x, k, X)
            gx_send[which, k - 1] = (g_own[which, to] + gc_recv[which, to]).astype(BF16)
            send(
                gx_send.at[which, k - 1],
                gx_recv.at[which, k - 1],
                gx_s.at[which, k - 1],
                gx_r.at[which, k - 1],
                mp=to,
            )
        g_own[which, x] = g_own[which, x] + gc_recv[which, x]

    halves(0, hidden, gm)

    def pre_gradient(i, carry):
        rows = pl.ds(pl.multiple_of(i * TR, TR), TR)
        back = dot(gm[rows, :], second[...], ((1,), (1,)))
        gpre[rows, :] = (back * slope[rows, :]).astype(BF16)
        return carry

    lax.fori_loop(0, R // TR, pre_gradient, 0)
    over_mp(0)

    halves(1, grid_ref, gpre)

    over_mp(1)

    ZR = HC // Z
    for which in range(2):
        total = g_own[which, x]
        for k in range(1, X):
            arrive(gx_recv.at[which, k - 1], gx_r.at[which, k - 1])
            total = total + gx_recv[which, k - 1].astype(F32)
        g_own[which, x] = total
        gz_send[:, which] = total.reshape(Z, ZR, F).astype(BF16)
    for k in range(1, Z):
        to = step(z, k, Z)
        send(gz_send.at[to], gz_recv.at[k - 1], gz_s.at[k - 1], gz_r.at[k - 1], patch_0=to)

    for k in range(1, Y):
        arrive(y_recv.at[k - 1], fy_r.at[k - 1])
    total = y_own[...]
    for k in range(1, Y):
        total = total + y_recv[k - 1].astype(F32)
    y_own[...] = total
    z_send[...] = total.astype(BF16)
    for k in range(1, Z):
        to = step(z, k, Z)
        send(z_send.at[to], z_recv.at[k - 1], fz_s.at[k - 1], fz_r.at[k - 1], patch_0=to)

    total = g_own[:, x, pl.ds(pl.multiple_of(z * ZR, ZR), ZR)]
    for k in range(1, Z):
        arrive(gz_recv.at[k - 1], gz_r.at[k - 1])
        total = total + gz_recv[k - 1].astype(F32)
    gy[y] = total
    for k in range(1, Y):
        to = step(y, k, Y)
        send(gy.at[y], gy.at[y], gy_s.at[k - 1], gy_r.at[k - 1], patch_1=to)

    for k in range(1, Y):
        arrive(gy.at[step(y, Y - k, Y)], gy_r.at[k - 1])
    total = gy[0]
    for yy in range(1, Y):
        total = total + gy[yy]
    own[...] = total.astype(BF16)
    for k in range(1, Z):
        to = step(z, k, Z)
        send(own, fin.at[c, z], az_s.at[k - 1], az_r.at[k - 1], patch_0=to)
    fin[c, z] = own[...]

    total = y_own[z]
    for k in range(1, Z):
        arrive(z_recv.at[k - 1], fz_r.at[k - 1])
        total = total + z_recv[k - 1].astype(F32)
    for q in range(X):
        x_send[q] = total[:, q * F : (q + 1) * F]
    own_sum = pltpu.make_async_copy(x_send.at[x], x_recv.at[x], loc.at[0])
    own_sum.start()
    for k in range(1, X):
        to = step(x, k, X)
        send(x_send.at[to], x_recv.at[x], fx_s.at[k - 1], fx_r.at[k - 1], mp=to)

    for k in range(1, Z):
        arrive(fin.at[c, step(z, Z - k, Z)], az_r.at[k - 1])
    send(fin.at[c], fin.at[c], ac_s.at[0], ac_r.at[0], patch_2=oc)
    own_sum.wait()
    for k in range(1, X):
        arrive(x_recv.at[step(x, X - k, X)], fx_r.at[k - 1])
    loads["latent"].wait()
    mesh_out[...] = (latent_ref[...].astype(F32) + x_recv[...].reshape(PATCH, F)).astype(BF16)
    arrive(fin.at[oc], ac_r.at[0])
    pltpu.make_async_remote_copy(
        src_ref=all_but_one(slots, NP),
        dst_ref=all_but_one(V, NP),
        send_sem=w_s,
        recv_sem=w_r.at[0],
        device_id={"patch_0": z, "patch_1": y, "patch_2": oc, "mp": x},
        device_id_type=pl.DeviceIdType.MESH,
    ).wait_send()
    for src, dst, ss, rs in sent:
        pltpu.make_async_copy(src, src, ss).wait()


def hand_out(mesh_sum, sums, mesh_out, first_out, second_out):
    mesh_out[...] = mesh_sum[...]
    second_out[...] = sums[:, :, 0].reshape(second_out.shape).astype(F32)
    first_out[...] = sums[:, :, 1].reshape(first_out.shape).astype(F32)


def all_but_one(ref, n):
    return ref.at[pl.ds(0, n - 1)]


def per_device(
    grid_latent,
    mesh_latent,
    edge_weight,
    block_source,
    block_live,
    mlp_first,
    mlp_second,
    mesh_cotangent,
):
    Z, Y, C = (lax.axis_size(a) for a in PATCH_AXES)
    X = lax.axis_size("mp")
    NP = Z * Y * C
    R, D = grid_latent.shape
    H = mlp_first.shape[1]
    F = mlp_second.shape[1]
    PX = PATCH // X
    GPD = R // PATCH
    HC = D // 2
    ZR = HC // Z
    scaling = 1.0 / math.sqrt(R * NP)

    vm = pltpu.VMEM
    dma = pltpu.SemaphoreType.DMA
    scratch = [
        vm((1, PATCH), F32),
        vm(grid_latent.shape, BF16),
        vm(mesh_latent.shape, BF16),
        vm(edge_weight.shape, BF16),
        vm(mlp_first.shape, BF16),
        vm(mlp_second.shape, BF16),
        vm(mesh_cotangent.shape, BF16),
        vm((NP, PX, PATCH), BF16),
        vm((NP, PX, PATCH), BF16),
        vm((Z, C, Y, PX, D), BF16),
        vm((Z, C, Y, 1, PATCH), F32),
        vm((H, D), BF16),
        vm((R, H), F32),
        vm((R, H), BF16),
        vm((R, D), BF16),
        vm((C * Y, Z, PX, R), BF16),
        vm((R, NP * PX), BF16),
        vm((Y, Z, PX, D), BF16),
        vm((Y, Z, PX, D), BF16),
        vm((Y - 1, Z, PX, D), BF16),
        vm((Y - 1, Z, PX, D), BF16),
        vm((Z, PX, D), F32),
        vm((Z, PX, D), BF16),
        vm((Z - 1, PX, D), BF16),
        vm((X, PX, F), F32),
        vm((X, PX, F), F32),
        vm((R, D), BF16),
        vm((R, H), BF16),
        vm((2, X, HC, F), F32),
        vm((2, X, HC, F), F32),
        vm((2, X, HC, F), F32),
        vm((2, X - 1, HC, F), BF16),
        vm((2, X - 1, HC, F), BF16),
        vm((Z, 2, ZR, F), BF16),
        vm((Z - 1, 2, ZR, F), BF16),
        vm((Y, 2, ZR, F), F32),
        vm((2, ZR, F), BF16),
        dma,
        dma((Z,)),
        dma((X - 1,)),
        dma((X - 1,)),
        dma((X - 1,)),
        dma((X - 1,)),
        dma((Z, X)),
        dma((Z,)),
        dma((Y - 1, Z)),
        dma((Y - 1,)),
        dma((4,)),
        dma((4,)),
        dma((Z - 1,)),
        dma((Z - 1,)),
        dma((Y - 1,)),
        dma((Y - 1,)),
        dma((1,)),
        dma((1,)),
        dma((Y,)),
        dma((Y,)),
        dma((Y - 1,)),
        dma((Y - 1,)),
        dma((Z - 1,)),
        dma((Z - 1,)),
        dma((X - 1,)),
        dma((X - 1,)),
        dma((2,)),
        dma((2,)),
        dma((2, X - 1)),
        dma((2, X - 1)),
        dma((Z - 1,)),
        dma((Z - 1,)),
        dma((Y - 1,)),
        dma((Y - 1,)),
        dma((Z - 1,)),
        dma((Z - 1,)),
        dma((1,)),
        dma((1,)),
        dma((4,)),
        dma((6,)),
    ]
    in_vmem = pl.BlockSpec(memory_space=pltpu.VMEM)
    mesh_sum, sums = pl.pallas_call(
        functools.partial(kernel, (Z, Y, C, X), scaling),
        out_shape=(
            jax.ShapeDtypeStruct((PATCH, F), BF16),
            jax.ShapeDtypeStruct((C, Z, 2, ZR, F), BF16),
        ),
        in_specs=[pl.BlockSpec(memory_space=pltpu.SMEM)] * 2
        + [pl.BlockSpec(memory_space=pl.ANY)] * 6,
        out_specs=(in_vmem, in_vmem),
        scratch_shapes=scratch,
        compiler_params=pltpu.CompilerParams(
            collective_id=0, has_side_effects=True, vmem_limit_bytes=62 * 1024 * 1024
        ),
    )(
        block_source,
        block_live,
        grid_latent,
        mesh_latent,
        edge_weight,
        mlp_first,
        mlp_second,
        mesh_cotangent,
    )
    return pl.pallas_call(
        hand_out,
        out_shape=(
            jax.ShapeDtypeStruct((PATCH, F), BF16),
            jax.ShapeDtypeStruct((D, F), F32),
            jax.ShapeDtypeStruct((H, F), F32),
        ),
        in_specs=[in_vmem] * 2,
        out_specs=(in_vmem, in_vmem, in_vmem),
    )(mesh_sum, sums)


def torus_of(mesh):
    return Mesh(mesh.devices.reshape(8, 4, 2, mesh.shape["mp"]), AXES)


def solution(mesh):
    torus = torus_of(mesh)
    in_specs = (
        P(PATCH_AXES, None),
        P(PATCH_AXES, "mp"),
        P(PATCH_AXES, None, None),
        P(PATCH_AXES),
        P(PATCH_AXES),
        P(),
        P(None, "mp"),
        P(PATCH_AXES, "mp"),
    )
    out_specs = (P(PATCH_AXES, "mp"), P(None, "mp"), P(None, "mp"))
    return jax.shard_map(
        per_device, mesh=torus, in_specs=in_specs, out_specs=out_specs, check_vma=False
    )
```

```python
import functools
import math

import jax
import jax.numpy as jnp
from jax import lax
from jax.experimental import pallas as pl
from jax.experimental.pallas import tpu as pltpu
from jax.sharding import Mesh
from jax.sharding import PartitionSpec as P

PATCH = 128
PATCH_AXES = ("patch_0", "patch_1", "patch_2")
AXES = PATCH_AXES + ("mp",)
F32 = jnp.float32
BF16 = jnp.bfloat16


def dot(a, b, dims=((1,), (0,))):
    return lax.dot_general(a, b, (dims, ((), ())), preferred_element_type=F32)


def kernel(
    sizes,
    scaling,
    source_ref,
    live_ref,
    grid_in,
    latent_in,
    w_in,
    first_in,
    second_in,
    cot_in,
    mesh_out,
    fin,
    meta_ref,
    grid_ref,
    latent_ref,
    w_ref,
    first_ref,
    second_ref,
    cot_ref,
    slots,
    V,
    cotb,
    metab,
    second,
    slope,
    hidden,
    msg,
    vbig,
    vbig_t,
    c_own,
    c_sum,
    c_send,
    c_recv,
    y_send,
    y_recv,
    y_own,
    z_send,
    z_recv,
    x_send,
    x_recv,
    gm_sum,
    gm,
    gpre,
    gc_send,
    gc_recv,
    g_own,
    gx_send,
    gx_recv,
    gz_send,
    gz_recv,
    gy,
    own,
    w_s,
    w_r,
    sec_s,
    sec_r,
    cx_s,
    cx_r,
    cz_s,
    cz_r,
    cy_s,
    cy_r,
    cc_s,
    cc_r,
    mz_s,
    mz_r,
    my_s,
    my_r,
    mc_s,
    mc_r,
    fc_s,
    fc_r,
    fy_s,
    fy_r,
    fz_s,
    fz_r,
    fx_s,
    fx_r,
    gc_s,
    gc_r,
    gx_s,
    gx_r,
    gz_s,
    gz_r,
    gy_s,
    gy_r,
    az_s,
    az_r,
    ac_s,
    ac_r,
    loc,
    load_s,
):
    Z, Y, C, X = sizes
    NP = Z * Y * C
    R, D = grid_in.shape
    H = first_in.shape[1]
    F = second_in.shape[1]
    PX = PATCH // X
    GPD = R // PATCH
    HC = D // 2
    z, y, c, x = (lax.axis_index(a) for a in AXES)
    oc = 1 - c
    sent = []

    def send(src, dst, ss, rs, **where):
        place = {"patch_0": z, "patch_1": y, "patch_2": c, "mp": x}
        place.update(where)
        copy = pltpu.make_async_remote_copy(
            src_ref=src,
            dst_ref=dst,
            send_sem=ss,
            recv_sem=rs,
            device_id=place,
            device_id_type=pl.DeviceIdType.MESH,
        )
        copy.start()
        sent.append((src, dst, ss, rs))

    def arrive(dst, rs):
        pltpu.make_async_copy(dst, dst, rs).wait()

    def step(i, k, n):
        return lax.rem(i + k, n)

    xf = pl.ds(pl.multiple_of(x * F, F), F)
    xp = pl.ds(pl.multiple_of(x * PX, PX), PX)

    loads = {}
    for i, (name, src, dst) in enumerate(
        (
            ("cot", cot_in, cot_ref),
            ("w", w_in, w_ref),
            ("second", second_in, second_ref),
            ("grid", grid_in, grid_ref),
            ("first", first_in, first_ref),
            ("latent", latent_in, latent_ref),
        )
    ):
        loads[name] = pltpu.make_async_copy(src, dst, load_s.at[i])
        loads[name].start()

    barrier = pltpu.get_barrier_semaphore()

    def greet(j, carry):
        dz, dy, dc = j // (Y * 2), (j // 2) % Y, j % 2
        pl.semaphore_signal(
            barrier,
            inc=1,
            device_id={
                "patch_0": lax.rem(z + dz, Z),
                "patch_1": lax.rem(y + dy, Y),
                "patch_2": lax.rem(c + dc, 2),
                "mp": x,
            },
            device_id_type=pl.DeviceIdType.MESH,
        )
        return carry

    def greet_mp(j, carry):
        pl.semaphore_signal(
            barrier,
            inc=1,
            device_id={
                "patch_0": lax.rem(z + j % Z, Z),
                "patch_1": y,
                "patch_2": c,
                "mp": lax.rem(x + j // Z, X),
            },
            device_id_type=pl.DeviceIdType.MESH,
        )
        return carry

    lax.fori_loop(1, NP, greet, 0)
    lax.fori_loop(Z, X * Z, greet_mp, 0)

    n_slots = w_in.shape[0]

    def feeder(j):
        return jnp.where(live_ref[j] == 1, lax.div(source_ref[j], GPD), -1)

    lane = lax.broadcasted_iota(jnp.int32, (1, PATCH), 1)
    meta = jnp.zeros((1, PATCH), F32)
    for j in range(n_slots):
        inside = lax.rem(source_ref[j], GPD).astype(F32)
        meta = jnp.where(lane == feeder(j), inside, meta)
    meta_ref[...] = meta
    loads["w"].wait()

    def pack(i, carry):
        z1, c1, y1 = i // (2 * Y), (i // Y) % 2, i % Y
        natural = (z1 * Y + y1) * 2 + c1
        slot, live = jnp.int32(0), jnp.int32(0)
        for j in range(n_slots):
            hit = feeder(j) == natural
            slot = jnp.where(hit, j, slot)
            live = jnp.where(hit, 1, live)
        block = w_ref[slot, xp, :]
        slots[i] = (block.astype(F32) * live.astype(F32)).astype(BF16)
        return carry

    lax.fori_loop(0, NP, pack, 0)
    loads["cot"].wait()
    loads["second"].wait()
    own_cot = pltpu.make_async_copy(cot_ref.at[xp, :], cotb.at[z, c, y, :, xf], loc.at[0])
    own_cot.start()
    own_second = pltpu.make_async_copy(second_ref, second.at[:, xf], loc.at[1])
    own_second.start()
    own_meta = pltpu.make_async_copy(meta_ref, metab.at[z, c, y], loc.at[2])
    own_meta.start()
    here = (z * 2 + c) * Y + y
    own_slot = pltpu.make_async_copy(slots.at[here], V.at[here], loc.at[3])
    own_slot.start()
    pl.semaphore_wait(barrier, NP - 1 + (X - 1) * Z)

    own_meta.wait()
    near = [0]
    for t in range(1, Z // 2 + 1):
        near += [t, Z - t] if 2 * t < Z else [t]
    for k in near:
        for m in range(X):
            if k or m:
                to = step(x, m, X)
                rows = pl.ds(pl.multiple_of(to * PX, PX), PX)
                send(
                    cot_ref.at[rows, :],
                    cotb.at[z, c, y, :, xf],
                    cz_s.at[k, m],
                    cz_r.at[k],
                    patch_0=step(z, k, Z),
                    mp=to,
                )
        if k:
            send(
                metab.at[z, c, y],
                metab.at[z, c, y],
                mz_s.at[k - 1],
                mz_r.at[k - 1],
                patch_0=step(z, k, Z),
            )
    for k in range(1, X):
        to = step(x, k, X)
        send(second_ref, second.at[:, xf], sec_s.at[k - 1], sec_r.at[k - 1], mp=to)

    def send_slot(j, carry):
        dz, dy, dc = j // (Y * 2), (j // 2) % Y, j % 2
        z1, y1, c1 = lax.rem(z + dz, Z), lax.rem(y + dy, Y), lax.rem(c + dc, 2)
        pltpu.make_async_remote_copy(
            src_ref=slots.at[(z1 * 2 + c1) * Y + y1],
            dst_ref=V.at[here],
            send_sem=w_s,
            recv_sem=w_r.at[z],
            device_id={"patch_0": z1, "patch_1": y1, "patch_2": c1, "mp": x},
            device_id_type=pl.DeviceIdType.MESH,
        ).start()
        return carry

    for dz in near:
        lax.fori_loop(max(1, dz * Y * 2), (dz + 1) * Y * 2, send_slot, 0)

    TR = 2 * PATCH
    T = R // TR

    def first_layer(i):
        rows = pl.ds(i * TR, TR)
        pre = dot(grid_ref[rows, :], first_ref[...])
        s = jax.nn.sigmoid(pre)
        hidden[rows, :] = (pre * s).astype(BF16)
        slope[rows, :] = s * (1.0 + pre * (1.0 - s))

    def second_layer(i):
        rows = pl.ds(i * TR, TR)
        msg[rows, :] = dot(hidden[rows, :], second[...]).astype(BF16)

    def over_y(k):
        at = step(z, (Z - k) % Z, Z)
        if k:
            arrive(cotb.at[at, c, y], cz_r.at[k])
        else:
            own_cot.wait()
            arrive(cotb.at[at, c, y, :, pl.ds(0, (X - 1) * F)], cz_r.at[k])
        for m in range(1, Y):
            block = cotb.at[at, c, y]
            send(block, block, cy_s.at[m - 1, k], cy_r.at[m - 1, k], patch_1=step(y, m, Y))

    loads["grid"].wait()
    loads["first"].wait()
    per = -(-Z // T)
    for i in range(T):
        first_layer(i)
        for k in near[i * per : (i + 1) * per]:
            over_y(k)
    for k in range(1, Z):
        arrive(metab.at[step(z, Z - k, Z), c, y], mz_r.at[k - 1])
    for m in range(1, Y):
        to = step(y, m, Y)
        send(metab.at[:, c, y], metab.at[:, c, y], my_s.at[m - 1], my_r.at[m - 1], patch_1=to)
    own_second.wait()
    for k in range(1, X):
        frm = step(x, X - k, X)
        arrive(second.at[:, pl.ds(pl.multiple_of(frm * F, F), F)], sec_r.at[k - 1])
    for i in range(T):
        second_layer(i)
    for m in range(1, Y):
        arrive(metab.at[:, c, step(y, Y - m, Y)], my_r.at[m - 1])
    send(metab.at[:, c], metab.at[:, c], mc_s.at[0], mc_r.at[0], patch_2=oc)
    arrive(metab.at[:, oc], mc_r.at[0])

    own_natural = (z * Y + y) * 2 + c
    PL = C * Y
    TP = PL * PX
    lanes = lax.broadcasted_iota(jnp.int32, (PL, PATCH), 1)

    def plane(k):
        return step(z, (Z - k) % Z, Z)

    def spread(at, slot):
        meta = metab[at].reshape(PL, PATCH)
        patch_of = jnp.sum(jnp.where(lanes == own_natural, meta, 0.0), axis=1, keepdims=True)
        patch_rows = jnp.broadcast_to(
            jnp.broadcast_to(patch_of, (PL, PATCH))[:, None, :], (PL, PX, PATCH)
        ).reshape(TP, PATCH)
        blocks = V[pl.ds(pl.multiple_of(at * PL, PL), PL)].reshape(TP, PATCH).astype(F32)
        blocks_t = blocks.T
        patch_cols = patch_rows.T
        for g in range(GPD):
            vbig[:, g * PATCH : (g + 1) * PATCH] = jnp.where(
                patch_rows == float(g), blocks, 0.0
            ).astype(BF16)
            vbig_t[slot, g * PATCH : (g + 1) * PATCH, :] = jnp.where(
                patch_cols == float(g), blocks_t, 0.0
            ).astype(BF16)

    def contribute(i, k):
        at, slot = plane(k), i % 2
        arrive(V.at[pl.ds(0, PL if k else PL - 1)], w_r.at[at])
        spread(at, slot)
        c_own[slot] = dot(vbig[...], msg[...]).reshape(C, Y, PX, D)
        c_send[at] = c_own[slot, oc].astype(BF16)
        send(c_send.at[at], c_recv.at[at], fc_s.at[k], fc_r.at[k], patch_2=oc)
        for m in range(1, Y):
            arrive(cotb.at[at, c, step(y, Y - m, Y)], cy_r.at[m - 1, k])
        send(cotb.at[at, c], cotb.at[at, c], cc_s.at[k], cc_r.at[k], patch_2=oc)

    def collect(i, k):
        at, slot = plane(k), i % 2
        arrive(c_recv.at[at], fc_r.at[k])
        c_sum[...] = c_own[slot, c] + c_recv[at].astype(F32)
        y_own[at] = c_sum[y]
        for m in range(1, Y):
            to = step(y, m, Y)
            y_send[m - 1, at] = c_sum[to].astype(BF16)
            send(
                y_send.at[m - 1, at],
                y_recv.at[m - 1, at],
                fy_s.at[m - 1, k],
                fy_r.at[m - 1, k],
                patch_1=to,
            )
        arrive(cotb.at[at, oc], cc_r.at[k])
        for t in range(T):
            rows = slice(t * TR, (t + 1) * TR)
            part = dot(vbig_t[slot, rows, :], cotb[at].reshape(TP, D))
            if i == 0:
                gm_sum[rows, :] = part
            elif i < Z - 1:
                gm_sum[rows, :] += part
            else:
                gm[rows, :] = (gm_sum[rows, :] + part).astype(BF16)

    own_slot.wait()
    for i, k in enumerate(near):
        contribute(i, k)
        if i:
            collect(i - 1, near[i - 1])
    collect(Z - 1, near[-1])

    def halves(which, left_ref, right_ref):
        for core in (oc, c):
            cols = pl.ds(pl.multiple_of(core * HC, HC), HC)
            part = dot(left_ref[:, cols], right_ref[...], ((0,), (0,))) * scaling
            for q in range(X):
                piece = part[:, q * F : (q + 1) * F]
                if core is oc:
                    gc_send[which, q] = piece
                else:
                    g_own[which, q] = piece
            if core is oc:
                send(
                    gc_send.at[which],
                    gc_recv.at[which],
                    gc_s.at[which],
                    gc_r.at[which],
                    patch_2=oc,
                )

    def over_mp(which):
        arrive(gc_recv.at[which], gc_r.at[which])
        for k in range(1, X):
            to = step(x, k, X)
            gx_send[which, k - 1] = (g_own[which, to] + gc_recv[which, to]).astype(BF16)
            send(
                gx_send.at[which, k - 1],
                gx_recv.at[which, k - 1],
                gx_s.at[which, k - 1],
                gx_r.at[which, k - 1],
                mp=to,
            )
        g_own[which, x] = g_own[which, x] + gc_recv[which, x]

    halves(0, hidden, gm)

    def pre_gradient(i, carry):
        rows = pl.ds(pl.multiple_of(i * TR, TR), TR)
        back = dot(gm[rows, :], second[...], ((1,), (1,)))
        gpre[rows, :] = (back * slope[rows, :]).astype(BF16)
        return carry

    lax.fori_loop(0, R // TR, pre_gradient, 0)
    over_mp(0)

    halves(1, grid_ref, gpre)

    over_mp(1)

    for k in near:
        at = plane(k)
        total = y_own[at]
        for m in range(1, Y):
            arrive(y_recv.at[m - 1, at], fy_r.at[m - 1, k])
            total = total + y_recv[m - 1, at].astype(F32)
        if k:
            z_send[at] = total.astype(BF16)
            send(z_send.at[at], z_recv.at[k - 1], fz_s.at[k - 1], fz_r.at[k - 1], patch_0=at)
        else:
            y_own[at] = total

    ZR = HC // Z
    for which in range(2):
        total = g_own[which, x]
        for k in range(1, X):
            arrive(gx_recv.at[which, k - 1], gx_r.at[which, k - 1])
            total = total + gx_recv[which, k - 1].astype(F32)
        g_own[which, x] = total
        gz_send[:, which] = total.reshape(Z, ZR, F).astype(BF16)
    for k in range(1, Z):
        to = step(z, k, Z)
        send(gz_send.at[to], gz_recv.at[k - 1], gz_s.at[k - 1], gz_r.at[k - 1], patch_0=to)

    total = g_own[:, x, pl.ds(pl.multiple_of(z * ZR, ZR), ZR)]
    for k in range(1, Z):
        arrive(gz_recv.at[k - 1], gz_r.at[k - 1])
        total = total + gz_recv[k - 1].astype(F32)
    gy[y] = total
    for k in range(1, Y):
        to = step(y, k, Y)
        send(gy.at[y], gy.at[y], gy_s.at[k - 1], gy_r.at[k - 1], patch_1=to)

    for k in range(1, Y):
        arrive(gy.at[step(y, Y - k, Y)], gy_r.at[k - 1])
    total = gy[0]
    for yy in range(1, Y):
        total = total + gy[yy]
    own[...] = total.astype(BF16)
    for k in range(1, Z):
        to = step(z, k, Z)
        send(own, fin.at[c, z], az_s.at[k - 1], az_r.at[k - 1], patch_0=to)
    fin[c, z] = own[...]

    total = y_own[z]
    for k in range(1, Z):
        arrive(z_recv.at[k - 1], fz_r.at[k - 1])
        total = total + z_recv[k - 1].astype(F32)
    for q in range(X):
        x_send[q] = total[:, q * F : (q + 1) * F]
    own_sum = pltpu.make_async_copy(x_send.at[x], x_recv.at[x], loc.at[0])
    own_sum.start()
    for k in range(1, X):
        to = step(x, k, X)
        send(x_send.at[to], x_recv.at[x], fx_s.at[k - 1], fx_r.at[k - 1], mp=to)

    for k in range(1, Z):
        arrive(fin.at[c, step(z, Z - k, Z)], az_r.at[k - 1])
    send(fin.at[c], fin.at[c], ac_s.at[0], ac_r.at[0], patch_2=oc)
    own_sum.wait()
    for k in range(1, X):
        arrive(x_recv.at[step(x, X - k, X)], fx_r.at[k - 1])
    loads["latent"].wait()
    mesh_out[...] = (latent_ref[...].astype(F32) + x_recv[...].reshape(PATCH, F)).astype(BF16)
    arrive(fin.at[oc], ac_r.at[0])
    pltpu.make_async_remote_copy(
        src_ref=all_but_one(slots, NP),
        dst_ref=all_but_one(V, NP),
        send_sem=w_s,
        recv_sem=w_r.at[0],
        device_id={"patch_0": z, "patch_1": y, "patch_2": oc, "mp": x},
        device_id_type=pl.DeviceIdType.MESH,
    ).wait_send()
    for src, dst, ss, rs in sent:
        pltpu.make_async_copy(src, src, ss).wait()


def hand_out(mesh_sum, sums, mesh_out, first_out, second_out):
    mesh_out[...] = mesh_sum[...]
    second_out[...] = sums[:, :, 0].reshape(second_out.shape).astype(F32)
    first_out[...] = sums[:, :, 1].reshape(first_out.shape).astype(F32)


def all_but_one(ref, n):
    return ref.at[pl.ds(0, n - 1)]


def per_device(
    grid_latent,
    mesh_latent,
    edge_weight,
    block_source,
    block_live,
    mlp_first,
    mlp_second,
    mesh_cotangent,
):
    Z, Y, C = (lax.axis_size(a) for a in PATCH_AXES)
    X = lax.axis_size("mp")
    NP = Z * Y * C
    R, D = grid_latent.shape
    H = mlp_first.shape[1]
    F = mlp_second.shape[1]
    PX = PATCH // X
    GPD = R // PATCH
    HC = D // 2
    ZR = HC // Z
    scaling = 1.0 / math.sqrt(R * NP)

    vm = pltpu.VMEM
    dma = pltpu.SemaphoreType.DMA
    scratch = [
        vm((1, PATCH), F32),
        vm(grid_latent.shape, BF16),
        vm(mesh_latent.shape, BF16),
        vm(edge_weight.shape, BF16),
        vm(mlp_first.shape, BF16),
        vm(mlp_second.shape, BF16),
        vm(mesh_cotangent.shape, BF16),
        vm((NP, PX, PATCH), BF16),
        vm((NP, PX, PATCH), BF16),
        vm((Z, C, Y, PX, D), BF16),
        vm((Z, C, Y, 1, PATCH), F32),
        vm((H, D), BF16),
        vm((R, H), F32),
        vm((R, H), BF16),
        vm((R, D), BF16),
        vm((C * Y * PX, R), BF16),
        vm((2, R, C * Y * PX), BF16),
        vm((2, C, Y, PX, D), F32),
        vm((Y, PX, D), F32),
        vm((Z, Y, PX, D), BF16),
        vm((Z, Y, PX, D), BF16),
        vm((Y - 1, Z, PX, D), BF16),
        vm((Y - 1, Z, PX, D), BF16),
        vm((Z, PX, D), F32),
        vm((Z, PX, D), BF16),
        vm((Z - 1, PX, D), BF16),
        vm((X, PX, F), F32),
        vm((X, PX, F), F32),
        vm((R, D), F32),
        vm((R, D), BF16),
        vm((R, H), BF16),
        vm((2, X, HC, F), F32),
        vm((2, X, HC, F), F32),
        vm((2, X, HC, F), F32),
        vm((2, X - 1, HC, F), BF16),
        vm((2, X - 1, HC, F), BF16),
        vm((Z, 2, ZR, F), BF16),
        vm((Z - 1, 2, ZR, F), BF16),
        vm((Y, 2, ZR, F), F32),
        vm((2, ZR, F), BF16),
        dma,
        dma((Z,)),
        dma((X - 1,)),
        dma((X - 1,)),
        dma((X - 1,)),
        dma((X - 1,)),
        dma((Z, X)),
        dma((Z,)),
        dma((Y - 1, Z)),
        dma((Y - 1, Z)),
        dma((Z,)),
        dma((Z,)),
        dma((Z - 1,)),
        dma((Z - 1,)),
        dma((Y - 1,)),
        dma((Y - 1,)),
        dma((1,)),
        dma((1,)),
        dma((Z,)),
        dma((Z,)),
        dma((Y - 1, Z)),
        dma((Y - 1, Z)),
        dma((Z - 1,)),
        dma((Z - 1,)),
        dma((X - 1,)),
        dma((X - 1,)),
        dma((2,)),
        dma((2,)),
        dma((2, X - 1)),
        dma((2, X - 1)),
        dma((Z - 1,)),
        dma((Z - 1,)),
        dma((Y - 1,)),
        dma((Y - 1,)),
        dma((Z - 1,)),
        dma((Z - 1,)),
        dma((1,)),
        dma((1,)),
        dma((4,)),
        dma((6,)),
    ]
    in_vmem = pl.BlockSpec(memory_space=pltpu.VMEM)
    mesh_sum, sums = pl.pallas_call(
        functools.partial(kernel, (Z, Y, C, X), scaling),
        out_shape=(
            jax.ShapeDtypeStruct((PATCH, F), BF16),
            jax.ShapeDtypeStruct((C, Z, 2, ZR, F), BF16),
        ),
        in_specs=[pl.BlockSpec(memory_space=pltpu.SMEM)] * 2
        + [pl.BlockSpec(memory_space=pl.ANY)] * 6,
        out_specs=(in_vmem, in_vmem),
        scratch_shapes=scratch,
        compiler_params=pltpu.CompilerParams(
            collective_id=0, has_side_effects=True, vmem_limit_bytes=62 * 1024 * 1024
        ),
    )(
        block_source,
        block_live,
        grid_latent,
        mesh_latent,
        edge_weight,
        mlp_first,
        mlp_second,
        mesh_cotangent,
    )
    return pl.pallas_call(
        hand_out,
        out_shape=(
            jax.ShapeDtypeStruct((PATCH, F), BF16),
            jax.ShapeDtypeStruct((D, F), F32),
            jax.ShapeDtypeStruct((H, F), F32),
        ),
        in_specs=[in_vmem] * 2,
        out_specs=(in_vmem, in_vmem, in_vmem),
    )(mesh_sum, sums)


def torus_of(mesh):
    return Mesh(mesh.devices.reshape(8, 4, 2, mesh.shape["mp"]), AXES)


def solution(mesh):
    torus = torus_of(mesh)
    in_specs = (
        P(PATCH_AXES, None),
        P(PATCH_AXES, "mp"),
        P(PATCH_AXES, None, None),
        P(PATCH_AXES),
        P(PATCH_AXES),
        P(),
        P(None, "mp"),
        P(PATCH_AXES, "mp"),
    )
    out_specs = (P(PATCH_AXES, "mp"), P(None, "mp"), P(None, "mp"))
    return jax.shard_map(
        per_device, mesh=torus, in_specs=in_specs, out_specs=out_specs, check_vma=False
    )
```

```python
import functools
import math

import jax
import jax.numpy as jnp
from jax import lax
from jax.experimental import pallas as pl
from jax.experimental.pallas import tpu as pltpu
from jax.sharding import Mesh
from jax.sharding import PartitionSpec as P

PATCH = 128
PATCH_AXES = ("patch_0", "patch_1", "patch_2")
AXES = PATCH_AXES + ("mp",)
F32 = jnp.float32
BF16 = jnp.bfloat16


def dot(a, b, dims=((1,), (0,))):
    return lax.dot_general(a, b, (dims, ((), ())), preferred_element_type=F32)


def kernel(
    sizes,
    scaling,
    source_ref,
    live_ref,
    grid_in,
    latent_in,
    w_in,
    first_in,
    second_in,
    cot_in,
    mesh_out,
    fin,
    meta_ref,
    grid_ref,
    latent_ref,
    w_ref,
    first_ref,
    second_ref,
    cot_ref,
    slots,
    V,
    cotb,
    metab,
    second,
    slope,
    hidden,
    msg,
    vbig,
    vbig_t,
    c_own,
    c_sum,
    c_send,
    c_recv,
    y_send,
    y_recv,
    y_own,
    z_send,
    z_recv,
    x_send,
    x_recv,
    gm_sum,
    gm,
    gpre,
    gc_send,
    gc_recv,
    g_own,
    gx_send,
    gx_recv,
    gz_send,
    gz_recv,
    gy,
    own,
    w_s,
    w_r,
    sec_s,
    sec_r,
    cx_s,
    cx_r,
    cz_s,
    cz_r,
    cy_s,
    cy_r,
    cc_s,
    cc_r,
    mz_s,
    mz_r,
    my_s,
    my_r,
    fc_s,
    fc_r,
    fy_s,
    fy_r,
    fz_s,
    fz_r,
    fx_s,
    fx_r,
    gc_s,
    gc_r,
    gx_s,
    gx_r,
    gz_s,
    gz_r,
    gy_s,
    gy_r,
    az_s,
    az_r,
    ac_s,
    ac_r,
    loc,
    load_s,
):
    Z, Y, C, X = sizes
    NP = Z * Y * C
    R, D = grid_in.shape
    H = first_in.shape[1]
    F = second_in.shape[1]
    PX = PATCH // X
    GPD = R // PATCH
    HC = D // 2
    z, y, c, x = (lax.axis_index(a) for a in AXES)
    oc = 1 - c
    sent = []

    def send(src, dst, ss, rs, **where):
        place = {"patch_0": z, "patch_1": y, "patch_2": c, "mp": x}
        place.update(where)
        copy = pltpu.make_async_remote_copy(
            src_ref=src,
            dst_ref=dst,
            send_sem=ss,
            recv_sem=rs,
            device_id=place,
            device_id_type=pl.DeviceIdType.MESH,
        )
        copy.start()
        sent.append((src, dst, ss, rs))

    def arrive(dst, rs):
        pltpu.make_async_copy(dst, dst, rs).wait()

    def step(i, k, n):
        return lax.rem(i + k, n)

    xf = pl.ds(pl.multiple_of(x * F, F), F)
    xp = pl.ds(pl.multiple_of(x * PX, PX), PX)

    loads = {}
    for i, (name, src, dst) in enumerate(
        (
            ("cot", cot_in, cot_ref),
            ("w", w_in, w_ref),
            ("second", second_in, second_ref),
            ("grid", grid_in, grid_ref),
            ("first", first_in, first_ref),
            ("latent", latent_in, latent_ref),
        )
    ):
        loads[name] = pltpu.make_async_copy(src, dst, load_s.at[i])
        loads[name].start()

    barrier = pltpu.get_barrier_semaphore()

    def greet(j, carry):
        dz, dy, dc = j // (Y * 2), (j // 2) % Y, j % 2
        pl.semaphore_signal(
            barrier,
            inc=1,
            device_id={
                "patch_0": lax.rem(z + dz, Z),
                "patch_1": lax.rem(y + dy, Y),
                "patch_2": lax.rem(c + dc, 2),
                "mp": x,
            },
            device_id_type=pl.DeviceIdType.MESH,
        )
        return carry

    def greet_mp(j, carry):
        pl.semaphore_signal(
            barrier,
            inc=1,
            device_id={
                "patch_0": lax.rem(z + j % Z, Z),
                "patch_1": y,
                "patch_2": c,
                "mp": lax.rem(x + j // Z, X),
            },
            device_id_type=pl.DeviceIdType.MESH,
        )
        return carry

    lax.fori_loop(1, NP, greet, 0)
    lax.fori_loop(Z, X * Z, greet_mp, 0)

    n_slots = w_in.shape[0]

    def feeder(j):
        return jnp.where(live_ref[j] == 1, lax.div(source_ref[j], GPD), -1)

    lane = lax.broadcasted_iota(jnp.int32, (1, PATCH), 1)
    meta = jnp.zeros((1, PATCH), F32)
    for j in range(n_slots):
        inside = lax.rem(source_ref[j], GPD).astype(F32)
        meta = jnp.where(lane == feeder(j), inside, meta)
    meta_ref[...] = meta
    loads["w"].wait()

    def pack(i, carry):
        z1, c1, y1 = i // (2 * Y), (i // Y) % 2, i % Y
        natural = (z1 * Y + y1) * 2 + c1
        slot, live = jnp.int32(0), jnp.int32(0)
        for j in range(n_slots):
            hit = feeder(j) == natural
            slot = jnp.where(hit, j, slot)
            live = jnp.where(hit, 1, live)
        block = w_ref[slot, xp, :]
        slots[i] = (block.astype(F32) * live.astype(F32)).astype(BF16)
        return carry

    lax.fori_loop(0, NP, pack, 0)
    loads["cot"].wait()
    loads["second"].wait()
    own_cot = pltpu.make_async_copy(cot_ref.at[xp, :], cotb.at[z, c, y, :, xf], loc.at[0])
    own_cot.start()
    own_second = pltpu.make_async_copy(second_ref, second.at[:, xf], loc.at[1])
    own_second.start()
    own_meta = pltpu.make_async_copy(meta_ref, metab.at[z, c, y], loc.at[2])
    own_meta.start()
    here = (z * 2 + c) * Y + y
    own_slot = pltpu.make_async_copy(slots.at[here], V.at[here], loc.at[3])
    own_slot.start()
    pl.semaphore_wait(barrier, NP - 1 + (X - 1) * Z)

    own_meta.wait()
    near = [0]
    for t in range(1, Z // 2 + 1):
        near += [t, Z - t] if 2 * t < Z else [t]
    for k in near[1:]:
        send(
            metab.at[z, c, y],
            metab.at[z, c, y],
            mz_s.at[k - 1],
            mz_r.at[k - 1],
            patch_0=step(z, k, Z),
        )
    for k in near:
        for m in range(X):
            if k or m:
                to = step(x, m, X)
                rows = pl.ds(pl.multiple_of(to * PX, PX), PX)
                send(
                    cot_ref.at[rows, :],
                    cotb.at[z, c, y, :, xf],
                    cz_s.at[k, m],
                    cz_r.at[k],
                    patch_0=step(z, k, Z),
                    mp=to,
                )
    for k in range(1, X):
        to = step(x, k, X)
        send(second_ref, second.at[:, xf], sec_s.at[k - 1], sec_r.at[k - 1], mp=to)

    def send_slot(j, carry):
        dz, dy, dc = j // (Y * 2), (j // 2) % Y, j % 2
        z1, y1, c1 = lax.rem(z + dz, Z), lax.rem(y + dy, Y), lax.rem(c + dc, 2)
        pltpu.make_async_remote_copy(
            src_ref=slots.at[(z1 * 2 + c1) * Y + y1],
            dst_ref=V.at[here],
            send_sem=w_s,
            recv_sem=w_r.at[z],
            device_id={"patch_0": z1, "patch_1": y1, "patch_2": c1, "mp": x},
            device_id_type=pl.DeviceIdType.MESH,
        ).start()
        return carry

    for dz in near:
        lax.fori_loop(max(1, dz * Y * 2), (dz + 1) * Y * 2, send_slot, 0)

    TR = 2 * PATCH
    T = R // TR

    def first_layer(i):
        rows = pl.ds(i * TR, TR)
        pre = dot(grid_ref[rows, :], first_ref[...])
        s = jax.nn.sigmoid(pre)
        hidden[rows, :] = (pre * s).astype(BF16)
        slope[rows, :] = s * (1.0 + pre * (1.0 - s))

    def second_layer(i):
        rows = pl.ds(i * TR, TR)
        msg[rows, :] = dot(hidden[rows, :], second[...]).astype(BF16)

    def over_y(k):
        at = step(z, (Z - k) % Z, Z)
        if k:
            arrive(cotb.at[at, c, y], cz_r.at[k])
        else:
            own_cot.wait()
            arrive(cotb.at[at, c, y, :, pl.ds(0, (X - 1) * F)], cz_r.at[k])
        for m in range(1, Y):
            block = cotb.at[at, c, y]
            send(block, block, cy_s.at[m - 1, k], cy_r.at[m - 1, k], patch_1=step(y, m, Y))

    loads["grid"].wait()
    loads["first"].wait()
    per = -(-Z // T)
    for i in range(T):
        first_layer(i)
        for k in near[i * per : (i + 1) * per]:
            over_y(k)
        if i == 0:
            for k in range(1, Z):
                arrive(metab.at[step(z, Z - k, Z), c, y], mz_r.at[k - 1])
            for j in range(1, 2 * Y):
                send(
                    metab.at[:, c, y],
                    metab.at[:, c, y],
                    my_s.at[j],
                    my_r.at[j],
                    patch_1=step(y, j // 2, Y),
                    patch_2=lax.rem(c + j % 2, 2),
                )
    own_second.wait()
    for k in range(1, X):
        frm = step(x, X - k, X)
        arrive(second.at[:, pl.ds(pl.multiple_of(frm * F, F), F)], sec_r.at[k - 1])
    for i in range(T):
        second_layer(i)
    for j in range(1, 2 * Y):
        core, yy = lax.rem(c + j % 2, 2), step(y, Y - j // 2, Y)
        arrive(metab.at[:, core, yy], my_r.at[j])

    own_natural = (z * Y + y) * 2 + c
    PL = C * Y
    TP = PL * PX
    lanes = lax.broadcasted_iota(jnp.int32, (PL, PATCH), 1)

    def plane(k):
        return step(z, (Z - k) % Z, Z)

    def spread(at, slot):
        meta = metab[at].reshape(PL, PATCH)
        patch_of = jnp.sum(jnp.where(lanes == own_natural, meta, 0.0), axis=1, keepdims=True)
        patch_rows = jnp.broadcast_to(
            jnp.broadcast_to(patch_of, (PL, PATCH))[:, None, :], (PL, PX, PATCH)
        ).reshape(TP, PATCH)
        blocks = V[pl.ds(pl.multiple_of(at * PL, PL), PL)].reshape(TP, PATCH).astype(F32)
        blocks_t = blocks.T
        patch_cols = patch_rows.T
        for g in range(GPD):
            vbig[:, g * PATCH : (g + 1) * PATCH] = jnp.where(
                patch_rows == float(g), blocks, 0.0
            ).astype(BF16)
            vbig_t[slot, g * PATCH : (g + 1) * PATCH, :] = jnp.where(
                patch_cols == float(g), blocks_t, 0.0
            ).astype(BF16)

    def contribute(i, k):
        at, slot = plane(k), i % 2
        arrive(V.at[pl.ds(0, PL if k else PL - 1)], w_r.at[at])
        spread(at, slot)
        c_own[slot] = dot(vbig[...], msg[...]).reshape(C, Y, PX, D)
        c_send[at] = c_own[slot, oc].astype(BF16)
        send(c_send.at[at], c_recv.at[at], fc_s.at[k], fc_r.at[k], patch_2=oc)
        for m in range(1, Y):
            arrive(cotb.at[at, c, step(y, Y - m, Y)], cy_r.at[m - 1, k])
        send(cotb.at[at, c], cotb.at[at, c], cc_s.at[k], cc_r.at[k], patch_2=oc)

    def collect(i, k):
        at, slot = plane(k), i % 2
        arrive(c_recv.at[at], fc_r.at[k])
        c_sum[...] = c_own[slot, c] + c_recv[at].astype(F32)
        y_own[at] = c_sum[y]
        for m in range(1, Y):
            to = step(y, m, Y)
            y_send[m - 1, at] = c_sum[to].astype(BF16)
            send(
                y_send.at[m - 1, at],
                y_recv.at[m - 1, at],
                fy_s.at[m - 1, k],
                fy_r.at[m - 1, k],
                patch_1=to,
            )
        arrive(cotb.at[at, oc], cc_r.at[k])
        for t in range(T):
            rows = slice(t * TR, (t + 1) * TR)
            part = dot(vbig_t[slot, rows, :], cotb[at].reshape(TP, D))
            if i == 0:
                gm_sum[rows, :] = part
            elif i < Z - 1:
                gm_sum[rows, :] += part
            else:
                gm[rows, :] = (gm_sum[rows, :] + part).astype(BF16)

    own_slot.wait()
    for i, k in enumerate(near):
        contribute(i, k)
        if i:
            collect(i - 1, near[i - 1])
    collect(Z - 1, near[-1])

    def halves(which, left_ref, right_ref):
        for core in (oc, c):
            cols = pl.ds(pl.multiple_of(core * HC, HC), HC)
            part = dot(left_ref[:, cols], right_ref[...], ((0,), (0,))) * scaling
            for q in range(X):
                piece = part[:, q * F : (q + 1) * F]
                if core is oc:
                    gc_send[which, q] = piece
                else:
                    g_own[which, q] = piece
            if core is oc:
                send(
                    gc_send.at[which],
                    gc_recv.at[which],
                    gc_s.at[which],
                    gc_r.at[which],
                    patch_2=oc,
                )

    def over_mp(which):
        arrive(gc_recv.at[which], gc_r.at[which])
        for k in range(1, X):
            to = step(x, k, X)
            gx_send[which, k - 1] = (g_own[which, to] + gc_recv[which, to]).astype(BF16)
            send(
                gx_send.at[which, k - 1],
                gx_recv.at[which, k - 1],
                gx_s.at[which, k - 1],
                gx_r.at[which, k - 1],
                mp=to,
            )
        g_own[which, x] = g_own[which, x] + gc_recv[which, x]

    halves(0, hidden, gm)

    def pre_gradient(i, carry):
        rows = pl.ds(pl.multiple_of(i * TR, TR), TR)
        back = dot(gm[rows, :], second[...], ((1,), (1,)))
        gpre[rows, :] = (back * slope[rows, :]).astype(BF16)
        return carry

    lax.fori_loop(0, R // TR, pre_gradient, 0)
    over_mp(0)

    halves(1, grid_ref, gpre)

    over_mp(1)

    for k in near:
        at = plane(k)
        total = y_own[at]
        for m in range(1, Y):
            arrive(y_recv.at[m - 1, at], fy_r.at[m - 1, k])
            total = total + y_recv[m - 1, at].astype(F32)
        if k:
            z_send[at] = total.astype(BF16)
            send(z_send.at[at], z_recv.at[k - 1], fz_s.at[k - 1], fz_r.at[k - 1], patch_0=at)
        else:
            y_own[at] = total

    ZR = HC // Z
    for which in range(2):
        total = g_own[which, x]
        for k in range(1, X):
            arrive(gx_recv.at[which, k - 1], gx_r.at[which, k - 1])
            total = total + gx_recv[which, k - 1].astype(F32)
        g_own[which, x] = total
        gz_send[:, which] = total.reshape(Z, ZR, F).astype(BF16)
    for k in range(1, Z):
        to = step(z, k, Z)
        send(gz_send.at[to], gz_recv.at[k - 1], gz_s.at[k - 1], gz_r.at[k - 1], patch_0=to)

    total = g_own[:, x, pl.ds(pl.multiple_of(z * ZR, ZR), ZR)]
    for k in range(1, Z):
        arrive(gz_recv.at[k - 1], gz_r.at[k - 1])
        total = total + gz_recv[k - 1].astype(F32)
    gy[y] = total
    for k in range(1, Y):
        to = step(y, k, Y)
        send(gy.at[y], gy.at[y], gy_s.at[k - 1], gy_r.at[k - 1], patch_1=to)

    for k in range(1, Y):
        arrive(gy.at[step(y, Y - k, Y)], gy_r.at[k - 1])
    total = gy[0]
    for yy in range(1, Y):
        total = total + gy[yy]
    own[...] = total.astype(BF16)
    for k in range(1, Z):
        to = step(z, k, Z)
        send(own, fin.at[c, z], az_s.at[k - 1], az_r.at[k - 1], patch_0=to)
    fin[c, z] = own[...]

    total = y_own[z]
    for k in range(1, Z):
        arrive(z_recv.at[k - 1], fz_r.at[k - 1])
        total = total + z_recv[k - 1].astype(F32)
    for q in range(X):
        x_send[q] = total[:, q * F : (q + 1) * F]
    own_sum = pltpu.make_async_copy(x_send.at[x], x_recv.at[x], loc.at[0])
    own_sum.start()
    for k in range(1, X):
        to = step(x, k, X)
        send(x_send.at[to], x_recv.at[x], fx_s.at[k - 1], fx_r.at[k - 1], mp=to)

    for k in range(1, Z):
        arrive(fin.at[c, step(z, Z - k, Z)], az_r.at[k - 1])
    send(fin.at[c], fin.at[c], ac_s.at[0], ac_r.at[0], patch_2=oc)
    own_sum.wait()
    for k in range(1, X):
        arrive(x_recv.at[step(x, X - k, X)], fx_r.at[k - 1])
    loads["latent"].wait()
    mesh_out[...] = (latent_ref[...].astype(F32) + x_recv[...].reshape(PATCH, F)).astype(BF16)
    arrive(fin.at[oc], ac_r.at[0])
    pltpu.make_async_remote_copy(
        src_ref=all_but_one(slots, NP),
        dst_ref=all_but_one(V, NP),
        send_sem=w_s,
        recv_sem=w_r.at[0],
        device_id={"patch_0": z, "patch_1": y, "patch_2": oc, "mp": x},
        device_id_type=pl.DeviceIdType.MESH,
    ).wait_send()
    for src, dst, ss, rs in sent:
        pltpu.make_async_copy(src, src, ss).wait()


def hand_out(mesh_sum, sums, mesh_out, first_out, second_out):
    mesh_out[...] = mesh_sum[...]
    second_out[...] = sums[:, :, 0].reshape(second_out.shape).astype(F32)
    first_out[...] = sums[:, :, 1].reshape(first_out.shape).astype(F32)


def all_but_one(ref, n):
    return ref.at[pl.ds(0, n - 1)]


def per_device(
    grid_latent,
    mesh_latent,
    edge_weight,
    block_source,
    block_live,
    mlp_first,
    mlp_second,
    mesh_cotangent,
):
    Z, Y, C = (lax.axis_size(a) for a in PATCH_AXES)
    X = lax.axis_size("mp")
    NP = Z * Y * C
    R, D = grid_latent.shape
    H = mlp_first.shape[1]
    F = mlp_second.shape[1]
    PX = PATCH // X
    GPD = R // PATCH
    HC = D // 2
    ZR = HC // Z
    scaling = 1.0 / math.sqrt(R * NP)

    vm = pltpu.VMEM
    dma = pltpu.SemaphoreType.DMA
    scratch = [
        vm((1, PATCH), F32),
        vm(grid_latent.shape, BF16),
        vm(mesh_latent.shape, BF16),
        vm(edge_weight.shape, BF16),
        vm(mlp_first.shape, BF16),
        vm(mlp_second.shape, BF16),
        vm(mesh_cotangent.shape, BF16),
        vm((NP, PX, PATCH), BF16),
        vm((NP, PX, PATCH), BF16),
        vm((Z, C, Y, PX, D), BF16),
        vm((Z, C, Y, 1, PATCH), F32),
        vm((H, D), BF16),
        vm((R, H), F32),
        vm((R, H), BF16),
        vm((R, D), BF16),
        vm((C * Y * PX, R), BF16),
        vm((2, R, C * Y * PX), BF16),
        vm((2, C, Y, PX, D), F32),
        vm((Y, PX, D), F32),
        vm((Z, Y, PX, D), BF16),
        vm((Z, Y, PX, D), BF16),
        vm((Y - 1, Z, PX, D), BF16),
        vm((Y - 1, Z, PX, D), BF16),
        vm((Z, PX, D), F32),
        vm((Z, PX, D), BF16),
        vm((Z - 1, PX, D), BF16),
        vm((X, PX, F), F32),
        vm((X, PX, F), F32),
        vm((R, D), F32),
        vm((R, D), BF16),
        vm((R, H), BF16),
        vm((2, X, HC, F), F32),
        vm((2, X, HC, F), F32),
        vm((2, X, HC, F), F32),
        vm((2, X - 1, HC, F), BF16),
        vm((2, X - 1, HC, F), BF16),
        vm((Z, 2, ZR, F), BF16),
        vm((Z - 1, 2, ZR, F), BF16),
        vm((Y, 2, ZR, F), F32),
        vm((2, ZR, F), BF16),
        dma,
        dma((Z,)),
        dma((X - 1,)),
        dma((X - 1,)),
        dma((X - 1,)),
        dma((X - 1,)),
        dma((Z, X)),
        dma((Z,)),
        dma((Y - 1, Z)),
        dma((Y - 1, Z)),
        dma((Z,)),
        dma((Z,)),
        dma((Z - 1,)),
        dma((Z - 1,)),
        dma((2 * Y,)),
        dma((2 * Y,)),
        dma((Z,)),
        dma((Z,)),
        dma((Y - 1, Z)),
        dma((Y - 1, Z)),
        dma((Z - 1,)),
        dma((Z - 1,)),
        dma((X - 1,)),
        dma((X - 1,)),
        dma((2,)),
        dma((2,)),
        dma((2, X - 1)),
        dma((2, X - 1)),
        dma((Z - 1,)),
        dma((Z - 1,)),
        dma((Y - 1,)),
        dma((Y - 1,)),
        dma((Z - 1,)),
        dma((Z - 1,)),
        dma((1,)),
        dma((1,)),
        dma((4,)),
        dma((6,)),
    ]
    in_vmem = pl.BlockSpec(memory_space=pltpu.VMEM)
    mesh_sum, sums = pl.pallas_call(
        functools.partial(kernel, (Z, Y, C, X), scaling),
        out_shape=(
            jax.ShapeDtypeStruct((PATCH, F), BF16),
            jax.ShapeDtypeStruct((C, Z, 2, ZR, F), BF16),
        ),
        in_specs=[pl.BlockSpec(memory_space=pltpu.SMEM)] * 2
        + [pl.BlockSpec(memory_space=pl.ANY)] * 6,
        out_specs=(in_vmem, in_vmem),
        scratch_shapes=scratch,
        compiler_params=pltpu.CompilerParams(
            collective_id=0, has_side_effects=True, vmem_limit_bytes=62 * 1024 * 1024
        ),
    )(
        block_source,
        block_live,
        grid_latent,
        mesh_latent,
        edge_weight,
        mlp_first,
        mlp_second,
        mesh_cotangent,
    )
    return pl.pallas_call(
        hand_out,
        out_shape=(
            jax.ShapeDtypeStruct((PATCH, F), BF16),
            jax.ShapeDtypeStruct((D, F), F32),
            jax.ShapeDtypeStruct((H, F), F32),
        ),
        in_specs=[in_vmem] * 2,
        out_specs=(in_vmem, in_vmem, in_vmem),
    )(mesh_sum, sums)


def torus_of(mesh):
    return Mesh(mesh.devices.reshape(8, 4, 2, mesh.shape["mp"]), AXES)


def solution(mesh):
    torus = torus_of(mesh)
    in_specs = (
        P(PATCH_AXES, None),
        P(PATCH_AXES, "mp"),
        P(PATCH_AXES, None, None),
        P(PATCH_AXES),
        P(PATCH_AXES),
        P(),
        P(None, "mp"),
        P(PATCH_AXES, "mp"),
    )
    out_specs = (P(PATCH_AXES, "mp"), P(None, "mp"), P(None, "mp"))
    return jax.shard_map(
        per_device, mesh=torus, in_specs=in_specs, out_specs=out_specs, check_vma=False
    )
```

```python
import functools
import math

import jax
import jax.numpy as jnp
from jax import lax
from jax.experimental import pallas as pl
from jax.experimental.pallas import tpu as pltpu
from jax.sharding import Mesh
from jax.sharding import PartitionSpec as P

PATCH = 128
PATCH_AXES = ("patch_0", "patch_1", "patch_2")
AXES = PATCH_AXES + ("mp",)
F32 = jnp.float32
BF16 = jnp.bfloat16


def dot(a, b, dims=((1,), (0,))):
    return lax.dot_general(a, b, (dims, ((), ())), preferred_element_type=F32)


def kernel(
    sizes,
    scaling,
    source_ref,
    live_ref,
    grid_in,
    latent_in,
    w_in,
    first_in,
    second_in,
    cot_in,
    mesh_out,
    fin,
    meta_ref,
    grid_ref,
    latent_ref,
    w_ref,
    first_ref,
    second_ref,
    cot_ref,
    slots,
    V,
    cotb,
    metab,
    second,
    slope,
    hidden,
    msg,
    vbig,
    vbig_t,
    c_own,
    c_sum,
    c_send,
    c_recv,
    y_send,
    y_recv,
    y_own,
    z_send,
    z_recv,
    x_send,
    x_recv,
    gm_sum,
    gm,
    gpre,
    gc_send,
    gc_recv,
    g_own,
    gx_send,
    gx_recv,
    gz_send,
    gz_recv,
    gy,
    own,
    w_s,
    w_r,
    sec_s,
    sec_r,
    cx_s,
    cx_r,
    cz_s,
    cz_r,
    cy_s,
    cy_r,
    cc_s,
    cc_r,
    mz_s,
    mz_r,
    my_s,
    my_r,
    fc_s,
    fc_r,
    fy_s,
    fy_r,
    fz_s,
    fz_r,
    fx_s,
    fx_r,
    gc_s,
    gc_r,
    gx_s,
    gx_r,
    gz_s,
    gz_r,
    gy_s,
    gy_r,
    az_s,
    az_r,
    ac_s,
    ac_r,
    loc,
    load_s,
):
    Z, Y, C, X = sizes
    NP = Z * Y * C
    R, D = grid_in.shape
    H = first_in.shape[1]
    F = second_in.shape[1]
    PX = PATCH // X
    GPD = R // PATCH
    HC = D // 2
    z, y, c, x = (lax.axis_index(a) for a in AXES)
    oc = 1 - c
    sent = []

    def send(src, dst, ss, rs, **where):
        place = {"patch_0": z, "patch_1": y, "patch_2": c, "mp": x}
        place.update(where)
        copy = pltpu.make_async_remote_copy(
            src_ref=src,
            dst_ref=dst,
            send_sem=ss,
            recv_sem=rs,
            device_id=place,
            device_id_type=pl.DeviceIdType.MESH,
        )
        copy.start()
        sent.append((src, dst, ss, rs))

    def arrive(dst, rs):
        pltpu.make_async_copy(dst, dst, rs).wait()

    def step(i, k, n):
        return lax.rem(i + k, n)

    xf = pl.ds(pl.multiple_of(x * F, F), F)
    xp = pl.ds(pl.multiple_of(x * PX, PX), PX)

    loads = {}
    for i, (name, src, dst) in enumerate(
        (
            ("cot", cot_in, cot_ref),
            ("w", w_in, w_ref),
            ("second", second_in, second_ref),
            ("grid", grid_in, grid_ref),
            ("first", first_in, first_ref),
            ("latent", latent_in, latent_ref),
        )
    ):
        loads[name] = pltpu.make_async_copy(src, dst, load_s.at[i])
        loads[name].start()

    barrier = pltpu.get_barrier_semaphore()

    def greet(j, carry):
        dz, dy, dc = j // (Y * 2), (j // 2) % Y, j % 2
        pl.semaphore_signal(
            barrier,
            inc=1,
            device_id={
                "patch_0": lax.rem(z + dz, Z),
                "patch_1": lax.rem(y + dy, Y),
                "patch_2": lax.rem(c + dc, 2),
                "mp": x,
            },
            device_id_type=pl.DeviceIdType.MESH,
        )
        return carry

    def greet_mp(j, carry):
        pl.semaphore_signal(
            barrier,
            inc=1,
            device_id={
                "patch_0": lax.rem(z + j % Z, Z),
                "patch_1": y,
                "patch_2": c,
                "mp": lax.rem(x + j // Z, X),
            },
            device_id_type=pl.DeviceIdType.MESH,
        )
        return carry

    lax.fori_loop(1, NP, greet, 0)
    lax.fori_loop(Z, X * Z, greet_mp, 0)

    n_slots = w_in.shape[0]

    def feeder(j):
        return jnp.where(live_ref[j] == 1, lax.div(source_ref[j], GPD), -1)

    lane = lax.broadcasted_iota(jnp.int32, (1, PATCH), 1)
    meta = jnp.zeros((1, PATCH), F32)
    for j in range(n_slots):
        inside = lax.rem(source_ref[j], GPD).astype(F32)
        meta = jnp.where(lane == feeder(j), inside, meta)
    meta_ref[...] = meta
    loads["w"].wait()

    def pack(i, carry):
        z1, c1, y1 = i // (2 * Y), (i // Y) % 2, i % Y
        natural = (z1 * Y + y1) * 2 + c1
        slot, live = jnp.int32(0), jnp.int32(0)
        for j in range(n_slots):
            hit = feeder(j) == natural
            slot = jnp.where(hit, j, slot)
            live = jnp.where(hit, 1, live)
        block = w_ref[slot, xp, :]
        slots[i] = (block.astype(F32) * live.astype(F32)).astype(BF16)
        return carry

    lax.fori_loop(0, NP, pack, 0)
    loads["cot"].wait()
    loads["second"].wait()
    own_cot = pltpu.make_async_copy(cot_ref.at[xp, :], cotb.at[z, c, y, :, xf], loc.at[0])
    own_cot.start()
    half = pl.ds(pl.multiple_of(c * (H // 2), H // 2), H // 2)
    other_half = pl.ds(pl.multiple_of(oc * (H // 2), H // 2), H // 2)
    own_second = pltpu.make_async_copy(second_ref.at[half], second.at[half, xf], loc.at[1])
    own_second.start()
    own_meta = pltpu.make_async_copy(meta_ref, metab.at[z, c, y], loc.at[2])
    own_meta.start()
    here = (z * 2 + c) * Y + y
    own_slot = pltpu.make_async_copy(slots.at[here], V.at[here], loc.at[3])
    own_slot.start()
    pl.semaphore_wait(barrier, NP - 1 + (X - 1) * Z)

    own_meta.wait()
    near = [0]
    for t in range(1, Z // 2 + 1):
        near += [t, Z - t] if 2 * t < Z else [t]
    for k in near[1:]:
        send(
            metab.at[z, c, y],
            metab.at[z, c, y],
            mz_s.at[k - 1],
            mz_r.at[k - 1],
            patch_0=step(z, k, Z),
        )
    for k in near:
        for m in range(X):
            if k or m:
                to = step(x, m, X)
                rows = pl.ds(pl.multiple_of(to * PX, PX), PX)
                send(
                    cot_ref.at[rows, :],
                    cotb.at[z, c, y, :, xf],
                    cz_s.at[k, m],
                    cz_r.at[k],
                    patch_0=step(z, k, Z),
                    mp=to,
                )
    for k in range(1, X):
        to = step(x, k, X)
        send(
            second_ref.at[half], second.at[half, xf], sec_s.at[k - 1], sec_r.at[k - 1], mp=to
        )

    def send_slot(j, carry):
        dz, dy, dc = j // (Y * 2), (j // 2) % Y, j % 2
        z1, y1, c1 = lax.rem(z + dz, Z), lax.rem(y + dy, Y), lax.rem(c + dc, 2)
        pltpu.make_async_remote_copy(
            src_ref=slots.at[(z1 * 2 + c1) * Y + y1],
            dst_ref=V.at[here],
            send_sem=w_s,
            recv_sem=w_r.at[z],
            device_id={"patch_0": z1, "patch_1": y1, "patch_2": c1, "mp": x},
            device_id_type=pl.DeviceIdType.MESH,
        ).start()
        return carry

    for dz in near:
        lax.fori_loop(max(1, dz * Y * 2), (dz + 1) * Y * 2, send_slot, 0)

    TR = 2 * PATCH
    T = R // TR

    def first_layer(i):
        rows = pl.ds(i * TR, TR)
        pre = dot(grid_ref[rows, :], first_ref[...])
        s = jax.nn.sigmoid(pre)
        hidden[rows, :] = (pre * s).astype(BF16)
        slope[rows, :] = s * (1.0 + pre * (1.0 - s))

    def second_layer(i):
        rows = pl.ds(i * TR, TR)
        msg[rows, :] = dot(hidden[rows, :], second[...]).astype(BF16)

    def over_y(k):
        at = step(z, (Z - k) % Z, Z)
        if k:
            arrive(cotb.at[at, c, y], cz_r.at[k])
        else:
            own_cot.wait()
            arrive(cotb.at[at, c, y, :, pl.ds(0, (X - 1) * F)], cz_r.at[k])
        for m in range(1, Y):
            block = cotb.at[at, c, y]
            send(block, block, cy_s.at[m - 1, k], cy_r.at[m - 1, k], patch_1=step(y, m, Y))

    loads["grid"].wait()
    loads["first"].wait()
    per = -(-Z // T)
    for i in range(T):
        first_layer(i)
        for k in near[i * per : (i + 1) * per]:
            over_y(k)
        if i == 0:
            for k in range(1, Z):
                arrive(metab.at[step(z, Z - k, Z), c, y], mz_r.at[k - 1])
            for j in range(1, 2 * Y):
                send(
                    metab.at[:, c, y],
                    metab.at[:, c, y],
                    my_s.at[j],
                    my_r.at[j],
                    patch_1=step(y, j // 2, Y),
                    patch_2=lax.rem(c + j % 2, 2),
                )
    own_second.wait()
    for k in range(1, X):
        frm = step(x, X - k, X)
        arrive(second.at[half, pl.ds(pl.multiple_of(frm * F, F), F)], sec_r.at[k - 1])
    send(second.at[half], second.at[half], sec_s.at[X - 1], sec_r.at[X - 1], patch_2=oc)
    arrive(second.at[other_half], sec_r.at[X - 1])
    for i in range(T):
        second_layer(i)
    for j in range(1, 2 * Y):
        core, yy = lax.rem(c + j % 2, 2), step(y, Y - j // 2, Y)
        arrive(metab.at[:, core, yy], my_r.at[j])

    own_natural = (z * Y + y) * 2 + c
    PL = C * Y
    TP = PL * PX
    lanes = lax.broadcasted_iota(jnp.int32, (PL, PATCH), 1)
    of_receiver = lax.broadcasted_iota(jnp.int32, (PL, TP), 1) // PX == lax.broadcasted_iota(
        jnp.int32, (PL, TP), 0
    )

    def plane(k):
        return step(z, (Z - k) % Z, Z)

    def spread(at, slot):
        meta = metab[at].reshape(PL, PATCH)
        patch_of = jnp.sum(jnp.where(lanes == own_natural, meta, 0.0), axis=1, keepdims=True)
        patch_rows = jnp.broadcast_to(jnp.broadcast_to(patch_of, (PL, PATCH))[:, None], (PL, 8, PATCH))
        patch_cols = jnp.sum(
            jnp.where(of_receiver, jnp.broadcast_to(patch_of, (PL, TP)), 0.0),
            axis=0,
            keepdims=True,
        )
        blocks = V[pl.ds(pl.multiple_of(at * PL, PL), PL)].reshape(TP, PATCH).astype(F32)
        blocks_t = blocks.T
        tiles = blocks.reshape(PL, PX // 8, 8, PATCH)
        for g in range(GPD):
            in_rows = jnp.where(patch_rows == float(g), 1.0, 0.0)
            vbig[:, g * PATCH : (g + 1) * PATCH] = (
                (tiles * in_rows[:, None]).reshape(TP, PATCH).astype(BF16)
            )
            in_cols = jnp.where(patch_cols == float(g), 1.0, 0.0)
            vbig_t[slot, g * PATCH : (g + 1) * PATCH, :] = (blocks_t * in_cols).astype(BF16)

    def contribute(i, k):
        at, slot = plane(k), i % 2
        arrive(V.at[pl.ds(0, PL if k else PL - 1)], w_r.at[at])
        spread(at, slot)
        c_own[slot] = dot(vbig[...], msg[...]).reshape(C, Y, PX, D)
        c_send[at] = c_own[slot, oc].astype(BF16)
        send(c_send.at[at], c_recv.at[at], fc_s.at[k], fc_r.at[k], patch_2=oc)
        for m in range(1, Y):
            arrive(cotb.at[at, c, step(y, Y - m, Y)], cy_r.at[m - 1, k])
        send(cotb.at[at, c], cotb.at[at, c], cc_s.at[k], cc_r.at[k], patch_2=oc)

    def collect(i, k):
        at, slot = plane(k), i % 2
        arrive(c_recv.at[at], fc_r.at[k])
        c_sum[...] = c_own[slot, c] + c_recv[at].astype(F32)
        y_own[at] = c_sum[y]
        for m in range(1, Y):
            to = step(y, m, Y)
            y_send[m - 1, at] = c_sum[to].astype(BF16)
            send(
                y_send.at[m - 1, at],
                y_recv.at[m - 1, at],
                fy_s.at[m - 1, k],
                fy_r.at[m - 1, k],
                patch_1=to,
            )
        arrive(cotb.at[at, oc], cc_r.at[k])
        for t in range(T):
            rows = slice(t * TR, (t + 1) * TR)
            part = dot(vbig_t[slot, rows, :], cotb[at].reshape(TP, D))
            if i == 0:
                gm_sum[rows, :] = part
            elif i < Z - 1:
                gm_sum[rows, :] += part
            else:
                gm[rows, :] = (gm_sum[rows, :] + part).astype(BF16)

    own_slot.wait()
    for i, k in enumerate(near):
        contribute(i, k)
        if i:
            collect(i - 1, near[i - 1])
    collect(Z - 1, near[-1])

    def halves(which, left_ref, right_ref):
        for core in (oc, c):
            cols = pl.ds(pl.multiple_of(core * HC, HC), HC)
            part = dot(left_ref[:, cols], right_ref[...], ((0,), (0,))) * scaling
            for q in range(X):
                piece = part[:, q * F : (q + 1) * F]
                if core is oc:
                    gc_send[which, q] = piece
                else:
                    g_own[which, q] = piece
            if core is oc:
                send(
                    gc_send.at[which],
                    gc_recv.at[which],
                    gc_s.at[which],
                    gc_r.at[which],
                    patch_2=oc,
                )

    def over_mp(which):
        arrive(gc_recv.at[which], gc_r.at[which])
        for k in range(1, X):
            to = step(x, k, X)
            gx_send[which, k - 1] = (g_own[which, to] + gc_recv[which, to]).astype(BF16)
            send(
                gx_send.at[which, k - 1],
                gx_recv.at[which, k - 1],
                gx_s.at[which, k - 1],
                gx_r.at[which, k - 1],
                mp=to,
            )
        g_own[which, x] = g_own[which, x] + gc_recv[which, x]

    halves(0, hidden, gm)

    def pre_gradient(i, carry):
        rows = pl.ds(pl.multiple_of(i * TR, TR), TR)
        back = dot(gm[rows, :], second[...], ((1,), (1,)))
        gpre[rows, :] = (back * slope[rows, :]).astype(BF16)
        return carry

    lax.fori_loop(0, R // TR, pre_gradient, 0)
    over_mp(0)

    halves(1, grid_ref, gpre)

    over_mp(1)

    for k in near:
        at = plane(k)
        total = y_own[at]
        for m in range(1, Y):
            arrive(y_recv.at[m - 1, at], fy_r.at[m - 1, k])
            total = total + y_recv[m - 1, at].astype(F32)
        if k:
            z_send[at] = total.astype(BF16)
            send(z_send.at[at], z_recv.at[k - 1], fz_s.at[k - 1], fz_r.at[k - 1], patch_0=at)
        else:
            y_own[at] = total

    ZR = HC // Z
    for which in range(2):
        total = g_own[which, x]
        for k in range(1, X):
            arrive(gx_recv.at[which, k - 1], gx_r.at[which, k - 1])
            total = total + gx_recv[which, k - 1].astype(F32)
        g_own[which, x] = total
        gz_send[:, which] = total.reshape(Z, ZR, F).astype(BF16)
    for k in range(1, Z):
        to = step(z, k, Z)
        send(gz_send.at[to], gz_recv.at[k - 1], gz_s.at[k - 1], gz_r.at[k - 1], patch_0=to)

    total = g_own[:, x, pl.ds(pl.multiple_of(z * ZR, ZR), ZR)]
    for k in range(1, Z):
        arrive(gz_recv.at[k - 1], gz_r.at[k - 1])
        total = total + gz_recv[k - 1].astype(F32)
    gy[y] = total
    for k in range(1, Y):
        to = step(y, k, Y)
        send(gy.at[y], gy.at[y], gy_s.at[k - 1], gy_r.at[k - 1], patch_1=to)

    for k in range(1, Y):
        arrive(gy.at[step(y, Y - k, Y)], gy_r.at[k - 1])
    total = gy[0]
    for yy in range(1, Y):
        total = total + gy[yy]
    own[...] = total.astype(BF16)
    for k in range(1, Z):
        to = step(z, k, Z)
        send(own, fin.at[c, z], az_s.at[k - 1], az_r.at[k - 1], patch_0=to)
    fin[c, z] = own[...]

    total = y_own[z]
    for k in range(1, Z):
        arrive(z_recv.at[k - 1], fz_r.at[k - 1])
        total = total + z_recv[k - 1].astype(F32)
    for q in range(X):
        x_send[q] = total[:, q * F : (q + 1) * F]
    own_sum = pltpu.make_async_copy(x_send.at[x], x_recv.at[x], loc.at[0])
    own_sum.start()
    for k in range(1, X):
        to = step(x, k, X)
        send(x_send.at[to], x_recv.at[x], fx_s.at[k - 1], fx_r.at[k - 1], mp=to)

    for k in range(1, Z):
        arrive(fin.at[c, step(z, Z - k, Z)], az_r.at[k - 1])
    send(fin.at[c], fin.at[c], ac_s.at[0], ac_r.at[0], patch_2=oc)
    own_sum.wait()
    for k in range(1, X):
        arrive(x_recv.at[step(x, X - k, X)], fx_r.at[k - 1])
    loads["latent"].wait()
    mesh_out[...] = (latent_ref[...].astype(F32) + x_recv[...].reshape(PATCH, F)).astype(BF16)
    arrive(fin.at[oc], ac_r.at[0])
    pltpu.make_async_remote_copy(
        src_ref=all_but_one(slots, NP),
        dst_ref=all_but_one(V, NP),
        send_sem=w_s,
        recv_sem=w_r.at[0],
        device_id={"patch_0": z, "patch_1": y, "patch_2": oc, "mp": x},
        device_id_type=pl.DeviceIdType.MESH,
    ).wait_send()
    for src, dst, ss, rs in sent:
        pltpu.make_async_copy(src, src, ss).wait()


def hand_out(mesh_sum, sums, mesh_out, first_out, second_out):
    mesh_out[...] = mesh_sum[...]
    second_out[...] = sums[:, :, 0].reshape(second_out.shape).astype(F32)
    first_out[...] = sums[:, :, 1].reshape(first_out.shape).astype(F32)


def all_but_one(ref, n):
    return ref.at[pl.ds(0, n - 1)]


def per_device(
    grid_latent,
    mesh_latent,
    edge_weight,
    block_source,
    block_live,
    mlp_first,
    mlp_second,
    mesh_cotangent,
):
    Z, Y, C = (lax.axis_size(a) for a in PATCH_AXES)
    X = lax.axis_size("mp")
    NP = Z * Y * C
    R, D = grid_latent.shape
    H = mlp_first.shape[1]
    F = mlp_second.shape[1]
    PX = PATCH // X
    GPD = R // PATCH
    HC = D // 2
    ZR = HC // Z
    scaling = 1.0 / math.sqrt(R * NP)

    vm = pltpu.VMEM
    dma = pltpu.SemaphoreType.DMA
    scratch = [
        vm((1, PATCH), F32),
        vm(grid_latent.shape, BF16),
        vm(mesh_latent.shape, BF16),
        vm(edge_weight.shape, BF16),
        vm(mlp_first.shape, BF16),
        vm(mlp_second.shape, BF16),
        vm(mesh_cotangent.shape, BF16),
        vm((NP, PX, PATCH), BF16),
        vm((NP, PX, PATCH), BF16),
        vm((Z, C, Y, PX, D), BF16),
        vm((Z, C, Y, 1, PATCH), F32),
        vm((H, D), BF16),
        vm((R, H), F32),
        vm((R, H), BF16),
        vm((R, D), BF16),
        vm((C * Y * PX, R), BF16),
        vm((2, R, C * Y * PX), BF16),
        vm((2, C, Y, PX, D), F32),
        vm((Y, PX, D), F32),
        vm((Z, Y, PX, D), BF16),
        vm((Z, Y, PX, D), BF16),
        vm((Y - 1, Z, PX, D), BF16),
        vm((Y - 1, Z, PX, D), BF16),
        vm((Z, PX, D), F32),
        vm((Z, PX, D), BF16),
        vm((Z - 1, PX, D), BF16),
        vm((X, PX, F), F32),
        vm((X, PX, F), F32),
        vm((R, D), F32),
        vm((R, D), BF16),
        vm((R, H), BF16),
        vm((2, X, HC, F), F32),
        vm((2, X, HC, F), F32),
        vm((2, X, HC, F), F32),
        vm((2, X - 1, HC, F), BF16),
        vm((2, X - 1, HC, F), BF16),
        vm((Z, 2, ZR, F), BF16),
        vm((Z - 1, 2, ZR, F), BF16),
        vm((Y, 2, ZR, F), F32),
        vm((2, ZR, F), BF16),
        dma,
        dma((Z,)),
        dma((X,)),
        dma((X,)),
        dma((X - 1,)),
        dma((X - 1,)),
        dma((Z, X)),
        dma((Z,)),
        dma((Y - 1, Z)),
        dma((Y - 1, Z)),
        dma((Z,)),
        dma((Z,)),
        dma((Z - 1,)),
        dma((Z - 1,)),
        dma((2 * Y,)),
        dma((2 * Y,)),
        dma((Z,)),
        dma((Z,)),
        dma((Y - 1, Z)),
        dma((Y - 1, Z)),
        dma((Z - 1,)),
        dma((Z - 1,)),
        dma((X - 1,)),
        dma((X - 1,)),
        dma((2,)),
        dma((2,)),
        dma((2, X - 1)),
        dma((2, X - 1)),
        dma((Z - 1,)),
        dma((Z - 1,)),
        dma((Y - 1,)),
        dma((Y - 1,)),
        dma((Z - 1,)),
        dma((Z - 1,)),
        dma((1,)),
        dma((1,)),
        dma((4,)),
        dma((6,)),
    ]
    in_vmem = pl.BlockSpec(memory_space=pltpu.VMEM)
    mesh_sum, sums = pl.pallas_call(
        functools.partial(kernel, (Z, Y, C, X), scaling),
        out_shape=(
            jax.ShapeDtypeStruct((PATCH, F), BF16),
            jax.ShapeDtypeStruct((C, Z, 2, ZR, F), BF16),
        ),
        in_specs=[pl.BlockSpec(memory_space=pltpu.SMEM)] * 2
        + [pl.BlockSpec(memory_space=pl.ANY)] * 6,
        out_specs=(in_vmem, in_vmem),
        scratch_shapes=scratch,
        compiler_params=pltpu.CompilerParams(
            collective_id=0, has_side_effects=True, vmem_limit_bytes=62 * 1024 * 1024
        ),
    )(
        block_source,
        block_live,
        grid_latent,
        mesh_latent,
        edge_weight,
        mlp_first,
        mlp_second,
        mesh_cotangent,
    )
    return pl.pallas_call(
        hand_out,
        out_shape=(
            jax.ShapeDtypeStruct((PATCH, F), BF16),
            jax.ShapeDtypeStruct((D, F), F32),
            jax.ShapeDtypeStruct((H, F), F32),
        ),
        in_specs=[in_vmem] * 2,
        out_specs=(in_vmem, in_vmem, in_vmem),
    )(mesh_sum, sums)


def torus_of(mesh):
    return Mesh(mesh.devices.reshape(8, 4, 2, mesh.shape["mp"]), AXES)


def solution(mesh):
    torus = torus_of(mesh)
    in_specs = (
        P(PATCH_AXES, None),
        P(PATCH_AXES, "mp"),
        P(PATCH_AXES, None, None),
        P(PATCH_AXES),
        P(PATCH_AXES),
        P(),
        P(None, "mp"),
        P(PATCH_AXES, "mp"),
    )
    out_specs = (P(PATCH_AXES, "mp"), P(None, "mp"), P(None, "mp"))
    return jax.shard_map(
        per_device, mesh=torus, in_specs=in_specs, out_specs=out_specs, check_vma=False
    )
```

```python
import functools
import math

import jax
import jax.numpy as jnp
from jax import lax
from jax.experimental import pallas as pl
from jax.experimental.pallas import tpu as pltpu
from jax.sharding import Mesh
from jax.sharding import PartitionSpec as P

PATCH = 128
PATCH_AXES = ("patch_0", "patch_1", "patch_2")
AXES = PATCH_AXES + ("mp",)
F32 = jnp.float32
BF16 = jnp.bfloat16


def dot(a, b, dims=((1,), (0,))):
    return lax.dot_general(a, b, (dims, ((), ())), preferred_element_type=F32)


def kernel(
    sizes,
    scaling,
    source_ref,
    live_ref,
    grid_in,
    latent_in,
    w_in,
    first_in,
    second_in,
    cot_in,
    mesh_out,
    fin,
    meta_ref,
    grid_ref,
    latent_ref,
    w_ref,
    first_ref,
    second_ref,
    cot_ref,
    slots,
    V,
    cotb,
    metab,
    second,
    slope,
    hidden,
    msg,
    vbig,
    vbig_t,
    c_own,
    c_sum,
    c_send,
    c_recv,
    y_send,
    y_recv,
    y_own,
    z_send,
    z_recv,
    x_send,
    x_recv,
    gm_sum,
    gm,
    gpre,
    gc_send,
    gc_recv,
    g_own,
    gx_send,
    gx_recv,
    gz_send,
    gz_recv,
    gy,
    own,
    w_s,
    w_r,
    sec_s,
    sec_r,
    cx_s,
    cx_r,
    cz_s,
    cz_r,
    cy_s,
    cy_r,
    cc_s,
    cc_r,
    mz_s,
    mz_r,
    my_s,
    my_r,
    fc_s,
    fc_r,
    fy_s,
    fy_r,
    fz_s,
    fz_r,
    fx_s,
    fx_r,
    gc_s,
    gc_r,
    gx_s,
    gx_r,
    gz_s,
    gz_r,
    gy_s,
    gy_r,
    az_s,
    az_r,
    ac_s,
    ac_r,
    loc,
    load_s,
):
    Z, Y, C, X = sizes
    NP = Z * Y * C
    R, D = grid_in.shape
    H = first_in.shape[1]
    F = second_in.shape[1]
    PX = PATCH // X
    GPD = R // PATCH
    HC = D // 2
    z, y, c, x = (lax.axis_index(a) for a in AXES)
    oc = 1 - c
    sent = []

    def send(src, dst, ss, rs, **where):
        place = {"patch_0": z, "patch_1": y, "patch_2": c, "mp": x}
        place.update(where)
        copy = pltpu.make_async_remote_copy(
            src_ref=src,
            dst_ref=dst,
            send_sem=ss,
            recv_sem=rs,
            device_id=place,
            device_id_type=pl.DeviceIdType.MESH,
        )
        copy.start()
        sent.append((src, dst, ss, rs))

    def arrive(dst, rs):
        pltpu.make_async_copy(dst, dst, rs).wait()

    def step(i, k, n):
        return lax.rem(i + k, n)

    xf = pl.ds(pl.multiple_of(x * F, F), F)
    xp = pl.ds(pl.multiple_of(x * PX, PX), PX)

    loads = {}
    for i, (name, src, dst) in enumerate(
        (
            ("cot", cot_in, cot_ref),
            ("w", w_in, w_ref),
            ("second", second_in, second_ref),
            ("grid", grid_in, grid_ref),
            ("first", first_in, first_ref),
            ("latent", latent_in, latent_ref),
        )
    ):
        loads[name] = pltpu.make_async_copy(src, dst, load_s.at[i])
        loads[name].start()

    barrier = pltpu.get_barrier_semaphore()

    def greet(j, carry):
        dz, dy, dc = j // (Y * 2), (j // 2) % Y, j % 2
        pl.semaphore_signal(
            barrier,
            inc=1,
            device_id={
                "patch_0": lax.rem(z + dz, Z),
                "patch_1": lax.rem(y + dy, Y),
                "patch_2": lax.rem(c + dc, 2),
                "mp": x,
            },
            device_id_type=pl.DeviceIdType.MESH,
        )
        return carry

    def greet_mp(j, carry):
        pl.semaphore_signal(
            barrier,
            inc=1,
            device_id={
                "patch_0": lax.rem(z + j % Z, Z),
                "patch_1": y,
                "patch_2": c,
                "mp": lax.rem(x + j // Z, X),
            },
            device_id_type=pl.DeviceIdType.MESH,
        )
        return carry

    lax.fori_loop(1, NP, greet, 0)
    lax.fori_loop(Z, X * Z, greet_mp, 0)

    n_slots = w_in.shape[0]

    def feeder(j):
        return jnp.where(live_ref[j] == 1, lax.div(source_ref[j], GPD), -1)

    lane = lax.broadcasted_iota(jnp.int32, (1, PATCH), 1)
    meta = jnp.zeros((1, PATCH), F32)
    for j in range(n_slots):
        inside = lax.rem(source_ref[j], GPD).astype(F32)
        meta = jnp.where(lane == feeder(j), inside, meta)
    meta_ref[...] = meta
    loads["cot"].wait()
    loads["second"].wait()
    own_cot = pltpu.make_async_copy(cot_ref.at[xp, :], cotb.at[z, c, y, :, xf], loc.at[0])
    own_cot.start()
    half = pl.ds(pl.multiple_of(c * (H // 2), H // 2), H // 2)
    other_half = pl.ds(pl.multiple_of(oc * (H // 2), H // 2), H // 2)
    own_second = pltpu.make_async_copy(second_ref.at[half], second.at[half, xf], loc.at[1])
    own_second.start()
    own_meta = pltpu.make_async_copy(meta_ref, metab.at[z, c, y], loc.at[2])
    own_meta.start()
    here = (z * 2 + c) * Y + y
    pl.semaphore_wait(barrier, NP - 1 + (X - 1) * Z)

    own_meta.wait()
    near = [0]
    for t in range(1, Z // 2 + 1):
        near += [t, Z - t] if 2 * t < Z else [t]
    for k in near[1:]:
        send(
            metab.at[z, c, y],
            metab.at[z, c, y],
            mz_s.at[k - 1],
            mz_r.at[k - 1],
            patch_0=step(z, k, Z),
        )
    for k in near:
        for m in range(X):
            if k or m:
                to = step(x, m, X)
                rows = pl.ds(pl.multiple_of(to * PX, PX), PX)
                send(
                    cot_ref.at[rows, :],
                    cotb.at[z, c, y, :, xf],
                    cz_s.at[k, m],
                    cz_r.at[k],
                    patch_0=step(z, k, Z),
                    mp=to,
                )
    for k in range(1, X):
        to = step(x, k, X)
        send(
            second_ref.at[half], second.at[half, xf], sec_s.at[k - 1], sec_r.at[k - 1], mp=to
        )

    loads["w"].wait()

    def pack(i, carry):
        z1, c1, y1 = i // (2 * Y), (i // Y) % 2, i % Y
        natural = (z1 * Y + y1) * 2 + c1
        slot, live = jnp.int32(0), jnp.int32(0)
        for j in range(n_slots):
            hit = feeder(j) == natural
            slot = jnp.where(hit, j, slot)
            live = jnp.where(hit, 1, live)
        block = w_ref[slot, xp, :]
        slots[i] = (block.astype(F32) * live.astype(F32)).astype(BF16)
        return carry

    lax.fori_loop(0, NP, pack, 0)
    own_slot = pltpu.make_async_copy(slots.at[here], V.at[here], loc.at[3])
    own_slot.start()

    def send_slot(j, carry):
        dz, dy, dc = j // (Y * 2), (j // 2) % Y, j % 2
        z1, y1, c1 = lax.rem(z + dz, Z), lax.rem(y + dy, Y), lax.rem(c + dc, 2)
        pltpu.make_async_remote_copy(
            src_ref=slots.at[(z1 * 2 + c1) * Y + y1],
            dst_ref=V.at[here],
            send_sem=w_s,
            recv_sem=w_r.at[z],
            device_id={"patch_0": z1, "patch_1": y1, "patch_2": c1, "mp": x},
            device_id_type=pl.DeviceIdType.MESH,
        ).start()
        return carry

    for dz in near:
        lax.fori_loop(max(1, dz * Y * 2), (dz + 1) * Y * 2, send_slot, 0)

    TR = 2 * PATCH
    T = R // TR

    def first_layer(i):
        rows = pl.ds(i * TR, TR)
        pre = dot(grid_ref[rows, :], first_ref[...])
        s = jax.nn.sigmoid(pre)
        hidden[rows, :] = (pre * s).astype(BF16)
        slope[rows, :] = s * (1.0 + pre * (1.0 - s))

    def second_layer(i):
        rows = pl.ds(i * TR, TR)
        msg[rows, :] = dot(hidden[rows, :], second[...]).astype(BF16)

    def over_y(k):
        at = step(z, (Z - k) % Z, Z)
        if k:
            arrive(cotb.at[at, c, y], cz_r.at[k])
        else:
            own_cot.wait()
            arrive(cotb.at[at, c, y, :, pl.ds(0, (X - 1) * F)], cz_r.at[k])
        for m in range(1, Y):
            block = cotb.at[at, c, y]
            send(block, block, cy_s.at[m - 1, k], cy_r.at[m - 1, k], patch_1=step(y, m, Y))

    loads["grid"].wait()
    loads["first"].wait()
    per = -(-Z // T)
    for i in range(T):
        first_layer(i)
        for k in near[i * per : (i + 1) * per]:
            over_y(k)
        if i == 0:
            for k in range(1, Z):
                arrive(metab.at[step(z, Z - k, Z), c, y], mz_r.at[k - 1])
            for j in range(1, 2 * Y):
                send(
                    metab.at[:, c, y],
                    metab.at[:, c, y],
                    my_s.at[j],
                    my_r.at[j],
                    patch_1=step(y, j // 2, Y),
                    patch_2=lax.rem(c + j % 2, 2),
                )
    own_second.wait()
    for k in range(1, X):
        frm = step(x, X - k, X)
        arrive(second.at[half, pl.ds(pl.multiple_of(frm * F, F), F)], sec_r.at[k - 1])
    send(second.at[half], second.at[half], sec_s.at[X - 1], sec_r.at[X - 1], patch_2=oc)
    arrive(second.at[other_half], sec_r.at[X - 1])
    for i in range(T):
        second_layer(i)
    for j in range(1, 2 * Y):
        core, yy = lax.rem(c + j % 2, 2), step(y, Y - j // 2, Y)
        arrive(metab.at[:, core, yy], my_r.at[j])

    own_natural = (z * Y + y) * 2 + c
    PL = C * Y
    TP = PL * PX
    lanes = lax.broadcasted_iota(jnp.int32, (PL, PATCH), 1)
    of_receiver = lax.broadcasted_iota(jnp.int32, (PL, TP), 1) // PX == lax.broadcasted_iota(
        jnp.int32, (PL, TP), 0
    )

    def plane(k):
        return step(z, (Z - k) % Z, Z)

    def spread(at, slot):
        meta = metab[at].reshape(PL, PATCH)
        patch_of = jnp.sum(jnp.where(lanes == own_natural, meta, 0.0), axis=1, keepdims=True)
        patch_rows = jnp.broadcast_to(jnp.broadcast_to(patch_of, (PL, PATCH))[:, None], (PL, 8, PATCH))
        patch_cols = jnp.sum(
            jnp.where(of_receiver, jnp.broadcast_to(patch_of, (PL, TP)), 0.0),
            axis=0,
            keepdims=True,
        )
        blocks = V[pl.ds(pl.multiple_of(at * PL, PL), PL)].reshape(TP, PATCH).astype(F32)
        blocks_t = blocks.T
        tiles = blocks.reshape(PL, PX // 8, 8, PATCH)
        for g in range(GPD):
            in_rows = jnp.where(patch_rows == float(g), 1.0, 0.0)
            vbig[:, g * PATCH : (g + 1) * PATCH] = (
                (tiles * in_rows[:, None]).reshape(TP, PATCH).astype(BF16)
            )
            in_cols = jnp.where(patch_cols == float(g), 1.0, 0.0)
            vbig_t[slot, g * PATCH : (g + 1) * PATCH, :] = (blocks_t * in_cols).astype(BF16)

    def contribute(i, k):
        at, slot = plane(k), i % 2
        arrive(V.at[pl.ds(0, PL if k else PL - 1)], w_r.at[at])
        spread(at, slot)
        c_own[slot] = dot(vbig[...], msg[...]).reshape(C, Y, PX, D)
        c_send[at] = c_own[slot, oc].astype(BF16)
        send(c_send.at[at], c_recv.at[at], fc_s.at[k], fc_r.at[k], patch_2=oc)
        for m in range(1, Y):
            arrive(cotb.at[at, c, step(y, Y - m, Y)], cy_r.at[m - 1, k])
        send(cotb.at[at, c], cotb.at[at, c], cc_s.at[k], cc_r.at[k], patch_2=oc)

    def collect(i, k):
        at, slot = plane(k), i % 2
        arrive(c_recv.at[at], fc_r.at[k])
        c_sum[...] = c_own[slot, c] + c_recv[at].astype(F32)
        y_own[at] = c_sum[y]
        for m in range(1, Y):
            to = step(y, m, Y)
            y_send[m - 1, at] = c_sum[to].astype(BF16)
            send(
                y_send.at[m - 1, at],
                y_recv.at[m - 1, at],
                fy_s.at[m - 1, k],
                fy_r.at[m - 1, k],
                patch_1=to,
            )
        arrive(cotb.at[at, oc], cc_r.at[k])
        for t in range(T):
            rows = slice(t * TR, (t + 1) * TR)
            part = dot(vbig_t[slot, rows, :], cotb[at].reshape(TP, D))
            if i == 0:
                gm_sum[rows, :] = part
            elif i < Z - 1:
                gm_sum[rows, :] += part
            else:
                gm[rows, :] = (gm_sum[rows, :] + part).astype(BF16)

    own_slot.wait()
    for i, k in enumerate(near):
        contribute(i, k)
        if i:
            collect(i - 1, near[i - 1])
    collect(Z - 1, near[-1])

    def halves(which, left_ref, right_ref):
        for core in (oc, c):
            cols = pl.ds(pl.multiple_of(core * HC, HC), HC)
            part = dot(left_ref[:, cols], right_ref[...], ((0,), (0,))) * scaling
            for q in range(X):
                piece = part[:, q * F : (q + 1) * F]
                if core is oc:
                    gc_send[which, q] = piece
                else:
                    g_own[which, q] = piece
            if core is oc:
                send(
                    gc_send.at[which],
                    gc_recv.at[which],
                    gc_s.at[which],
                    gc_r.at[which],
                    patch_2=oc,
                )

    def over_mp(which):
        arrive(gc_recv.at[which], gc_r.at[which])
        for k in range(1, X):
            to = step(x, k, X)
            gx_send[which, k - 1] = (g_own[which, to] + gc_recv[which, to]).astype(BF16)
            send(
                gx_send.at[which, k - 1],
                gx_recv.at[which, k - 1],
                gx_s.at[which, k - 1],
                gx_r.at[which, k - 1],
                mp=to,
            )
        g_own[which, x] = g_own[which, x] + gc_recv[which, x]

    halves(0, hidden, gm)

    def pre_gradient(i, carry):
        rows = pl.ds(pl.multiple_of(i * TR, TR), TR)
        back = dot(gm[rows, :], second[...], ((1,), (1,)))
        gpre[rows, :] = (back * slope[rows, :]).astype(BF16)
        return carry

    lax.fori_loop(0, R // TR, pre_gradient, 0)
    over_mp(0)

    halves(1, grid_ref, gpre)

    over_mp(1)

    ZR = HC // Z
    for which in range(2):
        total = g_own[which, x]
        for k in range(1, X):
            arrive(gx_recv.at[which, k - 1], gx_r.at[which, k - 1])
            total = total + gx_recv[which, k - 1].astype(F32)
        g_own[which, x] = total
        gz_send[:, which] = total.reshape(Z, ZR, F).astype(BF16)
    for k in range(1, Z):
        to = step(z, k, Z)
        send(gz_send.at[to], gz_recv.at[k - 1], gz_s.at[k - 1], gz_r.at[k - 1], patch_0=to)

    for k in near:
        at = plane(k)
        total = y_own[at]
        for m in range(1, Y):
            arrive(y_recv.at[m - 1, at], fy_r.at[m - 1, k])
            total = total + y_recv[m - 1, at].astype(F32)
        if k:
            z_send[at] = total.astype(BF16)
            send(z_send.at[at], z_recv.at[k - 1], fz_s.at[k - 1], fz_r.at[k - 1], patch_0=at)
        else:
            y_own[at] = total

    total = g_own[:, x, pl.ds(pl.multiple_of(z * ZR, ZR), ZR)]
    for k in range(1, Z):
        arrive(gz_recv.at[k - 1], gz_r.at[k - 1])
        total = total + gz_recv[k - 1].astype(F32)
    gy[y] = total
    for k in range(1, Y):
        to = step(y, k, Y)
        send(gy.at[y], gy.at[y], gy_s.at[k - 1], gy_r.at[k - 1], patch_1=to)

    for k in range(1, Y):
        arrive(gy.at[step(y, Y - k, Y)], gy_r.at[k - 1])
    total = gy[0]
    for yy in range(1, Y):
        total = total + gy[yy]
    own[...] = total.astype(BF16)
    for k in range(1, Z):
        to = step(z, k, Z)
        send(own, fin.at[c, z], az_s.at[k - 1], az_r.at[k - 1], patch_0=to)
    fin[c, z] = own[...]

    total = y_own[z]
    for k in range(1, Z):
        arrive(z_recv.at[k - 1], fz_r.at[k - 1])
        total = total + z_recv[k - 1].astype(F32)
    for q in range(X):
        x_send[q] = total[:, q * F : (q + 1) * F]
    own_sum = pltpu.make_async_copy(x_send.at[x], x_recv.at[x], loc.at[0])
    own_sum.start()
    for k in range(1, X):
        to = step(x, k, X)
        send(x_send.at[to], x_recv.at[x], fx_s.at[k - 1], fx_r.at[k - 1], mp=to)

    for k in range(1, Z):
        arrive(fin.at[c, step(z, Z - k, Z)], az_r.at[k - 1])
    send(fin.at[c], fin.at[c], ac_s.at[0], ac_r.at[0], patch_2=oc)
    own_sum.wait()
    for k in range(1, X):
        arrive(x_recv.at[step(x, X - k, X)], fx_r.at[k - 1])
    loads["latent"].wait()
    mesh_out[...] = (latent_ref[...].astype(F32) + x_recv[...].reshape(PATCH, F)).astype(BF16)
    arrive(fin.at[oc], ac_r.at[0])
    pltpu.make_async_remote_copy(
        src_ref=all_but_one(slots, NP),
        dst_ref=all_but_one(V, NP),
        send_sem=w_s,
        recv_sem=w_r.at[0],
        device_id={"patch_0": z, "patch_1": y, "patch_2": oc, "mp": x},
        device_id_type=pl.DeviceIdType.MESH,
    ).wait_send()
    for src, dst, ss, rs in sent:
        pltpu.make_async_copy(src, src, ss).wait()


def hand_out(mesh_sum, sums, mesh_out, first_out, second_out):
    mesh_out[...] = mesh_sum[...]
    second_out[...] = sums[:, :, 0].reshape(second_out.shape).astype(F32)
    first_out[...] = sums[:, :, 1].reshape(first_out.shape).astype(F32)


def all_but_one(ref, n):
    return ref.at[pl.ds(0, n - 1)]


def per_device(
    grid_latent,
    mesh_latent,
    edge_weight,
    block_source,
    block_live,
    mlp_first,
    mlp_second,
    mesh_cotangent,
):
    Z, Y, C = (lax.axis_size(a) for a in PATCH_AXES)
    X = lax.axis_size("mp")
    NP = Z * Y * C
    R, D = grid_latent.shape
    H = mlp_first.shape[1]
    F = mlp_second.shape[1]
    PX = PATCH // X
    GPD = R // PATCH
    HC = D // 2
    ZR = HC // Z
    scaling = 1.0 / math.sqrt(R * NP)

    vm = pltpu.VMEM
    dma = pltpu.SemaphoreType.DMA
    scratch = [
        vm((1, PATCH), F32),
        vm(grid_latent.shape, BF16),
        vm(mesh_latent.shape, BF16),
        vm(edge_weight.shape, BF16),
        vm(mlp_first.shape, BF16),
        vm(mlp_second.shape, BF16),
        vm(mesh_cotangent.shape, BF16),
        vm((NP, PX, PATCH), BF16),
        vm((NP, PX, PATCH), BF16),
        vm((Z, C, Y, PX, D), BF16),
        vm((Z, C, Y, 1, PATCH), F32),
        vm((H, D), BF16),
        vm((R, H), F32),
        vm((R, H), BF16),
        vm((R, D), BF16),
        vm((C * Y * PX, R), BF16),
        vm((2, R, C * Y * PX), BF16),
        vm((2, C, Y, PX, D), F32),
        vm((Y, PX, D), F32),
        vm((Z, Y, PX, D), BF16),
        vm((Z, Y, PX, D), BF16),
        vm((Y - 1, Z, PX, D), BF16),
        vm((Y - 1, Z, PX, D), BF16),
        vm((Z, PX, D), F32),
        vm((Z, PX, D), BF16),
        vm((Z - 1, PX, D), BF16),
        vm((X, PX, F), F32),
        vm((X, PX, F), F32),
        vm((R, D), F32),
        vm((R, D), BF16),
        vm((R, H), BF16),
        vm((2, X, HC, F), F32),
        vm((2, X, HC, F), F32),
        vm((2, X, HC, F), F32),
        vm((2, X - 1, HC, F), BF16),
        vm((2, X - 1, HC, F), BF16),
        vm((Z, 2, ZR, F), BF16),
        vm((Z - 1, 2, ZR, F), BF16),
        vm((Y, 2, ZR, F), F32),
        vm((2, ZR, F), BF16),
        dma,
        dma((Z,)),
        dma((X,)),
        dma((X,)),
        dma((X - 1,)),
        dma((X - 1,)),
        dma((Z, X)),
        dma((Z,)),
        dma((Y - 1, Z)),
        dma((Y - 1, Z)),
        dma((Z,)),
        dma((Z,)),
        dma((Z - 1,)),
        dma((Z - 1,)),
        dma((2 * Y,)),
        dma((2 * Y,)),
        dma((Z,)),
        dma((Z,)),
        dma((Y - 1, Z)),
        dma((Y - 1, Z)),
        dma((Z - 1,)),
        dma((Z - 1,)),
        dma((X - 1,)),
        dma((X - 1,)),
        dma((2,)),
        dma((2,)),
        dma((2, X - 1)),
        dma((2, X - 1)),
        dma((Z - 1,)),
        dma((Z - 1,)),
        dma((Y - 1,)),
        dma((Y - 1,)),
        dma((Z - 1,)),
        dma((Z - 1,)),
        dma((1,)),
        dma((1,)),
        dma((4,)),
        dma((6,)),
    ]
    in_vmem = pl.BlockSpec(memory_space=pltpu.VMEM)
    mesh_sum, sums = pl.pallas_call(
        functools.partial(kernel, (Z, Y, C, X), scaling),
        out_shape=(
            jax.ShapeDtypeStruct((PATCH, F), BF16),
            jax.ShapeDtypeStruct((C, Z, 2, ZR, F), BF16),
        ),
        in_specs=[pl.BlockSpec(memory_space=pltpu.SMEM)] * 2
        + [pl.BlockSpec(memory_space=pl.ANY)] * 6,
        out_specs=(in_vmem, in_vmem),
        scratch_shapes=scratch,
        compiler_params=pltpu.CompilerParams(
            collective_id=0, has_side_effects=True, vmem_limit_bytes=62 * 1024 * 1024
        ),
    )(
        block_source,
        block_live,
        grid_latent,
        mesh_latent,
        edge_weight,
        mlp_first,
        mlp_second,
        mesh_cotangent,
    )
    return pl.pallas_call(
        hand_out,
        out_shape=(
            jax.ShapeDtypeStruct((PATCH, F), BF16),
            jax.ShapeDtypeStruct((D, F), F32),
            jax.ShapeDtypeStruct((H, F), F32),
        ),
        in_specs=[in_vmem] * 2,
        out_specs=(in_vmem, in_vmem, in_vmem),
    )(mesh_sum, sums)


def torus_of(mesh):
    return Mesh(mesh.devices.reshape(8, 4, 2, mesh.shape["mp"]), AXES)


def solution(mesh):
    torus = torus_of(mesh)
    in_specs = (
        P(PATCH_AXES, None),
        P(PATCH_AXES, "mp"),
        P(PATCH_AXES, None, None),
        P(PATCH_AXES),
        P(PATCH_AXES),
        P(),
        P(None, "mp"),
        P(PATCH_AXES, "mp"),
    )
    out_specs = (P(PATCH_AXES, "mp"), P(None, "mp"), P(None, "mp"))
    return jax.shard_map(
        per_device, mesh=torus, in_specs=in_specs, out_specs=out_specs, check_vma=False
    )
```

```python
import functools
import math

import jax
import jax.numpy as jnp
from jax import lax
from jax.experimental import pallas as pl
from jax.experimental.pallas import tpu as pltpu
from jax.sharding import Mesh
from jax.sharding import PartitionSpec as P

PATCH = 128
PATCH_AXES = ("patch_0", "patch_1", "patch_2")
AXES = PATCH_AXES + ("mp",)
F32 = jnp.float32
BF16 = jnp.bfloat16


def dot(a, b, dims=((1,), (0,))):
    return lax.dot_general(a, b, (dims, ((), ())), preferred_element_type=F32)


def kernel(
    sizes,
    scaling,
    source_ref,
    live_ref,
    grid_in,
    latent_in,
    w_in,
    first_in,
    second_in,
    cot_in,
    mesh_out,
    fin,
    meta_ref,
    grid_ref,
    latent_ref,
    w_ref,
    first_ref,
    second_ref,
    cot_ref,
    slots,
    V,
    cotb,
    metab,
    second,
    slope,
    hidden,
    msg,
    vbig,
    vbig_t,
    c_own,
    c_sum,
    c_send,
    c_recv,
    y_send,
    y_recv,
    y_own,
    z_send,
    z_recv,
    x_send,
    x_recv,
    gm_sum,
    gm,
    gpre,
    gc_send,
    gc_recv,
    g_own,
    gx_send,
    gx_recv,
    gz_send,
    gz_recv,
    gy,
    own,
    w_s,
    w_r,
    sec_s,
    sec_r,
    cx_s,
    cx_r,
    cz_s,
    cz_r,
    ch_r,
    cy_s,
    cy_r,
    cc_s,
    cc_r,
    mz_s,
    mz_r,
    my_s,
    my_r,
    fc_s,
    fc_r,
    fy_s,
    fy_r,
    fz_s,
    fz_r,
    fx_s,
    fx_r,
    gc_s,
    gc_r,
    gx_s,
    gx_r,
    gz_s,
    gz_r,
    gy_s,
    gy_r,
    az_s,
    az_r,
    ac_s,
    ac_r,
    loc,
    load_s,
):
    Z, Y, C, X = sizes
    NP = Z * Y * C
    R, D = grid_in.shape
    H = first_in.shape[1]
    F = second_in.shape[1]
    PX = PATCH // X
    GPD = R // PATCH
    HC = D // 2
    z, y, c, x = (lax.axis_index(a) for a in AXES)
    oc = 1 - c
    sent = []

    def send(src, dst, ss, rs, **where):
        place = {"patch_0": z, "patch_1": y, "patch_2": c, "mp": x}
        place.update(where)
        copy = pltpu.make_async_remote_copy(
            src_ref=src,
            dst_ref=dst,
            send_sem=ss,
            recv_sem=rs,
            device_id=place,
            device_id_type=pl.DeviceIdType.MESH,
        )
        copy.start()
        sent.append((src, dst, ss, rs))

    def arrive(dst, rs):
        pltpu.make_async_copy(dst, dst, rs).wait()

    def step(i, k, n):
        return lax.rem(i + k, n)

    xf = pl.ds(pl.multiple_of(x * F, F), F)
    xp = pl.ds(pl.multiple_of(x * PX, PX), PX)

    loads = {}
    for i, (name, src, dst) in enumerate(
        (
            ("cot", cot_in, cot_ref),
            ("w", w_in, w_ref),
            ("second", second_in, second_ref),
            ("grid", grid_in, grid_ref),
            ("first", first_in, first_ref),
            ("latent", latent_in, latent_ref),
        )
    ):
        loads[name] = pltpu.make_async_copy(src, dst, load_s.at[i])
        loads[name].start()

    barrier = pltpu.get_barrier_semaphore()

    def greet(j, carry):
        dz, dy, dc = j // (Y * 2), (j // 2) % Y, j % 2
        pl.semaphore_signal(
            barrier,
            inc=1,
            device_id={
                "patch_0": lax.rem(z + dz, Z),
                "patch_1": lax.rem(y + dy, Y),
                "patch_2": lax.rem(c + dc, 2),
                "mp": x,
            },
            device_id_type=pl.DeviceIdType.MESH,
        )
        return carry

    def greet_mp(j, carry):
        pl.semaphore_signal(
            barrier,
            inc=1,
            device_id={
                "patch_0": lax.rem(z + j % Z, Z),
                "patch_1": y,
                "patch_2": c,
                "mp": lax.rem(x + j // Z, X),
            },
            device_id_type=pl.DeviceIdType.MESH,
        )
        return carry

    lax.fori_loop(1, NP, greet, 0)
    lax.fori_loop(Z, X * Z, greet_mp, 0)

    n_slots = w_in.shape[0]

    def feeder(j):
        return jnp.where(live_ref[j] == 1, lax.div(source_ref[j], GPD), -1)

    lane = lax.broadcasted_iota(jnp.int32, (1, PATCH), 1)
    meta = jnp.zeros((1, PATCH), F32)
    for j in range(n_slots):
        inside = lax.rem(source_ref[j], GPD).astype(F32)
        meta = jnp.where(lane == feeder(j), inside, meta)
    meta_ref[...] = meta
    loads["w"].wait()

    def pack(i, carry):
        z1, c1, y1 = i // (2 * Y), (i // Y) % 2, i % Y
        natural = (z1 * Y + y1) * 2 + c1
        slot, live = jnp.int32(0), jnp.int32(0)
        for j in range(n_slots):
            hit = feeder(j) == natural
            slot = jnp.where(hit, j, slot)
            live = jnp.where(hit, 1, live)
        block = w_ref[slot, xp, :]
        slots[i] = (block.astype(F32) * live.astype(F32)).astype(BF16)
        return carry

    lax.fori_loop(0, NP, pack, 0)
    loads["cot"].wait()
    loads["second"].wait()
    own_cot = pltpu.make_async_copy(cot_ref.at[xp, :], cotb.at[z, c, y, :, xf], loc.at[0])
    own_cot.start()
    half = pl.ds(pl.multiple_of(c * (H // 2), H // 2), H // 2)
    other_half = pl.ds(pl.multiple_of(oc * (H // 2), H // 2), H // 2)
    own_second = pltpu.make_async_copy(second_ref.at[half], second.at[half, xf], loc.at[1])
    own_second.start()
    own_meta = pltpu.make_async_copy(meta_ref, metab.at[z, c, y], loc.at[2])
    own_meta.start()
    here = (z * 2 + c) * Y + y
    own_slot = pltpu.make_async_copy(slots.at[here], V.at[here], loc.at[3])
    own_slot.start()
    pl.semaphore_wait(barrier, NP - 1 + (X - 1) * Z)

    own_meta.wait()
    near = [0]
    for t in range(1, Z // 2 + 1):
        near += [t, Z - t] if 2 * t < Z else [t]
    for k in near[1:]:
        send(
            metab.at[z, c, y],
            metab.at[z, c, y],
            mz_s.at[k - 1],
            mz_r.at[k - 1],
            patch_0=step(z, k, Z),
        )
    relayed = (3, 4, 5) if Z == 8 else ()
    for k in near:
        for m in range(X):
            if k not in relayed and (k or m):
                to = step(x, m, X)
                rows = pl.ds(pl.multiple_of(to * PX, PX), PX)
                send(
                    cot_ref.at[rows, :],
                    cotb.at[z, c, y, :, xf],
                    cz_s.at[k, m],
                    cz_r.at[k],
                    patch_0=step(z, k, Z),
                    mp=to,
                )
    for k in range(1, X):
        to = step(x, k, X)
        send(
            second_ref.at[half], second.at[half, xf], sec_s.at[k - 1], sec_r.at[k - 1], mp=to
        )

    def send_slot(j, carry):
        dz, dy, dc = j // (Y * 2), (j // 2) % Y, j % 2
        z1, y1, c1 = lax.rem(z + dz, Z), lax.rem(y + dy, Y), lax.rem(c + dc, 2)
        pltpu.make_async_remote_copy(
            src_ref=slots.at[(z1 * 2 + c1) * Y + y1],
            dst_ref=V.at[here],
            send_sem=w_s,
            recv_sem=w_r.at[z],
            device_id={"patch_0": z1, "patch_1": y1, "patch_2": c1, "mp": x},
            device_id_type=pl.DeviceIdType.MESH,
        ).start()
        return carry

    for dz in near:
        lax.fori_loop(max(1, dz * Y * 2), (dz + 1) * Y * 2, send_slot, 0)

    TR = 2 * PATCH
    T = R // TR

    def first_layer(i):
        rows = pl.ds(i * TR, TR)
        pre = dot(grid_ref[rows, :], first_ref[...])
        s = jax.nn.sigmoid(pre)
        hidden[rows, :] = (pre * s).astype(BF16)
        slope[rows, :] = s * (1.0 + pre * (1.0 - s))

    def second_layer(i):
        rows = pl.ds(i * TR, TR)
        msg[rows, :] = dot(hidden[rows, :], second[...]).astype(BF16)

    def over_y(k):
        at = step(z, (Z - k) % Z, Z)
        halves_of = [cotb.at[at, c, y, pl.ds(h * (PX // 2), PX // 2)] for h in range(2)]
        if relayed and k == 4:
            for h in range(2):
                arrive(halves_of[h], ch_r.at[h])
        elif k:
            arrive(cotb.at[at, c, y], cz_r.at[k])
        else:
            own_cot.wait()
            arrive(cotb.at[at, c, y, :, pl.ds(0, (X - 1) * F)], cz_r.at[k])
        block = cotb.at[at, c, y]
        if relayed and k in (2, Z - 2):
            h, far, one, two = (0, 3, 1, 2) if k == 2 else (1, 5, Z - 1, Z - 2)
            send(block, block, cz_s.at[far, 0], cz_r.at[far], patch_0=step(z, one, Z))
            send(halves_of[h], halves_of[h], cz_s.at[far, 1], ch_r.at[h], patch_0=step(z, two, Z))
        for m in range(1, Y):
            send(block, block, cy_s.at[m - 1, k], cy_r.at[m - 1, k], patch_1=step(y, m, Y))

    loads["grid"].wait()
    loads["first"].wait()
    per = -(-Z // T)
    for i in range(T):
        first_layer(i)
        for k in near[i * per : (i + 1) * per]:
            over_y(k)
        if i == 0:
            for k in range(1, Z):
                arrive(metab.at[step(z, Z - k, Z), c, y], mz_r.at[k - 1])
            for j in range(1, 2 * Y):
                send(
                    metab.at[:, c, y],
                    metab.at[:, c, y],
                    my_s.at[j],
                    my_r.at[j],
                    patch_1=step(y, j // 2, Y),
                    patch_2=lax.rem(c + j % 2, 2),
                )
    own_second.wait()
    for k in range(1, X):
        frm = step(x, X - k, X)
        arrive(second.at[half, pl.ds(pl.multiple_of(frm * F, F), F)], sec_r.at[k - 1])
    send(second.at[half], second.at[half], sec_s.at[X - 1], sec_r.at[X - 1], patch_2=oc)
    arrive(second.at[other_half], sec_r.at[X - 1])
    for i in range(T):
        second_layer(i)
    for j in range(1, 2 * Y):
        core, yy = lax.rem(c + j % 2, 2), step(y, Y - j // 2, Y)
        arrive(metab.at[:, core, yy], my_r.at[j])

    own_natural = (z * Y + y) * 2 + c
    PL = C * Y
    TP = PL * PX
    lanes = lax.broadcasted_iota(jnp.int32, (PL, PATCH), 1)
    of_receiver = lax.broadcasted_iota(jnp.int32, (PL, TP), 1) // PX == lax.broadcasted_iota(
        jnp.int32, (PL, TP), 0
    )

    def plane(k):
        return step(z, (Z - k) % Z, Z)

    def spread(at, slot):
        meta = metab[at].reshape(PL, PATCH)
        patch_of = jnp.sum(jnp.where(lanes == own_natural, meta, 0.0), axis=1, keepdims=True)
        patch_rows = jnp.broadcast_to(jnp.broadcast_to(patch_of, (PL, PATCH))[:, None], (PL, 8, PATCH))
        patch_cols = jnp.sum(
            jnp.where(of_receiver, jnp.broadcast_to(patch_of, (PL, TP)), 0.0),
            axis=0,
            keepdims=True,
        )
        blocks = V[pl.ds(pl.multiple_of(at * PL, PL), PL)].reshape(TP, PATCH).astype(F32)
        blocks_t = blocks.T
        tiles = blocks.reshape(PL, PX // 8, 8, PATCH)
        for g in range(GPD):
            in_rows = jnp.where(patch_rows == float(g), 1.0, 0.0)
            vbig[:, g * PATCH : (g + 1) * PATCH] = (
                (tiles * in_rows[:, None]).reshape(TP, PATCH).astype(BF16)
            )
            in_cols = jnp.where(patch_cols == float(g), 1.0, 0.0)
            vbig_t[slot, g * PATCH : (g + 1) * PATCH, :] = (blocks_t * in_cols).astype(BF16)

    def contribute(i, k):
        at, slot = plane(k), i % 2
        arrive(V.at[pl.ds(0, PL if k else PL - 1)], w_r.at[at])
        spread(at, slot)
        c_own[slot] = dot(vbig[...], msg[...]).reshape(C, Y, PX, D)
        c_send[at] = c_own[slot, oc].astype(BF16)
        send(c_send.at[at], c_recv.at[at], fc_s.at[k], fc_r.at[k], patch_2=oc)
        for m in range(1, Y):
            arrive(cotb.at[at, c, step(y, Y - m, Y)], cy_r.at[m - 1, k])
        send(cotb.at[at, c], cotb.at[at, c], cc_s.at[k], cc_r.at[k], patch_2=oc)

    def collect(i, k):
        at, slot = plane(k), i % 2
        arrive(c_recv.at[at], fc_r.at[k])
        c_sum[...] = c_own[slot, c] + c_recv[at].astype(F32)
        y_own[at] = c_sum[y]
        for m in range(1, Y):
            to = step(y, m, Y)
            y_send[m - 1, at] = c_sum[to].astype(BF16)
            send(
                y_send.at[m - 1, at],
                y_recv.at[m - 1, at],
                fy_s.at[m - 1, k],
                fy_r.at[m - 1, k],
                patch_1=to,
            )
        arrive(cotb.at[at, oc], cc_r.at[k])
        for t in range(T):
            rows = slice(t * TR, (t + 1) * TR)
            part = dot(vbig_t[slot, rows, :], cotb[at].reshape(TP, D))
            if i == 0:
                gm_sum[rows, :] = part
            elif i < Z - 1:
                gm_sum[rows, :] += part
            else:
                gm[rows, :] = (gm_sum[rows, :] + part).astype(BF16)

    own_slot.wait()
    for i, k in enumerate(near):
        contribute(i, k)
        if i:
            collect(i - 1, near[i - 1])
    collect(Z - 1, near[-1])

    def halves(which, left_ref, right_ref):
        for core in (oc, c):
            cols = pl.ds(pl.multiple_of(core * HC, HC), HC)
            part = dot(left_ref[:, cols], right_ref[...], ((0,), (0,))) * scaling
            for q in range(X):
                piece = part[:, q * F : (q + 1) * F]
                if core is oc:
                    gc_send[which, q] = piece
                else:
                    g_own[which, q] = piece
            if core is oc:
                send(
                    gc_send.at[which],
                    gc_recv.at[which],
                    gc_s.at[which],
                    gc_r.at[which],
                    patch_2=oc,
                )

    def over_mp(which):
        arrive(gc_recv.at[which], gc_r.at[which])
        for k in range(1, X):
            to = step(x, k, X)
            gx_send[which, k - 1] = (g_own[which, to] + gc_recv[which, to]).astype(BF16)
            send(
                gx_send.at[which, k - 1],
                gx_recv.at[which, k - 1],
                gx_s.at[which, k - 1],
                gx_r.at[which, k - 1],
                mp=to,
            )
        g_own[which, x] = g_own[which, x] + gc_recv[which, x]

    halves(0, hidden, gm)

    def pre_gradient(i, carry):
        rows = pl.ds(pl.multiple_of(i * TR, TR), TR)
        back = dot(gm[rows, :], second[...], ((1,), (1,)))
        gpre[rows, :] = (back * slope[rows, :]).astype(BF16)
        return carry

    lax.fori_loop(0, R // TR, pre_gradient, 0)
    over_mp(0)

    halves(1, grid_ref, gpre)

    over_mp(1)

    for k in near:
        at = plane(k)
        total = y_own[at]
        for m in range(1, Y):
            arrive(y_recv.at[m - 1, at], fy_r.at[m - 1, k])
            total = total + y_recv[m - 1, at].astype(F32)
        if k:
            z_send[at] = total.astype(BF16)
            send(z_send.at[at], z_recv.at[k - 1], fz_s.at[k - 1], fz_r.at[k - 1], patch_0=at)
        else:
            y_own[at] = total

    ZR = HC // Z
    for which in range(2):
        total = g_own[which, x]
        for k in range(1, X):
            arrive(gx_recv.at[which, k - 1], gx_r.at[which, k - 1])
            total = total + gx_recv[which, k - 1].astype(F32)
        g_own[which, x] = total
        gz_send[:, which] = total.reshape(Z, ZR, F).astype(BF16)
    for k in range(1, Z):
        to = step(z, k, Z)
        send(gz_send.at[to], gz_recv.at[k - 1], gz_s.at[k - 1], gz_r.at[k - 1], patch_0=to)

    total = g_own[:, x, pl.ds(pl.multiple_of(z * ZR, ZR), ZR)]
    for k in range(1, Z):
        arrive(gz_recv.at[k - 1], gz_r.at[k - 1])
        total = total + gz_recv[k - 1].astype(F32)
    gy[y] = total
    for k in range(1, Y):
        to = step(y, k, Y)
        send(gy.at[y], gy.at[y], gy_s.at[k - 1], gy_r.at[k - 1], patch_1=to)

    for k in range(1, Y):
        arrive(gy.at[step(y, Y - k, Y)], gy_r.at[k - 1])
    total = gy[0]
    for yy in range(1, Y):
        total = total + gy[yy]
    own[...] = total.astype(BF16)
    for k in range(1, Z):
        to = step(z, k, Z)
        send(own, fin.at[c, z], az_s.at[k - 1], az_r.at[k - 1], patch_0=to)
    fin[c, z] = own[...]

    total = y_own[z]
    for k in range(1, Z):
        arrive(z_recv.at[k - 1], fz_r.at[k - 1])
        total = total + z_recv[k - 1].astype(F32)
    for q in range(X):
        x_send[q] = total[:, q * F : (q + 1) * F]
    own_sum = pltpu.make_async_copy(x_send.at[x], x_recv.at[x], loc.at[0])
    own_sum.start()
    for k in range(1, X):
        to = step(x, k, X)
        send(x_send.at[to], x_recv.at[x], fx_s.at[k - 1], fx_r.at[k - 1], mp=to)

    for k in range(1, Z):
        arrive(fin.at[c, step(z, Z - k, Z)], az_r.at[k - 1])
    send(fin.at[c], fin.at[c], ac_s.at[0], ac_r.at[0], patch_2=oc)
    own_sum.wait()
    for k in range(1, X):
        arrive(x_recv.at[step(x, X - k, X)], fx_r.at[k - 1])
    loads["latent"].wait()
    mesh_out[...] = (latent_ref[...].astype(F32) + x_recv[...].reshape(PATCH, F)).astype(BF16)
    arrive(fin.at[oc], ac_r.at[0])
    pltpu.make_async_remote_copy(
        src_ref=all_but_one(slots, NP),
        dst_ref=all_but_one(V, NP),
        send_sem=w_s,
        recv_sem=w_r.at[0],
        device_id={"patch_0": z, "patch_1": y, "patch_2": oc, "mp": x},
        device_id_type=pl.DeviceIdType.MESH,
    ).wait_send()
    for src, dst, ss, rs in sent:
        pltpu.make_async_copy(src, src, ss).wait()


def hand_out(mesh_sum, sums, mesh_out, first_out, second_out):
    mesh_out[...] = mesh_sum[...]
    second_out[...] = sums[:, :, 0].reshape(second_out.shape).astype(F32)
    first_out[...] = sums[:, :, 1].reshape(first_out.shape).astype(F32)


def all_but_one(ref, n):
    return ref.at[pl.ds(0, n - 1)]


def per_device(
    grid_latent,
    mesh_latent,
    edge_weight,
    block_source,
    block_live,
    mlp_first,
    mlp_second,
    mesh_cotangent,
):
    Z, Y, C = (lax.axis_size(a) for a in PATCH_AXES)
    X = lax.axis_size("mp")
    NP = Z * Y * C
    R, D = grid_latent.shape
    H = mlp_first.shape[1]
    F = mlp_second.shape[1]
    PX = PATCH // X
    GPD = R // PATCH
    HC = D // 2
    ZR = HC // Z
    scaling = 1.0 / math.sqrt(R * NP)

    vm = pltpu.VMEM
    dma = pltpu.SemaphoreType.DMA
    scratch = [
        vm((1, PATCH), F32),
        vm(grid_latent.shape, BF16),
        vm(mesh_latent.shape, BF16),
        vm(edge_weight.shape, BF16),
        vm(mlp_first.shape, BF16),
        vm(mlp_second.shape, BF16),
        vm(mesh_cotangent.shape, BF16),
        vm((NP, PX, PATCH), BF16),
        vm((NP, PX, PATCH), BF16),
        vm((Z, C, Y, PX, D), BF16),
        vm((Z, C, Y, 1, PATCH), F32),
        vm((H, D), BF16),
        vm((R, H), F32),
        vm((R, H), BF16),
        vm((R, D), BF16),
        vm((C * Y * PX, R), BF16),
        vm((2, R, C * Y * PX), BF16),
        vm((2, C, Y, PX, D), F32),
        vm((Y, PX, D), F32),
        vm((Z, Y, PX, D), BF16),
        vm((Z, Y, PX, D), BF16),
        vm((Y - 1, Z, PX, D), BF16),
        vm((Y - 1, Z, PX, D), BF16),
        vm((Z, PX, D), F32),
        vm((Z, PX, D), BF16),
        vm((Z - 1, PX, D), BF16),
        vm((X, PX, F), F32),
        vm((X, PX, F), F32),
        vm((R, D), F32),
        vm((R, D), BF16),
        vm((R, H), BF16),
        vm((2, X, HC, F), F32),
        vm((2, X, HC, F), F32),
        vm((2, X, HC, F), F32),
        vm((2, X - 1, HC, F), BF16),
        vm((2, X - 1, HC, F), BF16),
        vm((Z, 2, ZR, F), BF16),
        vm((Z - 1, 2, ZR, F), BF16),
        vm((Y, 2, ZR, F), F32),
        vm((2, ZR, F), BF16),
        dma,
        dma((Z,)),
        dma((X,)),
        dma((X,)),
        dma((X - 1,)),
        dma((X - 1,)),
        dma((Z, X)),
        dma((Z,)),
        dma((2,)),
        dma((Y - 1, Z)),
        dma((Y - 1, Z)),
        dma((Z,)),
        dma((Z,)),
        dma((Z - 1,)),
        dma((Z - 1,)),
        dma((2 * Y,)),
        dma((2 * Y,)),
        dma((Z,)),
        dma((Z,)),
        dma((Y - 1, Z)),
        dma((Y - 1, Z)),
        dma((Z - 1,)),
        dma((Z - 1,)),
        dma((X - 1,)),
        dma((X - 1,)),
        dma((2,)),
        dma((2,)),
        dma((2, X - 1)),
        dma((2, X - 1)),
        dma((Z - 1,)),
        dma((Z - 1,)),
        dma((Y - 1,)),
        dma((Y - 1,)),
        dma((Z - 1,)),
        dma((Z - 1,)),
        dma((1,)),
        dma((1,)),
        dma((4,)),
        dma((6,)),
    ]
    in_vmem = pl.BlockSpec(memory_space=pltpu.VMEM)
    mesh_sum, sums = pl.pallas_call(
        functools.partial(kernel, (Z, Y, C, X), scaling),
        out_shape=(
            jax.ShapeDtypeStruct((PATCH, F), BF16),
            jax.ShapeDtypeStruct((C, Z, 2, ZR, F), BF16),
        ),
        in_specs=[pl.BlockSpec(memory_space=pltpu.SMEM)] * 2
        + [pl.BlockSpec(memory_space=pl.ANY)] * 6,
        out_specs=(in_vmem, in_vmem),
        scratch_shapes=scratch,
        compiler_params=pltpu.CompilerParams(
            collective_id=0, has_side_effects=True, vmem_limit_bytes=62 * 1024 * 1024
        ),
    )(
        block_source,
        block_live,
        grid_latent,
        mesh_latent,
        edge_weight,
        mlp_first,
        mlp_second,
        mesh_cotangent,
    )
    return pl.pallas_call(
        hand_out,
        out_shape=(
            jax.ShapeDtypeStruct((PATCH, F), BF16),
            jax.ShapeDtypeStruct((D, F), F32),
            jax.ShapeDtypeStruct((H, F), F32),
        ),
        in_specs=[in_vmem] * 2,
        out_specs=(in_vmem, in_vmem, in_vmem),
    )(mesh_sum, sums)


def torus_of(mesh):
    return Mesh(mesh.devices.reshape(8, 4, 2, mesh.shape["mp"]), AXES)


def solution(mesh):
    torus = torus_of(mesh)
    in_specs = (
        P(PATCH_AXES, None),
        P(PATCH_AXES, "mp"),
        P(PATCH_AXES, None, None),
        P(PATCH_AXES),
        P(PATCH_AXES),
        P(),
        P(None, "mp"),
        P(PATCH_AXES, "mp"),
    )
    out_specs = (P(PATCH_AXES, "mp"), P(None, "mp"), P(None, "mp"))
    return jax.shard_map(
        per_device, mesh=torus, in_specs=in_specs, out_specs=out_specs, check_vma=False
    )
```

```python
import functools
import math

import jax
import jax.numpy as jnp
from jax import lax
from jax.experimental import pallas as pl
from jax.experimental.pallas import tpu as pltpu
from jax.sharding import Mesh
from jax.sharding import PartitionSpec as P

PATCH = 128
PATCH_AXES = ("patch_0", "patch_1", "patch_2")
AXES = PATCH_AXES + ("mp",)
F32 = jnp.float32
BF16 = jnp.bfloat16


def dot(a, b, dims=((1,), (0,))):
    return lax.dot_general(a, b, (dims, ((), ())), preferred_element_type=F32)


def kernel(
    sizes,
    scaling,
    source_ref,
    live_ref,
    grid_in,
    latent_in,
    w_in,
    first_in,
    second_in,
    cot_in,
    mesh_out,
    fin,
    meta_ref,
    grid_ref,
    latent_ref,
    w_ref,
    first_ref,
    second_ref,
    cot_ref,
    slots,
    V,
    cotb,
    metab,
    second,
    slope,
    hidden,
    msg,
    vbig,
    vbig_t,
    c_own,
    c_sum,
    c_send,
    c_recv,
    y_send,
    y_recv,
    y_own,
    z_send,
    z_recv,
    x_send,
    x_recv,
    gm_sum,
    gm,
    gpre,
    gc_send,
    gc_recv,
    g_own,
    gx_send,
    gx_recv,
    gz_send,
    gz_recv,
    gy,
    own,
    w_s,
    w_r,
    sec_s,
    sec_r,
    cx_s,
    cx_r,
    cz_s,
    cz_r,
    cy_s,
    cy_r,
    cc_s,
    cc_r,
    mz_s,
    mz_r,
    my_s,
    my_r,
    fc_s,
    fc_r,
    fy_s,
    fy_r,
    fz_s,
    fz_r,
    fx_s,
    fx_r,
    gc_s,
    gc_r,
    gx_s,
    gx_r,
    gz_s,
    gz_r,
    gy_s,
    gy_r,
    az_s,
    az_r,
    ac_s,
    ac_r,
    loc,
    load_s,
):
    Z, Y, C, X = sizes
    NP = Z * Y * C
    R, D = grid_in.shape
    H = first_in.shape[1]
    F = second_in.shape[1]
    PX = PATCH // X
    GPD = R // PATCH
    HC = D // 2
    z, y, c, x = (lax.axis_index(a) for a in AXES)
    oc = 1 - c
    sent = []

    def send(src, dst, ss, rs, **where):
        place = {"patch_0": z, "patch_1": y, "patch_2": c, "mp": x}
        place.update(where)
        copy = pltpu.make_async_remote_copy(
            src_ref=src,
            dst_ref=dst,
            send_sem=ss,
            recv_sem=rs,
            device_id=place,
            device_id_type=pl.DeviceIdType.MESH,
        )
        copy.start()
        sent.append((src, dst, ss, rs))

    def arrive(dst, rs):
        pltpu.make_async_copy(dst, dst, rs).wait()

    def step(i, k, n):
        return lax.rem(i + k, n)

    xf = pl.ds(pl.multiple_of(x * F, F), F)
    xp = pl.ds(pl.multiple_of(x * PX, PX), PX)

    loads = {}
    for i, (name, src, dst) in enumerate(
        (
            ("cot", cot_in, cot_ref),
            ("w", w_in, w_ref),
            ("second", second_in, second_ref),
            ("grid", grid_in, grid_ref),
            ("first", first_in, first_ref),
            ("latent", latent_in, latent_ref),
        )
    ):
        loads[name] = pltpu.make_async_copy(src, dst, load_s.at[i])
        loads[name].start()

    barrier = pltpu.get_barrier_semaphore()

    def greet(j, carry):
        dz, dy, dc = j // (Y * 2), (j // 2) % Y, j % 2
        pl.semaphore_signal(
            barrier,
            inc=1,
            device_id={
                "patch_0": lax.rem(z + dz, Z),
                "patch_1": lax.rem(y + dy, Y),
                "patch_2": lax.rem(c + dc, 2),
                "mp": x,
            },
            device_id_type=pl.DeviceIdType.MESH,
        )
        return carry

    def greet_mp(j, carry):
        pl.semaphore_signal(
            barrier,
            inc=1,
            device_id={
                "patch_0": lax.rem(z + j % Z, Z),
                "patch_1": y,
                "patch_2": c,
                "mp": lax.rem(x + j // Z, X),
            },
            device_id_type=pl.DeviceIdType.MESH,
        )
        return carry

    lax.fori_loop(1, NP, greet, 0)
    lax.fori_loop(Z, X * Z, greet_mp, 0)

    n_slots = w_in.shape[0]

    def feeder(j):
        return jnp.where(live_ref[j] == 1, lax.div(source_ref[j], GPD), -1)

    lane = lax.broadcasted_iota(jnp.int32, (1, PATCH), 1)
    meta = jnp.zeros((1, PATCH), F32)
    for j in range(n_slots):
        inside = lax.rem(source_ref[j], GPD).astype(F32)
        meta = jnp.where(lane == feeder(j), inside, meta)
    meta_ref[...] = meta
    loads["w"].wait()

    def pack(i, carry):
        z1, c1, y1 = i // (2 * Y), (i // Y) % 2, i % Y
        natural = (z1 * Y + y1) * 2 + c1
        slot, live = jnp.int32(0), jnp.int32(0)
        for j in range(n_slots):
            hit = feeder(j) == natural
            slot = jnp.where(hit, j, slot)
            live = jnp.where(hit, 1, live)
        block = w_ref[slot, xp, :]
        slots[i] = (block.astype(F32) * live.astype(F32)).astype(BF16)
        return carry

    lax.fori_loop(0, NP, pack, 0)
    loads["cot"].wait()
    loads["second"].wait()
    own_cot = pltpu.make_async_copy(cot_ref.at[xp, :], cotb.at[z, c, y, :, xf], loc.at[0])
    own_cot.start()
    half = pl.ds(pl.multiple_of(c * (H // 2), H // 2), H // 2)
    other_half = pl.ds(pl.multiple_of(oc * (H // 2), H // 2), H // 2)
    own_second = pltpu.make_async_copy(second_ref.at[half], second.at[half, xf], loc.at[1])
    own_second.start()
    own_meta = pltpu.make_async_copy(meta_ref, metab.at[z, c, y], loc.at[2])
    own_meta.start()
    here = (z * 2 + c) * Y + y
    own_slot = pltpu.make_async_copy(slots.at[here], V.at[here], loc.at[3])
    own_slot.start()
    pl.semaphore_wait(barrier, NP - 1 + (X - 1) * Z)

    own_meta.wait()
    near = [0]
    for t in range(1, Z // 2 + 1):
        near += [t, Z - t] if 2 * t < Z else [t]
    for k in near[1:]:
        send(
            metab.at[z, c, y],
            metab.at[z, c, y],
            mz_s.at[k - 1],
            mz_r.at[k - 1],
            patch_0=step(z, k, Z),
        )
    for k in near:
        for m in range(X):
            if k or m:
                to = step(x, m, X)
                rows = pl.ds(pl.multiple_of(to * PX, PX), PX)
                send(
                    cot_ref.at[rows, :],
                    cotb.at[z, c, y, :, xf],
                    cz_s.at[k, m],
                    cz_r.at[k],
                    patch_0=step(z, k, Z),
                    mp=to,
                )
    for k in range(1, X):
        to = step(x, k, X)
        send(
            second_ref.at[half], second.at[half, xf], sec_s.at[k - 1], sec_r.at[k - 1], mp=to
        )

    def send_slot(j, carry):
        dz, dy, dc = j // (Y * 2), (j // 2) % Y, j % 2
        z1, y1, c1 = lax.rem(z + dz, Z), lax.rem(y + dy, Y), lax.rem(c + dc, 2)
        pltpu.make_async_remote_copy(
            src_ref=slots.at[(z1 * 2 + c1) * Y + y1],
            dst_ref=V.at[here],
            send_sem=w_s,
            recv_sem=w_r.at[z],
            device_id={"patch_0": z1, "patch_1": y1, "patch_2": c1, "mp": x},
            device_id_type=pl.DeviceIdType.MESH,
        ).start()
        return carry

    def send_planes(planes):
        for dz in planes:
            lax.fori_loop(max(1, dz * Y * 2), (dz + 1) * Y * 2, send_slot, 0)

    TR = 2 * PATCH
    T = R // TR

    def first_layer(i):
        rows = pl.ds(i * TR, TR)
        pre = dot(grid_ref[rows, :], first_ref[...])
        s = jax.nn.sigmoid(pre)
        hidden[rows, :] = (pre * s).astype(BF16)
        slope[rows, :] = s * (1.0 + pre * (1.0 - s))

    def second_layer(i):
        rows = pl.ds(i * TR, TR)
        msg[rows, :] = dot(hidden[rows, :], second[...]).astype(BF16)

    def over_y(k):
        at = step(z, (Z - k) % Z, Z)
        if k:
            arrive(cotb.at[at, c, y], cz_r.at[k])
        else:
            own_cot.wait()
            arrive(cotb.at[at, c, y, :, pl.ds(0, (X - 1) * F)], cz_r.at[k])
        for m in range(1, Y):
            block = cotb.at[at, c, y]
            send(block, block, cy_s.at[m - 1, k], cy_r.at[m - 1, k], patch_1=step(y, m, Y))

    loads["grid"].wait()
    loads["first"].wait()
    per = -(-Z // T)
    send_planes(near[:per])
    for i in range(T):
        first_layer(i)
        for k in near[i * per : (i + 1) * per]:
            over_y(k)
        send_planes(near[(i + 1) * per : (i + 2) * per])
        if i == 0:
            for k in range(1, Z):
                arrive(metab.at[step(z, Z - k, Z), c, y], mz_r.at[k - 1])
            for j in range(1, 2 * Y):
                send(
                    metab.at[:, c, y],
                    metab.at[:, c, y],
                    my_s.at[j],
                    my_r.at[j],
                    patch_1=step(y, j // 2, Y),
                    patch_2=lax.rem(c + j % 2, 2),
                )
    own_second.wait()
    for k in range(1, X):
        frm = step(x, X - k, X)
        arrive(second.at[half, pl.ds(pl.multiple_of(frm * F, F), F)], sec_r.at[k - 1])
    send(second.at[half], second.at[half], sec_s.at[X - 1], sec_r.at[X - 1], patch_2=oc)
    arrive(second.at[other_half], sec_r.at[X - 1])
    for i in range(T):
        second_layer(i)
    for j in range(1, 2 * Y):
        core, yy = lax.rem(c + j % 2, 2), step(y, Y - j // 2, Y)
        arrive(metab.at[:, core, yy], my_r.at[j])

    own_natural = (z * Y + y) * 2 + c
    PL = C * Y
    TP = PL * PX
    lanes = lax.broadcasted_iota(jnp.int32, (PL, PATCH), 1)
    of_receiver = lax.broadcasted_iota(jnp.int32, (PL, TP), 1) // PX == lax.broadcasted_iota(
        jnp.int32, (PL, TP), 0
    )

    def plane(k):
        return step(z, (Z - k) % Z, Z)

    def spread(at, slot):
        meta = metab[at].reshape(PL, PATCH)
        patch_of = jnp.sum(jnp.where(lanes == own_natural, meta, 0.0), axis=1, keepdims=True)
        patch_rows = jnp.broadcast_to(jnp.broadcast_to(patch_of, (PL, PATCH))[:, None], (PL, 8, PATCH))
        patch_cols = jnp.sum(
            jnp.where(of_receiver, jnp.broadcast_to(patch_of, (PL, TP)), 0.0),
            axis=0,
            keepdims=True,
        )
        blocks = V[pl.ds(pl.multiple_of(at * PL, PL), PL)].reshape(TP, PATCH).astype(F32)
        blocks_t = blocks.T
        tiles = blocks.reshape(PL, PX // 8, 8, PATCH)
        for g in range(GPD):
            in_rows = jnp.where(patch_rows == float(g), 1.0, 0.0)
            vbig[:, g * PATCH : (g + 1) * PATCH] = (
                (tiles * in_rows[:, None]).reshape(TP, PATCH).astype(BF16)
            )
            in_cols = jnp.where(patch_cols == float(g), 1.0, 0.0)
            vbig_t[slot, g * PATCH : (g + 1) * PATCH, :] = (blocks_t * in_cols).astype(BF16)

    def contribute(i, k):
        at, slot = plane(k), i % 2
        arrive(V.at[pl.ds(0, PL if k else PL - 1)], w_r.at[at])
        spread(at, slot)
        c_own[slot] = dot(vbig[...], msg[...]).reshape(C, Y, PX, D)
        c_send[at] = c_own[slot, oc].astype(BF16)
        send(c_send.at[at], c_recv.at[at], fc_s.at[k], fc_r.at[k], patch_2=oc)
        for m in range(1, Y):
            arrive(cotb.at[at, c, step(y, Y - m, Y)], cy_r.at[m - 1, k])
        send(cotb.at[at, c], cotb.at[at, c], cc_s.at[k], cc_r.at[k], patch_2=oc)

    def collect(i, k):
        at, slot = plane(k), i % 2
        arrive(c_recv.at[at], fc_r.at[k])
        c_sum[...] = c_own[slot, c] + c_recv[at].astype(F32)
        y_own[at] = c_sum[y]
        for m in range(1, Y):
            to = step(y, m, Y)
            y_send[m - 1, at] = c_sum[to].astype(BF16)
            send(
                y_send.at[m - 1, at],
                y_recv.at[m - 1, at],
                fy_s.at[m - 1, k],
                fy_r.at[m - 1, k],
                patch_1=to,
            )
        arrive(cotb.at[at, oc], cc_r.at[k])
        for t in range(T):
            rows = slice(t * TR, (t + 1) * TR)
            part = dot(vbig_t[slot, rows, :], cotb[at].reshape(TP, D))
            if i == 0:
                gm_sum[rows, :] = part
            elif i < Z - 1:
                gm_sum[rows, :] += part
            else:
                gm[rows, :] = (gm_sum[rows, :] + part).astype(BF16)

    own_slot.wait()
    for i, k in enumerate(near):
        contribute(i, k)
        if i:
            collect(i - 1, near[i - 1])
    collect(Z - 1, near[-1])

    def halves(which, left_ref, right_ref):
        for core in (oc, c):
            cols = pl.ds(pl.multiple_of(core * HC, HC), HC)
            part = dot(left_ref[:, cols], right_ref[...], ((0,), (0,))) * scaling
            for q in range(X):
                piece = part[:, q * F : (q + 1) * F]
                if core is oc:
                    gc_send[which, q] = piece
                else:
                    g_own[which, q] = piece
            if core is oc:
                send(
                    gc_send.at[which],
                    gc_recv.at[which],
                    gc_s.at[which],
                    gc_r.at[which],
                    patch_2=oc,
                )

    def over_mp(which):
        arrive(gc_recv.at[which], gc_r.at[which])
        for k in range(1, X):
            to = step(x, k, X)
            gx_send[which, k - 1] = (g_own[which, to] + gc_recv[which, to]).astype(BF16)
            send(
                gx_send.at[which, k - 1],
                gx_recv.at[which, k - 1],
                gx_s.at[which, k - 1],
                gx_r.at[which, k - 1],
                mp=to,
            )
        g_own[which, x] = g_own[which, x] + gc_recv[which, x]

    halves(0, hidden, gm)

    def pre_gradient(i, carry):
        rows = pl.ds(pl.multiple_of(i * TR, TR), TR)
        back = dot(gm[rows, :], second[...], ((1,), (1,)))
        gpre[rows, :] = (back * slope[rows, :]).astype(BF16)
        return carry

    lax.fori_loop(0, R // TR, pre_gradient, 0)
    over_mp(0)

    halves(1, grid_ref, gpre)

    over_mp(1)

    for k in near:
        at = plane(k)
        total = y_own[at]
        for m in range(1, Y):
            arrive(y_recv.at[m - 1, at], fy_r.at[m - 1, k])
            total = total + y_recv[m - 1, at].astype(F32)
        if k:
            z_send[at] = total.astype(BF16)
            send(z_send.at[at], z_recv.at[k - 1], fz_s.at[k - 1], fz_r.at[k - 1], patch_0=at)
        else:
            y_own[at] = total

    ZR = HC // Z
    for which in range(2):
        total = g_own[which, x]
        for k in range(1, X):
            arrive(gx_recv.at[which, k - 1], gx_r.at[which, k - 1])
            total = total + gx_recv[which, k - 1].astype(F32)
        g_own[which, x] = total
        gz_send[:, which] = total.reshape(Z, ZR, F).astype(BF16)
    for k in range(1, Z):
        to = step(z, k, Z)
        send(gz_send.at[to], gz_recv.at[k - 1], gz_s.at[k - 1], gz_r.at[k - 1], patch_0=to)

    total = g_own[:, x, pl.ds(pl.multiple_of(z * ZR, ZR), ZR)]
    for k in range(1, Z):
        arrive(gz_recv.at[k - 1], gz_r.at[k - 1])
        total = total + gz_recv[k - 1].astype(F32)
    gy[y] = total
    for k in range(1, Y):
        to = step(y, k, Y)
        send(gy.at[y], gy.at[y], gy_s.at[k - 1], gy_r.at[k - 1], patch_1=to)

    for k in range(1, Y):
        arrive(gy.at[step(y, Y - k, Y)], gy_r.at[k - 1])
    total = gy[0]
    for yy in range(1, Y):
        total = total + gy[yy]
    own[...] = total.astype(BF16)
    for k in range(1, Z):
        to = step(z, k, Z)
        send(own, fin.at[c, z], az_s.at[k - 1], az_r.at[k - 1], patch_0=to)
    fin[c, z] = own[...]

    total = y_own[z]
    for k in range(1, Z):
        arrive(z_recv.at[k - 1], fz_r.at[k - 1])
        total = total + z_recv[k - 1].astype(F32)
    for q in range(X):
        x_send[q] = total[:, q * F : (q + 1) * F]
    own_sum = pltpu.make_async_copy(x_send.at[x], x_recv.at[x], loc.at[0])
    own_sum.start()
    for k in range(1, X):
        to = step(x, k, X)
        send(x_send.at[to], x_recv.at[x], fx_s.at[k - 1], fx_r.at[k - 1], mp=to)

    for k in range(1, Z):
        arrive(fin.at[c, step(z, Z - k, Z)], az_r.at[k - 1])
    send(fin.at[c], fin.at[c], ac_s.at[0], ac_r.at[0], patch_2=oc)
    own_sum.wait()
    for k in range(1, X):
        arrive(x_recv.at[step(x, X - k, X)], fx_r.at[k - 1])
    loads["latent"].wait()
    mesh_out[...] = (latent_ref[...].astype(F32) + x_recv[...].reshape(PATCH, F)).astype(BF16)
    arrive(fin.at[oc], ac_r.at[0])
    pltpu.make_async_remote_copy(
        src_ref=all_but_one(slots, NP),
        dst_ref=all_but_one(V, NP),
        send_sem=w_s,
        recv_sem=w_r.at[0],
        device_id={"patch_0": z, "patch_1": y, "patch_2": oc, "mp": x},
        device_id_type=pl.DeviceIdType.MESH,
    ).wait_send()
    for src, dst, ss, rs in sent:
        pltpu.make_async_copy(src, src, ss).wait()


def hand_out(mesh_sum, sums, mesh_out, first_out, second_out):
    mesh_out[...] = mesh_sum[...]
    second_out[...] = sums[:, :, 0].reshape(second_out.shape).astype(F32)
    first_out[...] = sums[:, :, 1].reshape(first_out.shape).astype(F32)


def all_but_one(ref, n):
    return ref.at[pl.ds(0, n - 1)]


def per_device(
    grid_latent,
    mesh_latent,
    edge_weight,
    block_source,
    block_live,
    mlp_first,
    mlp_second,
    mesh_cotangent,
):
    Z, Y, C = (lax.axis_size(a) for a in PATCH_AXES)
    X = lax.axis_size("mp")
    NP = Z * Y * C
    R, D = grid_latent.shape
    H = mlp_first.shape[1]
    F = mlp_second.shape[1]
    PX = PATCH // X
    GPD = R // PATCH
    HC = D // 2
    ZR = HC // Z
    scaling = 1.0 / math.sqrt(R * NP)

    vm = pltpu.VMEM
    dma = pltpu.SemaphoreType.DMA
    scratch = [
        vm((1, PATCH), F32),
        vm(grid_latent.shape, BF16),
        vm(mesh_latent.shape, BF16),
        vm(edge_weight.shape, BF16),
        vm(mlp_first.shape, BF16),
        vm(mlp_second.shape, BF16),
        vm(mesh_cotangent.shape, BF16),
        vm((NP, PX, PATCH), BF16),
        vm((NP, PX, PATCH), BF16),
        vm((Z, C, Y, PX, D), BF16),
        vm((Z, C, Y, 1, PATCH), F32),
        vm((H, D), BF16),
        vm((R, H), F32),
        vm((R, H), BF16),
        vm((R, D), BF16),
        vm((C * Y * PX, R), BF16),
        vm((2, R, C * Y * PX), BF16),
        vm((2, C, Y, PX, D), F32),
        vm((Y, PX, D), F32),
        vm((Z, Y, PX, D), BF16),
        vm((Z, Y, PX, D), BF16),
        vm((Y - 1, Z, PX, D), BF16),
        vm((Y - 1, Z, PX, D), BF16),
        vm((Z, PX, D), F32),
        vm((Z, PX, D), BF16),
        vm((Z - 1, PX, D), BF16),
        vm((X, PX, F), F32),
        vm((X, PX, F), F32),
        vm((R, D), F32),
        vm((R, D), BF16),
        vm((R, H), BF16),
        vm((2, X, HC, F), F32),
        vm((2, X, HC, F), F32),
        vm((2, X, HC, F), F32),
        vm((2, X - 1, HC, F), BF16),
        vm((2, X - 1, HC, F), BF16),
        vm((Z, 2, ZR, F), BF16),
        vm((Z - 1, 2, ZR, F), BF16),
        vm((Y, 2, ZR, F), F32),
        vm((2, ZR, F), BF16),
        dma,
        dma((Z,)),
        dma((X,)),
        dma((X,)),
        dma((X - 1,)),
        dma((X - 1,)),
        dma((Z, X)),
        dma((Z,)),
        dma((Y - 1, Z)),
        dma((Y - 1, Z)),
        dma((Z,)),
        dma((Z,)),
        dma((Z - 1,)),
        dma((Z - 1,)),
        dma((2 * Y,)),
        dma((2 * Y,)),
        dma((Z,)),
        dma((Z,)),
        dma((Y - 1, Z)),
        dma((Y - 1, Z)),
        dma((Z - 1,)),
        dma((Z - 1,)),
        dma((X - 1,)),
        dma((X - 1,)),
        dma((2,)),
        dma((2,)),
        dma((2, X - 1)),
        dma((2, X - 1)),
        dma((Z - 1,)),
        dma((Z - 1,)),
        dma((Y - 1,)),
        dma((Y - 1,)),
        dma((Z - 1,)),
        dma((Z - 1,)),
        dma((1,)),
        dma((1,)),
        dma((4,)),
        dma((6,)),
    ]
    in_vmem = pl.BlockSpec(memory_space=pltpu.VMEM)
    mesh_sum, sums = pl.pallas_call(
        functools.partial(kernel, (Z, Y, C, X), scaling),
        out_shape=(
            jax.ShapeDtypeStruct((PATCH, F), BF16),
            jax.ShapeDtypeStruct((C, Z, 2, ZR, F), BF16),
        ),
        in_specs=[pl.BlockSpec(memory_space=pltpu.SMEM)] * 2
        + [pl.BlockSpec(memory_space=pl.ANY)] * 6,
        out_specs=(in_vmem, in_vmem),
        scratch_shapes=scratch,
        compiler_params=pltpu.CompilerParams(
            collective_id=0, has_side_effects=True, vmem_limit_bytes=62 * 1024 * 1024
        ),
    )(
        block_source,
        block_live,
        grid_latent,
        mesh_latent,
        edge_weight,
        mlp_first,
        mlp_second,
        mesh_cotangent,
    )
    return pl.pallas_call(
        hand_out,
        out_shape=(
            jax.ShapeDtypeStruct((PATCH, F), BF16),
            jax.ShapeDtypeStruct((D, F), F32),
            jax.ShapeDtypeStruct((H, F), F32),
        ),
        in_specs=[in_vmem] * 2,
        out_specs=(in_vmem, in_vmem, in_vmem),
    )(mesh_sum, sums)


def torus_of(mesh):
    return Mesh(mesh.devices.reshape(8, 4, 2, mesh.shape["mp"]), AXES)


def solution(mesh):
    torus = torus_of(mesh)
    in_specs = (
        P(PATCH_AXES, None),
        P(PATCH_AXES, "mp"),
        P(PATCH_AXES, None, None),
        P(PATCH_AXES),
        P(PATCH_AXES),
        P(),
        P(None, "mp"),
        P(PATCH_AXES, "mp"),
    )
    out_specs = (P(PATCH_AXES, "mp"), P(None, "mp"), P(None, "mp"))
    return jax.shard_map(
        per_device, mesh=torus, in_specs=in_specs, out_specs=out_specs, check_vma=False
    )
```

```python
import functools
import math

import jax
import jax.numpy as jnp
from jax import lax
from jax.experimental import pallas as pl
from jax.experimental.pallas import tpu as pltpu
from jax.sharding import Mesh
from jax.sharding import PartitionSpec as P

PATCH = 128
PATCH_AXES = ("patch_0", "patch_1", "patch_2")
AXES = PATCH_AXES + ("mp",)
F32 = jnp.float32
BF16 = jnp.bfloat16


def dot(a, b, dims=((1,), (0,))):
    return lax.dot_general(a, b, (dims, ((), ())), preferred_element_type=F32)


def kernel(
    sizes,
    scaling,
    source_ref,
    live_ref,
    grid_in,
    latent_in,
    w_in,
    first_in,
    second_in,
    cot_in,
    mesh_out,
    fin,
    meta_ref,
    grid_ref,
    latent_ref,
    w_ref,
    first_ref,
    second_ref,
    cot_ref,
    slots,
    V,
    cotb,
    metab,
    second,
    slope,
    hidden,
    msg,
    vbig,
    vbig_t,
    c_own,
    c_sum,
    c_send,
    c_recv,
    y_send,
    y_recv,
    y_own,
    z_send,
    z_recv,
    x_send,
    x_recv,
    gm_sum,
    gm,
    gpre,
    gc_send,
    gc_recv,
    g_own,
    gx_send,
    gx_recv,
    gz_send,
    gz_recv,
    gy,
    own,
    w_s,
    w_r,
    sec_s,
    sec_r,
    cx_s,
    cx_r,
    cz_s,
    cz_r,
    cy_s,
    cy_r,
    cc_s,
    cc_r,
    mz_s,
    mz_r,
    my_s,
    my_r,
    fc_s,
    fc_r,
    fy_s,
    fy_r,
    fz_s,
    fz_r,
    fx_s,
    fx_r,
    gc_s,
    gc_r,
    gx_s,
    gx_r,
    gz_s,
    gz_r,
    gy_s,
    gy_r,
    az_s,
    az_r,
    ac_s,
    ac_r,
    loc,
    load_s,
):
    Z, Y, C, X = sizes
    NP = Z * Y * C
    R, D = grid_in.shape
    H = first_in.shape[1]
    F = second_in.shape[1]
    PX = PATCH // X
    GPD = R // PATCH
    HC = D // 2
    z, y, c, x = (lax.axis_index(a) for a in AXES)
    oc = 1 - c
    sent = []

    def send(src, dst, ss, rs, **where):
        place = {"patch_0": z, "patch_1": y, "patch_2": c, "mp": x}
        place.update(where)
        copy = pltpu.make_async_remote_copy(
            src_ref=src,
            dst_ref=dst,
            send_sem=ss,
            recv_sem=rs,
            device_id=place,
            device_id_type=pl.DeviceIdType.MESH,
        )
        copy.start()
        sent.append((src, dst, ss, rs))

    def arrive(dst, rs):
        pltpu.make_async_copy(dst, dst, rs).wait()

    def step(i, k, n):
        return lax.rem(i + k, n)

    xf = pl.ds(pl.multiple_of(x * F, F), F)
    xp = pl.ds(pl.multiple_of(x * PX, PX), PX)

    loads = {}
    for i, (name, src, dst) in enumerate(
        (
            ("cot", cot_in, cot_ref),
            ("w", w_in, w_ref),
            ("second", second_in, second_ref),
            ("grid", grid_in, grid_ref),
            ("first", first_in, first_ref),
            ("latent", latent_in, latent_ref),
        )
    ):
        loads[name] = pltpu.make_async_copy(src, dst, load_s.at[i])
        loads[name].start()

    barrier = pltpu.get_barrier_semaphore()

    def greet(j, carry):
        dz, dy, dc = j // (Y * 2), (j // 2) % Y, j % 2
        pl.semaphore_signal(
            barrier,
            inc=1,
            device_id={
                "patch_0": lax.rem(z + dz, Z),
                "patch_1": lax.rem(y + dy, Y),
                "patch_2": lax.rem(c + dc, 2),
                "mp": x,
            },
            device_id_type=pl.DeviceIdType.MESH,
        )
        return carry

    def greet_mp(j, carry):
        pl.semaphore_signal(
            barrier,
            inc=1,
            device_id={
                "patch_0": lax.rem(z + j % Z, Z),
                "patch_1": y,
                "patch_2": c,
                "mp": lax.rem(x + j // Z, X),
            },
            device_id_type=pl.DeviceIdType.MESH,
        )
        return carry

    lax.fori_loop(1, NP, greet, 0)
    lax.fori_loop(Z, X * Z, greet_mp, 0)

    n_slots = w_in.shape[0]

    def feeder(j):
        return jnp.where(live_ref[j] == 1, lax.div(source_ref[j], GPD), -1)

    lane = lax.broadcasted_iota(jnp.int32, (1, PATCH), 1)
    meta = jnp.zeros((1, PATCH), F32)
    for j in range(n_slots):
        inside = lax.rem(source_ref[j], GPD).astype(F32)
        meta = jnp.where(lane == feeder(j), inside, meta)
    meta_ref[...] = meta
    loads["w"].wait()

    def pack(i, carry):
        z1, c1, y1 = i // (2 * Y), (i // Y) % 2, i % Y
        natural = (z1 * Y + y1) * 2 + c1
        slot, live = jnp.int32(0), jnp.int32(0)
        for j in range(n_slots):
            hit = feeder(j) == natural
            slot = jnp.where(hit, j, slot)
            live = jnp.where(hit, 1, live)
        block = w_ref[slot, xp, :]
        slots[i] = (block.astype(F32) * live.astype(F32)).astype(BF16)
        return carry

    lax.fori_loop(0, NP, pack, 0)
    loads["cot"].wait()
    loads["second"].wait()
    own_cot = pltpu.make_async_copy(cot_ref.at[xp, :], cotb.at[z, c, y, :, xf], loc.at[0])
    own_cot.start()
    own_second = pltpu.make_async_copy(second_ref, second.at[:, xf], loc.at[1])
    own_second.start()
    own_meta = pltpu.make_async_copy(meta_ref, metab.at[z, c, y], loc.at[2])
    own_meta.start()
    here = (z * 2 + c) * Y + y
    own_slot = pltpu.make_async_copy(slots.at[here], V.at[here], loc.at[3])
    own_slot.start()
    pl.semaphore_wait(barrier, NP - 1 + (X - 1) * Z)

    own_meta.wait()
    near = [0]
    for t in range(1, Z // 2 + 1):
        near += [t, Z - t] if 2 * t < Z else [t]
    for k in near[1:]:
        send(
            metab.at[z, c, y],
            metab.at[z, c, y],
            mz_s.at[k - 1],
            mz_r.at[k - 1],
            patch_0=step(z, k, Z),
        )
    for k in near:
        for m in range(X):
            if k or m:
                to = step(x, m, X)
                rows = pl.ds(pl.multiple_of(to * PX, PX), PX)
                send(
                    cot_ref.at[rows, :],
                    cotb.at[z, c, y, :, xf],
                    cz_s.at[k, m],
                    cz_r.at[k],
                    patch_0=step(z, k, Z),
                    mp=to,
                )
    for k in range(1, X):
        to = step(x, k, X)
        send(second_ref, second.at[:, xf], sec_s.at[k - 1], sec_r.at[k - 1], mp=to)

    def send_slot(j, carry):
        dz, dy, dc = j // (Y * 2), (j // 2) % Y, j % 2
        z1, y1, c1 = lax.rem(z + dz, Z), lax.rem(y + dy, Y), lax.rem(c + dc, 2)
        pltpu.make_async_remote_copy(
            src_ref=slots.at[(z1 * 2 + c1) * Y + y1],
            dst_ref=V.at[here],
            send_sem=w_s,
            recv_sem=w_r.at[z],
            device_id={"patch_0": z1, "patch_1": y1, "patch_2": c1, "mp": x},
            device_id_type=pl.DeviceIdType.MESH,
        ).start()
        return carry

    for dz in near:
        lax.fori_loop(max(1, dz * Y * 2), (dz + 1) * Y * 2, send_slot, 0)

    TR = 2 * PATCH
    T = R // TR

    def first_layer(i):
        rows = pl.ds(i * TR, TR)
        pre = dot(grid_ref[rows, :], first_ref[...])
        s = jax.nn.sigmoid(pre)
        hidden[rows, :] = (pre * s).astype(BF16)
        slope[rows, :] = s * (1.0 + pre * (1.0 - s))

    def second_layer(i):
        rows = pl.ds(i * TR, TR)
        msg[rows, :] = dot(hidden[rows, :], second[...]).astype(BF16)

    def over_y(k):
        at = step(z, (Z - k) % Z, Z)
        if k:
            arrive(cotb.at[at, c, y], cz_r.at[k])
        else:
            own_cot.wait()
            arrive(cotb.at[at, c, y, :, pl.ds(0, (X - 1) * F)], cz_r.at[k])
        for m in range(1, Y):
            block = cotb.at[at, c, y]
            send(block, block, cy_s.at[m - 1, k], cy_r.at[m - 1, k], patch_1=step(y, m, Y))

    loads["grid"].wait()
    loads["first"].wait()
    per = -(-Z // T)
    for i in range(T):
        first_layer(i)
        for k in near[i * per : (i + 1) * per]:
            over_y(k)
        if i == 0:
            for k in range(1, Z):
                arrive(metab.at[step(z, Z - k, Z), c, y], mz_r.at[k - 1])
            for j in range(1, 2 * Y):
                send(
                    metab.at[:, c, y],
                    metab.at[:, c, y],
                    my_s.at[j],
                    my_r.at[j],
                    patch_1=step(y, j // 2, Y),
                    patch_2=lax.rem(c + j % 2, 2),
                )
    own_second.wait()
    for k in range(1, X):
        frm = step(x, X - k, X)
        arrive(second.at[:, pl.ds(pl.multiple_of(frm * F, F), F)], sec_r.at[k - 1])
    for i in range(T):
        second_layer(i)
    for j in range(1, 2 * Y):
        core, yy = lax.rem(c + j % 2, 2), step(y, Y - j // 2, Y)
        arrive(metab.at[:, core, yy], my_r.at[j])

    own_natural = (z * Y + y) * 2 + c
    PL = C * Y
    TP = PL * PX
    lanes = lax.broadcasted_iota(jnp.int32, (PL, PATCH), 1)

    def plane(k):
        return step(z, (Z - k) % Z, Z)

    def spread(at, slot):
        meta = metab[at].reshape(PL, PATCH)
        patch_of = jnp.sum(jnp.where(lanes == own_natural, meta, 0.0), axis=1, keepdims=True)
        patch_rows = jnp.broadcast_to(
            jnp.broadcast_to(patch_of, (PL, PATCH))[:, None, :], (PL, PX, PATCH)
        ).reshape(TP, PATCH)
        blocks = V[pl.ds(pl.multiple_of(at * PL, PL), PL)].reshape(TP, PATCH).astype(F32)
        blocks_t = blocks.T
        patch_cols = patch_rows.T
        for g in range(GPD):
            vbig[:, g * PATCH : (g + 1) * PATCH] = jnp.where(
                patch_rows == float(g), blocks, 0.0
            ).astype(BF16)
            vbig_t[slot, g * PATCH : (g + 1) * PATCH, :] = jnp.where(
                patch_cols == float(g), blocks_t, 0.0
            ).astype(BF16)

    def contribute(i, k):
        at, slot = plane(k), i % 2
        arrive(V.at[pl.ds(0, PL if k else PL - 1)], w_r.at[at])
        spread(at, slot)
        c_own[slot] = dot(vbig[...], msg[...]).reshape(C, Y, PX, D)
        c_send[at] = c_own[slot, oc].astype(BF16)
        send(c_send.at[at], c_recv.at[at], fc_s.at[k], fc_r.at[k], patch_2=oc)
        for m in range(1, Y):
            arrive(cotb.at[at, c, step(y, Y - m, Y)], cy_r.at[m - 1, k])
        send(cotb.at[at, c], cotb.at[at, c], cc_s.at[k], cc_r.at[k], patch_2=oc)

    def collect(i, k):
        at, slot = plane(k), i % 2
        arrive(c_recv.at[at], fc_r.at[k])
        c_sum[...] = c_own[slot, c] + c_recv[at].astype(F32)
        y_own[at] = c_sum[y]
        for m in range(1, Y):
            to = step(y, m, Y)
            y_send[m - 1, at] = c_sum[to].astype(BF16)
            send(
                y_send.at[m - 1, at],
                y_recv.at[m - 1, at],
                fy_s.at[m - 1, k],
                fy_r.at[m - 1, k],
                patch_1=to,
            )
        arrive(cotb.at[at, oc], cc_r.at[k])
        for t in range(T):
            rows = slice(t * TR, (t + 1) * TR)
            part = dot(vbig_t[slot, rows, :], cotb[at].reshape(TP, D))
            if i == 0:
                gm_sum[rows, :] = part
            elif i < Z - 1:
                gm_sum[rows, :] += part
            else:
                gm[rows, :] = (gm_sum[rows, :] + part).astype(BF16)

    own_slot.wait()
    for i, k in enumerate(near):
        contribute(i, k)
        if i:
            collect(i - 1, near[i - 1])
    collect(Z - 1, near[-1])

    def half_of(core, which, left_ref, right_ref, into):
        cols = pl.ds(pl.multiple_of(core * HC, HC), HC)
        part = dot(left_ref[:, cols], right_ref[...], ((0,), (0,))) * scaling
        for q in range(X):
            into[which, q] = part[:, q * F : (q + 1) * F]

    def give(which, left_ref, right_ref):
        half_of(oc, which, left_ref, right_ref, gc_send)
        send(
            gc_send.at[which], gc_recv.at[which], gc_s.at[which], gc_r.at[which], patch_2=oc
        )

    def keep(which, left_ref, right_ref):
        half_of(c, which, left_ref, right_ref, g_own)

    def over_mp(which):
        arrive(gc_recv.at[which], gc_r.at[which])
        for k in range(1, X):
            to = step(x, k, X)
            gx_send[which, k - 1] = (g_own[which, to] + gc_recv[which, to]).astype(BF16)
            send(
                gx_send.at[which, k - 1],
                gx_recv.at[which, k - 1],
                gx_s.at[which, k - 1],
                gx_r.at[which, k - 1],
                mp=to,
            )
        g_own[which, x] = g_own[which, x] + gc_recv[which, x]

    give(0, hidden, gm)

    def pre_gradient(i, carry):
        rows = pl.ds(pl.multiple_of(i * TR, TR), TR)
        back = dot(gm[rows, :], second[...], ((1,), (1,)))
        gpre[rows, :] = (back * slope[rows, :]).astype(BF16)
        return carry

    lax.fori_loop(0, R // TR, pre_gradient, 0)
    give(1, grid_ref, gpre)
    keep(0, hidden, gm)
    over_mp(0)
    keep(1, grid_ref, gpre)

    over_mp(1)

    for k in near:
        at = plane(k)
        total = y_own[at]
        for m in range(1, Y):
            arrive(y_recv.at[m - 1, at], fy_r.at[m - 1, k])
            total = total + y_recv[m - 1, at].astype(F32)
        if k:
            z_send[at] = total.astype(BF16)
            send(z_send.at[at], z_recv.at[k - 1], fz_s.at[k - 1], fz_r.at[k - 1], patch_0=at)
        else:
            y_own[at] = total

    ZR = HC // Z
    for which in range(2):
        total = g_own[which, x]
        for k in range(1, X):
            arrive(gx_recv.at[which, k - 1], gx_r.at[which, k - 1])
            total = total + gx_recv[which, k - 1].astype(F32)
        g_own[which, x] = total
        gz_send[:, which] = total.reshape(Z, ZR, F).astype(BF16)
    for k in range(1, Z):
        to = step(z, k, Z)
        send(gz_send.at[to], gz_recv.at[k - 1], gz_s.at[k - 1], gz_r.at[k - 1], patch_0=to)

    total = g_own[:, x, pl.ds(pl.multiple_of(z * ZR, ZR), ZR)]
    for k in range(1, Z):
        arrive(gz_recv.at[k - 1], gz_r.at[k - 1])
        total = total + gz_recv[k - 1].astype(F32)
    gy[y] = total
    for k in range(1, Y):
        to = step(y, k, Y)
        send(gy.at[y], gy.at[y], gy_s.at[k - 1], gy_r.at[k - 1], patch_1=to)

    for k in range(1, Y):
        arrive(gy.at[step(y, Y - k, Y)], gy_r.at[k - 1])
    total = gy[0]
    for yy in range(1, Y):
        total = total + gy[yy]
    own[...] = total.astype(BF16)
    for k in range(1, Z):
        to = step(z, k, Z)
        send(own, fin.at[c, z], az_s.at[k - 1], az_r.at[k - 1], patch_0=to)
    fin[c, z] = own[...]

    total = y_own[z]
    for k in range(1, Z):
        arrive(z_recv.at[k - 1], fz_r.at[k - 1])
        total = total + z_recv[k - 1].astype(F32)
    for q in range(X):
        x_send[q] = total[:, q * F : (q + 1) * F]
    own_sum = pltpu.make_async_copy(x_send.at[x], x_recv.at[x], loc.at[0])
    own_sum.start()
    for k in range(1, X):
        to = step(x, k, X)
        send(x_send.at[to], x_recv.at[x], fx_s.at[k - 1], fx_r.at[k - 1], mp=to)

    for k in range(1, Z):
        arrive(fin.at[c, step(z, Z - k, Z)], az_r.at[k - 1])
    send(fin.at[c], fin.at[c], ac_s.at[0], ac_r.at[0], patch_2=oc)
    own_sum.wait()
    for k in range(1, X):
        arrive(x_recv.at[step(x, X - k, X)], fx_r.at[k - 1])
    loads["latent"].wait()
    mesh_out[...] = (latent_ref[...].astype(F32) + x_recv[...].reshape(PATCH, F)).astype(BF16)
    arrive(fin.at[oc], ac_r.at[0])
    pltpu.make_async_remote_copy(
        src_ref=all_but_one(slots, NP),
        dst_ref=all_but_one(V, NP),
        send_sem=w_s,
        recv_sem=w_r.at[0],
        device_id={"patch_0": z, "patch_1": y, "patch_2": oc, "mp": x},
        device_id_type=pl.DeviceIdType.MESH,
    ).wait_send()
    for src, dst, ss, rs in sent:
        pltpu.make_async_copy(src, src, ss).wait()


def hand_out(mesh_sum, sums, mesh_out, first_out, second_out):
    mesh_out[...] = mesh_sum[...]
    second_out[...] = sums[:, :, 0].reshape(second_out.shape).astype(F32)
    first_out[...] = sums[:, :, 1].reshape(first_out.shape).astype(F32)


def all_but_one(ref, n):
    return ref.at[pl.ds(0, n - 1)]


def per_device(
    grid_latent,
    mesh_latent,
    edge_weight,
    block_source,
    block_live,
    mlp_first,
    mlp_second,
    mesh_cotangent,
):
    Z, Y, C = (lax.axis_size(a) for a in PATCH_AXES)
    X = lax.axis_size("mp")
    NP = Z * Y * C
    R, D = grid_latent.shape
    H = mlp_first.shape[1]
    F = mlp_second.shape[1]
    PX = PATCH // X
    GPD = R // PATCH
    HC = D // 2
    ZR = HC // Z
    scaling = 1.0 / math.sqrt(R * NP)

    vm = pltpu.VMEM
    dma = pltpu.SemaphoreType.DMA
    scratch = [
        vm((1, PATCH), F32),
        vm(grid_latent.shape, BF16),
        vm(mesh_latent.shape, BF16),
        vm(edge_weight.shape, BF16),
        vm(mlp_first.shape, BF16),
        vm(mlp_second.shape, BF16),
        vm(mesh_cotangent.shape, BF16),
        vm((NP, PX, PATCH), BF16),
        vm((NP, PX, PATCH), BF16),
        vm((Z, C, Y, PX, D), BF16),
        vm((Z, C, Y, 1, PATCH), F32),
        vm((H, D), BF16),
        vm((R, H), F32),
        vm((R, H), BF16),
        vm((R, D), BF16),
        vm((C * Y * PX, R), BF16),
        vm((2, R, C * Y * PX), BF16),
        vm((2, C, Y, PX, D), F32),
        vm((Y, PX, D), F32),
        vm((Z, Y, PX, D), BF16),
        vm((Z, Y, PX, D), BF16),
        vm((Y - 1, Z, PX, D), BF16),
        vm((Y - 1, Z, PX, D), BF16),
        vm((Z, PX, D), F32),
        vm((Z, PX, D), BF16),
        vm((Z - 1, PX, D), BF16),
        vm((X, PX, F), F32),
        vm((X, PX, F), F32),
        vm((R, D), F32),
        vm((R, D), BF16),
        vm((R, H), BF16),
        vm((2, X, HC, F), F32),
        vm((2, X, HC, F), F32),
        vm((2, X, HC, F), F32),
        vm((2, X - 1, HC, F), BF16),
        vm((2, X - 1, HC, F), BF16),
        vm((Z, 2, ZR, F), BF16),
        vm((Z - 1, 2, ZR, F), BF16),
        vm((Y, 2, ZR, F), F32),
        vm((2, ZR, F), BF16),
        dma,
        dma((Z,)),
        dma((X - 1,)),
        dma((X - 1,)),
        dma((X - 1,)),
        dma((X - 1,)),
        dma((Z, X)),
        dma((Z,)),
        dma((Y - 1, Z)),
        dma((Y - 1, Z)),
        dma((Z,)),
        dma((Z,)),
        dma((Z - 1,)),
        dma((Z - 1,)),
        dma((2 * Y,)),
        dma((2 * Y,)),
        dma((Z,)),
        dma((Z,)),
        dma((Y - 1, Z)),
        dma((Y - 1, Z)),
        dma((Z - 1,)),
        dma((Z - 1,)),
        dma((X - 1,)),
        dma((X - 1,)),
        dma((2,)),
        dma((2,)),
        dma((2, X - 1)),
        dma((2, X - 1)),
        dma((Z - 1,)),
        dma((Z - 1,)),
        dma((Y - 1,)),
        dma((Y - 1,)),
        dma((Z - 1,)),
        dma((Z - 1,)),
        dma((1,)),
        dma((1,)),
        dma((4,)),
        dma((6,)),
    ]
    in_vmem = pl.BlockSpec(memory_space=pltpu.VMEM)
    mesh_sum, sums = pl.pallas_call(
        functools.partial(kernel, (Z, Y, C, X), scaling),
        out_shape=(
            jax.ShapeDtypeStruct((PATCH, F), BF16),
            jax.ShapeDtypeStruct((C, Z, 2, ZR, F), BF16),
        ),
        in_specs=[pl.BlockSpec(memory_space=pltpu.SMEM)] * 2
        + [pl.BlockSpec(memory_space=pl.ANY)] * 6,
        out_specs=(in_vmem, in_vmem),
        scratch_shapes=scratch,
        compiler_params=pltpu.CompilerParams(
            collective_id=0, has_side_effects=True, vmem_limit_bytes=62 * 1024 * 1024
        ),
    )(
        block_source,
        block_live,
        grid_latent,
        mesh_latent,
        edge_weight,
        mlp_first,
        mlp_second,
        mesh_cotangent,
    )
    return pl.pallas_call(
        hand_out,
        out_shape=(
            jax.ShapeDtypeStruct((PATCH, F), BF16),
            jax.ShapeDtypeStruct((D, F), F32),
            jax.ShapeDtypeStruct((H, F), F32),
        ),
        in_specs=[in_vmem] * 2,
        out_specs=(in_vmem, in_vmem, in_vmem),
    )(mesh_sum, sums)


def torus_of(mesh):
    return Mesh(mesh.devices.reshape(8, 4, 2, mesh.shape["mp"]), AXES)


def solution(mesh):
    torus = torus_of(mesh)
    in_specs = (
        P(PATCH_AXES, None),
        P(PATCH_AXES, "mp"),
        P(PATCH_AXES, None, None),
        P(PATCH_AXES),
        P(PATCH_AXES),
        P(),
        P(None, "mp"),
        P(PATCH_AXES, "mp"),
    )
    out_specs = (P(PATCH_AXES, "mp"), P(None, "mp"), P(None, "mp"))
    return jax.shard_map(
        per_device, mesh=torus, in_specs=in_specs, out_specs=out_specs, check_vma=False
    )
```
